32 devices in a mesh: groups: 2 (over y), slab: 16 (over z, x, core).
Axes of the slice: x: 2, y: 2, z: 4, core: 2. Of those that a mesh axis runs over, the one named last changes fastest.
Arguments:
- rhs: float32 [2, 64, 128, 128], P('groups', 'slab'), parts along dimension 0, may hold values from -6 to 6
- labels: int32 [64, 256, 128], P('slab', 'groups'), parts along dimension 1, may hold values from 0 to 4, as said below
- sigma_table: float32 [5, 3], replicated, may hold values from 0.05 to 2
Outputs:
- correction: float32 [2, 64, 128, 128], P('groups', 'slab'), parts along dimension 0
The draws below stay inside these ranges and needn't reach their ends.
There are 2 independent parts, one for each index of `groups`. The reference program is written for one: setup_inputs(seed, part) draws one part's arguments, and reference() takes and returns one part's arrays. A program takes and returns all parts, laid end to end along the dimension named above; an argument that names none is the same for every part. Nothing has to cross between parts.
Inputs may be any that keep to these rules, and one draw needn't show every extreme that they name: Label 0 marks exactly the voxels outside an ellipsoid centred on the grid with semi-axes 0.45 * 128, 0.45 * 128 and 0.55 * 64 cells; inside, labels 1 to 4 are drawn independently for each voxel.
All inputs are finite; a program needn't handle non-finite values.
Results may differ from the reference program's by a relative error of at most 0.0002.
Values sent between devices are 32-bit elements; how exact they have to be, the bound alone decides.
A program may use at most 64 MiB of HBM per device.

```python
import math
import jax
import jax.numpy as jnp
from jax import lax

R = 1
NX = 128
NY = 128
LABELS = 5
NZ = 64


def draw_labels(key, part):
    shape = (NZ, NX, NY)
    zcoord = lax.broadcasted_iota(jnp.int32, shape, 0)
    xcoord = lax.broadcasted_iota(jnp.int32, shape, 1)
    ycoord = lax.broadcasted_iota(jnp.int32, shape, 2)
    dist_z = 2 * zcoord + 1 - NZ
    dist_x = 2 * xcoord + 1 - NX
    dist_y = 2 * ycoord + 1 - NY
    term_x = 1000 * dist_x * dist_x // (81 * NX * NX // 100)
    term_y = 1000 * dist_y * dist_y // (81 * NY * NY // 100)
    term_z = 1000 * dist_z * dist_z // (121 * NZ * NZ // 100)
    inside = term_x + term_y + term_z < 1000
    tissue = jax.random.randint(jax.random.fold_in(key, 7), shape, 1, LABELS)
    return jnp.where(inside, tissue, 0).astype(jnp.int32)


def level_of(rng, dims, shards, smallest, high):
    def one(position, parts):
        steps = jax.random.uniform(jax.random.fold_in(jax.random.fold_in(rng, 6), position), (parts,), jnp.float32, smallest / len(shards), high / len(shards))
        return jnp.repeat(jnp.exp(steps), dims[position] // parts).reshape((-1,) + (1,) * (len(dims) - position - 1))

    factor_of = one(*shards[0])
    for cut in shards[1:]:
        factor_of = factor_of * one(*cut)
    return factor_of


def centred(key, dims, scale, bound, pieces=(), dtype=jnp.bfloat16):
    result = scale * jax.random.normal(key, dims, jnp.float32)
    if pieces:
        result = result * level_of(key, dims, pieces, -0.22, 0.18)
    return jnp.clip(result, -bound, bound).astype(dtype)


def setup_inputs(seed: int = 0, part: int = 0) -> dict:
    key_list = jax.random.split(jax.random.key(seed), 4)
    own_keys = jax.random.split(jax.random.fold_in(key_list[3], part), 4)
    return {
        "rhs": centred(own_keys[0], (R, NZ, NX, NY), 1.0, 6.0, ((1, 16),), jnp.float32),
        "labels": draw_labels(jax.random.fold_in(jax.random.fold_in(key_list[3], part), 71), part),
        "sigma_table": jnp.clip(jnp.exp(jax.random.uniform(key_list[2], (LABELS, 3), jnp.float32, math.log(0.05), math.log(2.0))), 0.05, 2.0),
    }


OMEGA = 0.8

def harmonic(lower_side, upper_side):
    return 2.0 * lower_side * upper_side / (lower_side + upper_side)

def conductivity(padded, sigma_table, column):
    running = jnp.zeros(padded.shape, jnp.float32)
    for tissue in range(LABELS):
        running = running + jnp.where(padded == tissue, sigma_table[tissue, column], 0.0)
    return running

def coefficients(labels_ext, sigma_table):
    padded = jnp.pad(labels_ext, ((0, 0), (1, 1), (1, 1)))
    active = (padded > 0).astype(jnp.float32)
    sigma_x = conductivity(padded, sigma_table, 0)
    sigma_y = conductivity(padded, sigma_table, 1)
    sigma_z = conductivity(padded, sigma_table, 2)
    inner_x = harmonic(sigma_x[1:-1, :-1, 1:-1], sigma_x[1:-1, 1:, 1:-1])
    couple_x = inner_x * active[1:-1, :-1, 1:-1] * active[1:-1, 1:, 1:-1]
    inner_y = harmonic(sigma_y[1:-1, 1:-1, :-1], sigma_y[1:-1, 1:-1, 1:])
    couple_y = inner_y * active[1:-1, 1:-1, :-1] * active[1:-1, 1:-1, 1:]
    inner_z = harmonic(sigma_z[:-1, 1:-1, 1:-1], sigma_z[1:, 1:-1, 1:-1])
    couple_z = inner_z * active[:-1, 1:-1, 1:-1] * active[1:, 1:-1, 1:-1]
    centre_mask = active[1:-1, 1:-1, 1:-1]
    faces = inner_x[:, :-1] + inner_x[:, 1:] + inner_y[:, :, :-1] + inner_y[:, :, 1:] + inner_z[:-1] + inner_z[1:]
    diagonal = centre_mask * faces + (1.0 - centre_mask)
    return (centre_mask, diagonal, couple_x, couple_y, couple_z)

def operate(extended, terms):
    couple_x, couple_y, couple_z = (terms[2], terms[3], terms[4])
    centre = extended[:, 1:-1]
    widened = jnp.pad(centre, ((0, 0), (0, 0), (1, 1), (1, 1)))
    neighbours = couple_x[:, :-1] * widened[:, :, :-2, 1:-1] + couple_x[:, 1:] * widened[:, :, 2:, 1:-1]
    neighbours = neighbours + couple_y[:, :, :-1] * widened[:, :, 1:-1, :-2] + couple_y[:, :, 1:] * widened[:, :, 1:-1, 2:]
    neighbours = neighbours + couple_z[:-1] * extended[:, :-2] + couple_z[1:] * extended[:, 2:]
    return terms[1] * centre - neighbours

def smooth(extended, source, terms):
    image = operate(extended, terms)
    return extended[:, 1:-1] + OMEGA * terms[0] * (source - image) / terms[1]

def start(source, terms):
    return OMEGA * terms[0] * source / terms[1]

def leftover(extended, source, terms):
    return terms[0] * (source - operate(extended, terms))

def pair_sum(values, along):
    even_part = [slice(None)] * values.ndim
    odd_part = [slice(None)] * values.ndim
    even_part[along] = slice(0, None, 2)
    odd_part[along] = slice(1, None, 2)
    return values[tuple(even_part)] + values[tuple(odd_part)]

def coarsen(terms):
    centre_mask, diagonal, couple_x, couple_y, couple_z = terms
    coarse_x = pair_sum(pair_sum(couple_x[:, 0::2], 0), 2)
    coarse_y = pair_sum(pair_sum(couple_y[:, :, 0::2], 0), 1)
    coarse_z = pair_sum(pair_sum(couple_z[0::2], 1), 2)
    internal = pair_sum(pair_sum(couple_x[:, 1::2], 0), 2) + pair_sum(pair_sum(couple_y[:, :, 1::2], 0), 1) + pair_sum(pair_sum(couple_z[1::2], 1), 2)
    counted = pair_sum(pair_sum(pair_sum(centre_mask, 0), 1), 2)
    raw_diag = pair_sum(pair_sum(pair_sum(centre_mask * diagonal, 0), 1), 2) - 2.0 * internal
    coarse_mask = jnp.minimum(counted, 1.0)
    coarse_diag = raw_diag + (1.0 - coarse_mask)
    return ((coarse_mask, coarse_diag, coarse_x, coarse_y, coarse_z), raw_diag)

def restrict(field):
    return pair_sum(pair_sum(pair_sum(field, 1), 2), 3)

def widen(field):
    return jnp.repeat(jnp.repeat(jnp.repeat(field, 2, axis=1), 2, axis=2), 2, axis=3)

def plane_total(values):
    return jnp.sum(values, axis=(-2, -1))

def line_terms(coarse_terms, raw_diag):
    line_diag = plane_total(raw_diag) - 2.0 * (plane_total(coarse_terms[2]) + plane_total(coarse_terms[3]))
    return (line_diag, plane_total(coarse_terms[4]))

def zeros_rim(field):
    return jnp.pad(field, ((0, 0), (1, 1), (0, 0), (0, 0)))

def reference(rhs, labels, sigma_table):
    padded_labels = jnp.pad(labels, ((1, 1), (0, 0), (0, 0)))
    fine_terms = coefficients(padded_labels, sigma_table)
    coarse_terms, raw_diag = coarsen(fine_terms)
    line_diag, line_faces = line_terms(coarse_terms, raw_diag)
    lower_band = -line_faces[:-1]
    upper_band = -line_faces[1:]

    def one_side(single):
        source = fine_terms[0] * single
        fine_first = start(source, fine_terms)
        fine_second = smooth(zeros_rim(fine_first), source, fine_terms)
        fine_left = leftover(zeros_rim(fine_second), source, fine_terms)
        coarse_source = restrict(fine_left)
        coarse_first = start(coarse_source, coarse_terms)
        coarse_second = smooth(zeros_rim(coarse_first), coarse_source, coarse_terms)
        coarse_left = leftover(zeros_rim(coarse_second), coarse_source, coarse_terms)
        line_rows = plane_total(coarse_left).T
        line_solution = lax.linalg.tridiagonal_solve(lower_band, line_diag, upper_band, line_rows)
        coarse_fix = coarse_second + coarse_terms[0] * line_solution.T[:, :, None, None]
        coarse_post = smooth(zeros_rim(coarse_fix), coarse_source, coarse_terms)
        coarse_final = smooth(zeros_rim(coarse_post), coarse_source, coarse_terms)
        fine_third = fine_second + fine_terms[0] * widen(coarse_final)
        fine_fourth = smooth(zeros_rim(fine_third), source, fine_terms)
        return smooth(zeros_rim(fine_fourth), source, fine_terms)
    return lax.map(one_side, rhs[:, None])[:, 0]
```

```python
import functools

import jax
import jax.numpy as jnp
from jax import lax
from jax.experimental import pallas as pl
from jax.experimental.pallas import tpu as pltpu
from jax.sharding import PartitionSpec as P

OMEGA = 0.8
LABELS = 5
MESH = pl.DeviceIdType.MESH


def copy_to(src, dst, sems, slot, target):
    return pltpu.make_async_remote_copy(
        src_ref=src,
        dst_ref=dst,
        send_sem=sems.at[0, slot],
        recv_sem=sems.at[1, slot],
        device_id={"slab": target},
        device_id_type=MESH,
    )


def kernel(
    n, rhs_hbm, lab_hbm, table_hbm, out,
    lab, rhs, gx, gy, gz, idf, dg, ua, ub, tmp, pro,
    cof, part, edge, b1, vn, line_out, line_all, row_out, row_all, xs, table,
    load_sem, sems, gather_sem, tokens,
):
    me = lax.axis_index("slab")
    nx, ny = lab.shape[1:]
    hx_rows = nx // 2
    has_low, has_up = me > 0, me < n - 1

    load_table = pltpu.make_async_copy(table_hbm, table, load_sem.at[2])
    load_table.start()
    own_lab = pltpu.make_async_copy(lab_hbm, lab.at[pl.ds(2, 4)], load_sem.at[0])
    own_rhs = pltpu.make_async_copy(rhs_hbm.at[0], rhs.at[pl.ds(2, 4)], load_sem.at[1])
    own_lab.start()
    own_rhs.start()
    barrier = pltpu.get_barrier_semaphore()

    up, low = lax.rem(me + 1, n), lax.rem(me + n - 1, n)

    def greet(sem, distance):
        for near, other in ((me >= distance, me - distance), (me + distance < n, me + distance)):

            @pl.when(near)
            def _():
                pl.semaphore_signal(sem, inc=1, device_id={"slab": other}, device_id_type=MESH)

    def greeted(sem, distance):
        both = jnp.logical_and(me >= distance, me + distance < n)
        one = jnp.logical_xor(me >= distance, me + distance < n)
        pl.when(both)(lambda: pl.semaphore_wait(sem, 2))
        pl.when(one)(lambda: pl.semaphore_wait(sem, 1))

    greet(barrier, 1)
    greeted(barrier, 1)

    rounds = [2**r for r in range((n - 1).bit_length())]

    def round_start(r):
        if r < len(rounds):
            greet(tokens.at[r], rounds[r])

    def round_end(r):
        if r < len(rounds):
            greeted(tokens.at[r], rounds[r])

    near_up = copy_to(lab_hbm.at[3], lab.at[1], sems, 0, up)
    near_low = copy_to(lab_hbm.at[0], lab.at[6], sems, 1, low)
    next_up = copy_to(lab_hbm.at[2], lab.at[0], sems, 2, up)
    next_low = copy_to(lab_hbm.at[1], lab.at[7], sems, 3, low)
    rhs_up = copy_to(rhs_hbm.at[0, 3], rhs.at[1], sems, 4, up)
    rhs_low = copy_to(rhs_hbm.at[0, 0], rhs.at[6], sems, 5, low)
    u1_up = copy_to(ua.at[4], ua.at[0], sems, 6, up)
    u1_low = copy_to(ua.at[3], ua.at[7], sems, 7, low)
    cof_up = copy_to(cof.at[1, pl.ds(0, 4)], cof.at[0, pl.ds(0, 4)], sems, 8, up)
    cof_low = copy_to(cof.at[1, pl.ds(1, 4)], cof.at[2, pl.ds(1, 4)], sems, 9, low)
    b1_up = copy_to(b1.at[1], b1.at[0], sems, 10, up)
    b1_low = copy_to(b1.at[1], b1.at[2], sems, 11, low)
    u2_up = copy_to(ub.at[4], ub.at[0], sems, 12, up)
    u2_low = copy_to(ub.at[3], ub.at[7], sems, 13, low)
    vn_up = copy_to(vn.at[1], vn.at[0], sems, 14, up)
    vn_low = copy_to(vn.at[1], vn.at[2], sems, 15, low)
    edge_up = copy_to(part.at[0], edge.at[0], sems, 16, up)
    edge_low = copy_to(part.at[1], edge.at[1], sems, 17, low)

    def send(upward, downward):
        pl.when(has_up)(upward.start)
        pl.when(has_low)(downward.start)

    def receive(upward, downward):
        pl.when(has_low)(upward.wait_recv)
        pl.when(has_up)(downward.wait_recv)

    send(near_up, near_low)
    send(next_up, next_low)
    send(rhs_up, rhs_low)
    round_start(0)

    def clear(ref, first, count):
        for k in range(first, first + count):
            ref[k] = jnp.zeros(ref.shape[1:], ref.dtype)

    @pl.when(me == 0)
    def _():
        clear(lab, 0, 2)
        clear(rhs, 1, 1)
        clear(ua, 0, 1)
        clear(edge.at[0], 0, 2)
        clear(cof.at[0], 0, 4)
        clear(b1, 0, 1)
        clear(ub, 0, 1)
        clear(vn, 0, 1)

    @pl.when(me == n - 1)
    def _():
        clear(lab, 6, 2)
        clear(rhs, 6, 1)
        clear(ua, 7, 1)
        clear(edge.at[1], 0, 2)
        clear(cof.at[2], 1, 4)
        clear(b1, 2, 1)
        clear(ub, 7, 1)
        clear(vn, 2, 1)

    xs[...] = jnp.zeros(xs.shape, xs.dtype)

    fine_row = lax.broadcasted_iota(jnp.int32, (nx, ny), 0) % 2 == 1
    fine_lane = lax.broadcasted_iota(jnp.int32, (nx, ny), 1) % 2 == 1
    even = lax.broadcasted_iota(jnp.int32, (hx_rows, ny), 1) % 2 == 0

    def select(values, column):
        chosen = jnp.full(values.shape, table[column, 0], jnp.float32)
        for tissue in range(1, LABELS):
            chosen = jnp.where(values == tissue, table[column, tissue], chosen)
        return chosen

    def harmonic(a, b):
        return 2.0 * a * b / (a + b)

    def active(k):
        return (lab[k] > 0).astype(jnp.float32)

    def side_faces(k):
        here = lab[k]
        a = (here > 0).astype(jnp.float32)
        sx, sy = select(here, 0), select(here, 1)
        hx = harmonic(pltpu.roll(sx, 1, 0), sx)
        gx[k] = hx * a * pltpu.roll(a, 1, 0)
        hy = harmonic(pltpu.roll(sy, 1, 1), sy)
        gy[k] = hy * a * pltpu.roll(a, 1, 1)
        return hx + pltpu.roll(hx, nx - 1, 0) + hy + pltpu.roll(hy, ny - 1, 1)

    def face_below(k):
        h = harmonic(select(lab[k - 1], 2), select(lab[k], 2))
        gz[k] = h * active(k - 1) * active(k)
        return h

    def finish(k, faces):
        a = active(k)
        diagonal = a * faces + (1.0 - a)
        dg[k] = diagonal
        idf[k] = OMEGA * a / diagonal

    def over(first, last, body):
        for k in range(first, last):
            body(k)

    def first_sweep(k):
        ua[k] = idf[k] * rhs[k]

    def neighbours(field, k):
        u = field[k]
        cx, cy = gx[k], gy[k]
        total = cx * pltpu.roll(u, 1, 0) + pltpu.roll(cx * u, nx - 1, 0)
        total = total + cy * pltpu.roll(u, 1, 1) + pltpu.roll(cy * u, ny - 1, 1)
        return u, total + gz[k] * field[k - 1] + gz[k + 1] * field[k + 1]

    def sweep(src, dst, shift=0):
        def body(k):
            u, total = neighbours(src, k)
            dst[k - shift] = (1.0 - OMEGA) * u + idf[k] * (rhs[k] + total)

        return body

    def residual(k):
        u, total = neighbours(ub, k)
        return jnp.where(idf[k] > 0.0, rhs[k] - dg[k] * u + total, 0.0)

    second_sweep = sweep(ua, ub)

    load_table.wait()
    own_lab.wait()
    h3, h4, h5 = face_below(3), face_below(4), face_below(5)
    finish(3, side_faces(3) + h3 + h4)
    finish(4, side_faces(4) + h4 + h5)
    dg[2] = side_faces(2) + h3
    dg[5] = side_faces(5) + h5
    own_rhs.wait()
    over(3, 5, first_sweep)

    def rows_even(plane):
        tmp[0] = plane
        return tmp[0, pl.ds(0, hx_rows, 2), :]

    def rows_sum(plane):
        tmp[0] = plane
        return tmp[0, pl.ds(0, hx_rows, 2), :] + tmp[0, pl.ds(1, hx_rows, 2), :]

    def lanes_sum(t0, t1):
        return jnp.where(even, t0 + pltpu.roll(t0, ny - 1, 1), t1 + pltpu.roll(t1, 1, 1))

    def lanes_even(t0, t1):
        return jnp.where(even, t0, pltpu.roll(t1, 1, 1))

    def restrict(p0, p1):
        return lanes_sum(rows_sum(p0), rows_sum(p1))

    def inner(k):
        doubled = jnp.where(fine_row, gx[k], 0.0) + jnp.where(fine_lane, gy[k], 0.0)
        if k % 2 == 1:
            doubled = doubled + gz[k]
        return active(k) * dg[k] - 2.0 * doubled

    def swap(pack):
        return jnp.where(even, pltpu.roll(pack, ny - 1, 1), pltpu.roll(pack, 1, 1))

    raw_part = restrict(inner(2) + inner(3), inner(4) + inner(5))
    coarse_x = lanes_sum(rows_even(gx[2] + gx[3]), rows_even(gx[4] + gx[5]))
    coarse_y = lanes_even(rows_sum(gy[2] + gy[3]), rows_sum(gy[4] + gy[5]))
    side = coarse_x + pltpu.roll(coarse_x, hx_rows - 1, 0) + coarse_y + pltpu.roll(coarse_y, ny - 2, 1)
    middle = rows_sum(gz[4])
    z_in = lanes_sum(middle, middle)
    part[0, 0] = jnp.where(even, pltpu.roll(raw_part, ny - 1, 1), side)
    part[1, 0] = jnp.where(even, raw_part, pltpu.roll(side, 1, 1))
    part[0, 1] = z_in
    part[1, 1] = z_in
    send(edge_up, edge_low)
    send(u1_up, u1_low)
    cof[1, 2] = coarse_x
    cof[1, 3] = coarse_y

    round_end(0)
    round_start(1)
    receive(near_up, near_low)
    h2, h6 = face_below(2), face_below(6)
    tmp[6] = h2
    tmp[7] = h6
    finish(2, dg[2] + h2)
    finish(5, dg[5] + h6)
    over(0, 2, lambda k: first_sweep(2 + 3 * k))
    raw = raw_part + restrict(active(2) * h2, active(5) * h6)
    active1 = jnp.where(raw_part > 0.0, 1.0, 0.0)
    diag1 = raw + (1.0 - active1)
    weight1 = OMEGA * active1 / diag1
    z_out = restrict(gz[2], gz[6])
    outer = restrict(active(1) * h2, active(6) * h6)
    cof[1, 1] = weight1
    cof[1, 0] = jnp.where(even, z_out, z_in)
    cof[1, 4] = jnp.where(even, z_in, z_out)

    sub = lax.broadcasted_iota(jnp.int32, (8, ny), 0)
    sub_even = lax.broadcasted_iota(jnp.int32, (8, ny), 1) % 2 == 0

    def row_sum(pack):
        return jnp.sum(pack, axis=0, keepdims=True)

    def gather(out, everyone, slot, rows_of):
        tile = jnp.zeros((8, ny), jnp.float32)
        for row, values in enumerate(rows_of):
            tile = jnp.where(sub == row, values, tile)
        lower = jnp.sum(jnp.where(sub_even, tile, 0.0), axis=1, keepdims=True)
        upper = jnp.sum(jnp.where(sub_even, 0.0, tile), axis=1, keepdims=True)
        tile = jnp.where(sub_even, lower, upper)
        out[...] = tile
        everyone[me] = tile
        rows = pl.ds(0, len(rows_of))

        def one(step, carry):
            pltpu.make_async_remote_copy(
                src_ref=out.at[rows],
                dst_ref=everyone.at[me, rows],
                send_sem=gather_sem.at[0, slot],
                recv_sem=gather_sem.at[1, slot],
                device_id={"slab": lax.rem(me + step, n)},
                device_id_type=MESH,
            ).start()
            return carry

        lax.fori_loop(1, n, one, 0)

    def gather_wait(everyone, side, slot, count):
        rest = everyone.at[pl.ds(0, n - 1), pl.ds(0, count)]
        pltpu.make_async_copy(rest, rest, gather_sem.at[side, slot]).wait()

    line_diag = row_sum(raw - 2.0 * (coarse_x + coarse_y))
    line_face = row_sum(cof[1, 0])
    round_end(1)
    round_start(2)

    over(3, 5, second_sweep)
    receive(next_up, next_low)
    finish(1, side_faces(1) + face_below(1) + tmp[6])
    finish(6, side_faces(6) + face_below(7) + tmp[7])
    round_end(2)
    round_start(3)
    receive(rhs_up, rhs_low)
    send(cof_up, cof_low)
    over(0, 2, lambda k: first_sweep(1 + 5 * k))
    over(0, 2, lambda k: second_sweep(2 + 3 * k))
    r3, r4 = residual(3), residual(4)

    def beside(f):
        total = coarse_x * pltpu.roll(f, 1, 0) + pltpu.roll(coarse_x * f, hx_rows - 1, 0)
        return total + coarse_y * pltpu.roll(f, 2, 1) + pltpu.roll(coarse_y * f, ny - 2, 1)

    receive(edge_up, edge_low)
    edge_part = jnp.where(even, edge[0, 0], pltpu.roll(edge[1, 0], 1, 1))
    edge_side = jnp.where(even, pltpu.roll(edge[0, 0], ny - 1, 1), edge[1, 0])
    edge_in = jnp.where(even, edge[0, 1], edge[1, 1])
    edge_diag = edge_part + outer
    edge_weight = jnp.where(edge_part > 0.0, OMEGA / jnp.where(edge_part > 0.0, edge_diag, 1.0), 0.0)
    y_out, y_in, y_own = -weight1 * z_out, -weight1 * z_in, weight1 * (diag1 - side)
    edge_y_out, edge_y_in, edge_y_own = -edge_weight * z_out, -edge_weight * edge_in, edge_weight * (edge_diag - edge_side)
    to_out2 = -weight1 * z_out * edge_y_in
    to_out1 = (OMEGA - 2.0) * y_out - weight1 * (beside(y_out) + z_out * edge_y_own)
    to_own = 1.0 + (OMEGA - 2.0) * y_own - weight1 * (beside(y_own) + z_out * edge_y_out + z_in * swap(y_in))
    to_in1 = (OMEGA - 2.0) * y_in - weight1 * (beside(y_in) + z_in * swap(y_own))
    to_in2 = -weight1 * z_in * swap(y_out)

    for r in range(3, len(rounds)):
        round_end(r)
        round_start(r + 1)
    gather(line_out, line_all, 0, (line_diag, line_face))

    receive(u1_up, u1_low)
    over(0, 2, lambda k: second_sweep(1 + 5 * k))
    own_b1 = restrict(residual(2) + r3, r4 + residual(5))
    b1[1] = own_b1

    row_even = even[:1]

    def row_swap(row):
        return jnp.where(row_even, pltpu.roll(row, ny - 1, 1), pltpu.roll(row, 1, 1))

    gather(
        row_out, row_all, 1,
        (
            row_sum(to_own * own_b1) + row_swap(row_sum(to_in1 * own_b1)),
            row_swap(row_sum(to_out1 * own_b1)) + row_sum(to_in2 * own_b1),
            row_sum(to_out2 * own_b1),
        ),
    )
    send(b1_up, b1_low)
    send(u2_up, u2_low)

    receive(cof_up, cof_low)
    cof[0, 4] = jnp.where(even, pltpu.roll(cof[0, 0], ny - 1, 1), pltpu.roll(cof[1, 0], 1, 1))
    cof[2, 0] = jnp.where(even, pltpu.roll(cof[1, 4], ny - 1, 1), pltpu.roll(cof[2, 4], 1, 1))
    receive(b1_up, b1_low)

    zero = jnp.zeros((hx_rows, ny), jnp.float32)

    def coarse_neighbours(k, below, f, above):
        cx, cy = cof[k, 2], cof[k, 3]
        zl = jnp.where(even, pltpu.roll(below, ny - 1, 1), pltpu.roll(f, 1, 1))
        zh = jnp.where(even, pltpu.roll(f, ny - 1, 1), pltpu.roll(above, 1, 1))
        total = cx * pltpu.roll(f, 1, 0)
        total = total + pltpu.roll(cx * f, hx_rows - 1, 0)
        total = total + cy * pltpu.roll(f, 2, 1)
        total = total + pltpu.roll(cy * f, ny - 2, 1)
        return total + cof[k, 0] * zl + cof[k, 4] * zh

    def coarse_sweep(fields):
        swept = []
        for k in range(3):
            total = coarse_neighbours(k, fields[k], fields[k + 1], fields[k + 2])
            swept.append((1.0 - OMEGA) * fields[k + 1] + cof[k, 1] * (b1[k] + total))
        return [zero] + swept + [zero]

    v1 = [zero] + [cof[k, 1] * b1[k] for k in range(3)] + [zero]
    v2 = coarse_sweep(v1)
    own_total = coarse_neighbours(1, v2[1], v2[2], v2[3])
    vn[1] = (1.0 - OMEGA) * v2[2] + cof[1, 1] * (b1[1] + own_total)
    send(vn_up, vn_low)

    parts = []
    for k in range(3):
        weight, cx, cy = cof[k, 1], cof[k, 2], cof[k, 3]
        around = cx + pltpu.roll(cx, hx_rows - 1, 0) + cy + pltpu.roll(cy, ny - 2, 1)
        own_part = jnp.where(weight > 0.0, 1.0 - OMEGA, 0.0) + weight * around
        parts.append((own_part, weight * cof[k, 0], weight * cof[k, 4]))

    gather_wait(line_all, 1, 0, 2)

    line_even = lax.broadcasted_iota(jnp.int32, (n, ny), 1) % 2 == 0

    def line_row(everyone, row):
        return everyone.reshape(n * 8, ny)[pl.ds(row, n, 8), :]

    def apart(both):
        lower = jnp.where(line_even, both, pltpu.roll(both, 1, 1))
        return lower, jnp.where(line_even, pltpu.roll(both, ny - 1, 1), both)

    (de, do), (fe, fo) = apart(line_row(line_all, 0)), apart(line_row(line_all, 1))

    def back(x, s):
        return pltpu.roll(x, s % n, 0)

    def ahead(x, s):
        return pltpu.roll(x, (n - s) % n, 0)

    inv_odd = 1.0 / do
    to_low = fe * back(inv_odd, 1)
    to_up = fo * inv_odd
    fe_next = ahead(fe, 1)
    diag = de - fe * to_low - fo * to_up
    lower = -to_low * back(fo, 1)
    upper = -to_up * fe_next
    steps = []
    shift = 1
    while shift < n:
        alpha, gamma = lower / back(diag, shift), upper / ahead(diag, shift)
        steps.append((shift, alpha, gamma))
        diag = diag - alpha * back(upper, shift) - gamma * ahead(lower, shift)
        lower, upper = -alpha * back(lower, shift), -gamma * ahead(upper, shift)
        shift *= 2
    inv_diag = 1.0 / diag

    receive(vn_up, vn_low)
    gather_wait(row_all, 1, 1, 3)
    one, two = line_row(row_all, 1), line_row(row_all, 2)
    sums = line_row(row_all, 0) + jnp.where(line_even, back(one, 1) + ahead(two, 1), ahead(one, 1) + back(two, 1))
    be, bo = apart(sums)
    reduced = be + to_low * back(bo, 1) + to_up * bo
    for shift, alpha, gamma in steps:
        reduced = reduced - alpha * back(reduced, shift) - gamma * ahead(reduced, shift)
    e_even = reduced * inv_diag
    e_odd = (bo + fo * e_even + fe_next * ahead(e_even, 1)) * inv_odd
    packed = jnp.where(line_even, e_even, e_odd)
    xs[0, pl.ds(8, n), :] = packed
    xs[1, pl.ds(8, n), :] = jnp.where(line_even, back(e_odd, 1), e_even)
    xs[2, pl.ds(8, n), :] = jnp.where(line_even, e_odd, ahead(e_even, 1))

    def line(slot, k):
        return jnp.broadcast_to(xs[slot, pl.ds(me + 7 + k, 1), :], (hx_rows, ny))

    w2 = [zero]
    for k, (own_part, lower_part, upper_part) in enumerate(parts):
        fixed = own_part * line(0, k) + lower_part * line(1, k) + upper_part * line(2, k)
        w2.append(vn[k] + fixed)
    w3 = coarse_sweep(w2 + [zero])

    def prolong(slot, plane):
        pro[slot, pl.ds(0, hx_rows, 2), :] = plane
        pro[slot, pl.ds(1, hx_rows, 2), :] = plane

    def lower_plane(pack):
        return jnp.where(even, pack, pltpu.roll(pack, 1, 1))

    def upper_plane(pack):
        return jnp.where(even, pltpu.roll(pack, ny - 1, 1), pack)

    prolong(0, upper_plane(w3[1]))
    prolong(1, lower_plane(w3[2]))
    prolong(2, upper_plane(w3[2]))
    prolong(3, lower_plane(w3[3]))

    receive(u2_up, u2_low)

    def correct(k):
        ua[k] = ub[k] + jnp.where(lab[k] > 0, pro[k // 2], 0.0)

    pl.when(has_up)(u1_up.wait_send)
    pl.when(has_low)(u1_low.wait_send)
    over(0, 8, correct)

    over(1, 7, sweep(ua, tmp))
    over(2, 6, sweep(tmp, out.at[0], 2))

    for upward, downward in (
        (near_up, near_low), (next_up, next_low), (rhs_up, rhs_low), (cof_up, cof_low), (b1_up, b1_low), (vn_up, vn_low),
        (u2_up, u2_low), (edge_up, edge_low),
    ):
        pl.when(has_up)(upward.wait_send)
        pl.when(has_low)(downward.wait_send)
    gather_wait(line_all, 0, 0, 2)
    gather_wait(row_all, 0, 1, 3)


def on_device(n, rhs, labels, sigma_table):
    planes, nx, ny = labels.shape
    fine = lambda count: pltpu.VMEM((count, nx, ny), jnp.float32)
    packs = lambda *counts: pltpu.VMEM((*counts, nx // 2, ny), jnp.float32)
    tiles = lambda *counts: pltpu.VMEM((*counts, 8, ny), jnp.float32)
    return pl.pallas_call(
        functools.partial(kernel, n),
        out_shape=pltpu.VMEM(rhs.shape, jnp.float32),
        in_specs=[
            pl.BlockSpec(memory_space=pl.ANY),
            pl.BlockSpec(memory_space=pl.ANY),
            pl.BlockSpec(memory_space=pl.ANY),
        ],
        out_specs=pl.BlockSpec(memory_space=pltpu.VMEM),
        scratch_shapes=[
            pltpu.VMEM((8, nx, ny), jnp.int32),
            fine(8), fine(8), fine(8), fine(8), fine(8), fine(8), fine(8), fine(8),
            fine(8), fine(4),
            packs(3, 5), packs(2, 2), packs(2, 2), packs(3), packs(3),
            tiles(), tiles(n), tiles(), tiles(n),
            pltpu.VMEM((3, n + 16, ny), jnp.float32),
            pltpu.SMEM((3, LABELS), jnp.float32),
            pltpu.SemaphoreType.DMA((3,)),
            pltpu.SemaphoreType.DMA((2, 18)),
            pltpu.SemaphoreType.DMA((2, 2)),
            pltpu.SemaphoreType.REGULAR((n.bit_length(),)),
        ],
        compiler_params=pltpu.CompilerParams(collective_id=0, has_side_effects=True),
    )(rhs, labels, sigma_table.T)


def solution(mesh):
    placed = (P("groups", "slab", None, None), P("slab", "groups", None), P())
    return jax.shard_map(
        functools.partial(on_device, mesh.shape["slab"]),
        mesh=mesh,
        in_specs=placed,
        out_specs=P("groups", "slab", None, None),
        check_vma=False,
    )
```

```python
import functools
import itertools

import jax
import jax.numpy as jnp
from jax import lax
from jax.experimental import pallas as pl
from jax.experimental.pallas import tpu as pltpu
from jax.sharding import PartitionSpec as P

OMEGA = 0.8
LABELS = 5
MESH = pl.DeviceIdType.MESH


def copy_to(src, dst, sems, slot, target):
    return pltpu.make_async_remote_copy(
        src_ref=src,
        dst_ref=dst,
        send_sem=sems.at[0, slot],
        recv_sem=sems.at[1, slot],
        device_id={"slab": target},
        device_id_type=MESH,
    )


def kernel(
    n, rhs_hbm, lab_hbm, table_hbm, out,
    lab, rhs, gx, gy, gz, idf, dg, ua, ub, tmp, pro,
    part, edge, far_out, far, ends, begin, vn, spread, line_out, line_all, row_out, row_all, xs, table,
    load_sem, sems, gather_sem,
):
    me = lax.axis_index("slab")
    nx, ny = lab.shape[1:]
    hx_rows = nx // 2
    has_low, has_up = me > 0, me < n - 1

    load_table = pltpu.make_async_copy(table_hbm, table, load_sem.at[2])
    load_table.start()
    own_lab = pltpu.make_async_copy(lab_hbm, lab.at[pl.ds(2, 4)], load_sem.at[0])
    own_rhs = pltpu.make_async_copy(rhs_hbm.at[0], rhs.at[pl.ds(2, 4)], load_sem.at[1])
    own_lab.start()
    own_rhs.start()
    barrier = pltpu.get_barrier_semaphore()

    up, low = lax.rem(me + 1, n), lax.rem(me + n - 1, n)

    def greet(step, carry):
        pl.semaphore_signal(barrier, inc=1, device_id={"slab": lax.rem(me + step, n)}, device_id_type=MESH)
        return carry

    lax.fori_loop(1, n, greet, 0)
    pl.semaphore_wait(barrier, n - 1)

    near_up = copy_to(lab_hbm.at[3], lab.at[1], sems, 0, up)
    near_low = copy_to(lab_hbm.at[0], lab.at[6], sems, 1, low)
    next_up = copy_to(lab_hbm.at[2], lab.at[0], sems, 2, up)
    next_low = copy_to(lab_hbm.at[1], lab.at[7], sems, 3, low)
    rhs_up = copy_to(rhs_hbm.at[0, 3], rhs.at[1], sems, 4, up)
    rhs_low = copy_to(rhs_hbm.at[0, 0], rhs.at[6], sems, 5, low)
    u1_up = copy_to(ua.at[4], ua.at[0], sems, 6, up)
    u1_low = copy_to(ua.at[3], ua.at[7], sems, 7, low)
    far_up = copy_to(far_out.at[0], far.at[0], sems, 8, up)
    far_low = copy_to(far_out.at[1], far.at[1], sems, 9, low)
    ends_up = copy_to(begin.at[0], ends.at[0], sems, 10, up)
    ends_low = copy_to(begin.at[1], ends.at[1], sems, 11, low)
    u2_up = copy_to(ub.at[4], ub.at[0], sems, 12, up)
    u2_low = copy_to(ub.at[3], ub.at[7], sems, 13, low)
    vn_up = copy_to(vn.at[1], vn.at[0], sems, 14, up)
    vn_low = copy_to(vn.at[1], vn.at[2], sems, 15, low)
    edge_up = copy_to(part.at[0], edge.at[0], sems, 16, up)
    edge_low = copy_to(part.at[1], edge.at[1], sems, 17, low)

    def send(upward, downward):
        pl.when(has_up)(upward.start)
        pl.when(has_low)(downward.start)

    def receive(upward, downward):
        pl.when(has_low)(upward.wait_recv)
        pl.when(has_up)(downward.wait_recv)

    send(near_up, near_low)
    send(next_up, next_low)
    send(rhs_up, rhs_low)

    def clear(ref, first, count):
        for k in range(first, first + count):
            ref[k] = jnp.zeros(ref.shape[1:], ref.dtype)

    @pl.when(me == 0)
    def _():
        clear(lab, 0, 2)
        clear(rhs, 1, 1)
        clear(ua, 0, 1)
        clear(edge.at[0], 0, 2)
        clear(far, 0, 1)
        clear(ends, 0, 1)
        clear(ub, 0, 1)
        clear(vn, 0, 1)

    @pl.when(me == n - 1)
    def _():
        clear(lab, 6, 2)
        clear(rhs, 6, 1)
        clear(ua, 7, 1)
        clear(edge.at[1], 0, 2)
        clear(far, 1, 1)
        clear(ends, 1, 1)
        clear(ub, 7, 1)
        clear(vn, 2, 1)

    xs[...] = jnp.zeros(xs.shape, xs.dtype)

    fine_row = lax.broadcasted_iota(jnp.int32, (nx, ny), 0) % 2 == 1
    fine_lane = lax.broadcasted_iota(jnp.int32, (nx, ny), 1) % 2 == 1
    even = lax.broadcasted_iota(jnp.int32, (hx_rows, ny), 1) % 2 == 0

    def select(values, column):
        chosen = jnp.full(values.shape, table[column, 0], jnp.float32)
        for tissue in range(1, LABELS):
            chosen = jnp.where(values == tissue, table[column, tissue], chosen)
        return chosen

    def harmonic(a, b):
        return 2.0 * a * b / (a + b)

    def active(k):
        return (lab[k] > 0).astype(jnp.float32)

    def side_faces(k):
        here = lab[k]
        a = (here > 0).astype(jnp.float32)
        sx, sy = select(here, 0), select(here, 1)
        hx = harmonic(pltpu.roll(sx, 1, 0), sx)
        gx[k] = hx * a * pltpu.roll(a, 1, 0)
        hy = harmonic(pltpu.roll(sy, 1, 1), sy)
        gy[k] = hy * a * pltpu.roll(a, 1, 1)
        return hx + pltpu.roll(hx, nx - 1, 0) + hy + pltpu.roll(hy, ny - 1, 1)

    def face_below(k):
        h = harmonic(select(lab[k - 1], 2), select(lab[k], 2))
        gz[k] = h * active(k - 1) * active(k)
        return h

    def finish(k, faces):
        a = active(k)
        diagonal = a * faces + (1.0 - a)
        dg[k] = diagonal
        idf[k] = OMEGA * a / diagonal

    def over(first, last, body):
        for k in range(first, last):
            body(k)

    def first_sweep(k):
        ua[k] = idf[k] * rhs[k]

    def neighbours(field, k):
        u = field[k]
        cx, cy = gx[k], gy[k]
        total = cx * pltpu.roll(u, 1, 0) + pltpu.roll(cx * u, nx - 1, 0)
        total = total + cy * pltpu.roll(u, 1, 1) + pltpu.roll(cy * u, ny - 1, 1)
        return u, total + gz[k] * field[k - 1] + gz[k + 1] * field[k + 1]

    def sweep(src, dst, shift=0):
        def body(k):
            u, total = neighbours(src, k)
            dst[k - shift] = (1.0 - OMEGA) * u + idf[k] * (rhs[k] + total)

        return body

    def residual(k):
        u, total = neighbours(ub, k)
        return jnp.where(idf[k] > 0.0, rhs[k] - dg[k] * u + total, 0.0)

    second_sweep = sweep(ua, ub)

    load_table.wait()
    own_lab.wait()
    h3, h4, h5 = face_below(3), face_below(4), face_below(5)
    finish(3, side_faces(3) + h3 + h4)
    finish(4, side_faces(4) + h4 + h5)
    dg[2] = side_faces(2) + h3
    dg[5] = side_faces(5) + h5
    own_rhs.wait()
    over(3, 5, first_sweep)

    turn = itertools.count()

    def rows_apart(plane):
        slot = next(turn) % 6
        tmp[slot] = plane
        return tmp[slot, pl.ds(0, hx_rows, 2), :], tmp[slot, pl.ds(1, hx_rows, 2), :]

    def rows_even(plane):
        return rows_apart(plane)[0]

    def rows_sum(plane):
        first, second = rows_apart(plane)
        return first + second

    def lanes_sum(t0, t1):
        return jnp.where(even, t0 + pltpu.roll(t0, ny - 1, 1), t1 + pltpu.roll(t1, 1, 1))

    def lanes_even(t0, t1):
        return jnp.where(even, t0, pltpu.roll(t1, 1, 1))

    def restrict(p0, p1):
        return lanes_sum(rows_sum(p0), rows_sum(p1))

    def inner(k):
        doubled = jnp.where(fine_row, gx[k], 0.0) + jnp.where(fine_lane, gy[k], 0.0)
        if k % 2 == 1:
            doubled = doubled + gz[k]
        return active(k) * dg[k] - 2.0 * doubled

    def to_even(pack):
        return pltpu.roll(pack, ny - 1, 1)

    def to_odd(pack):
        return pltpu.roll(pack, 1, 1)

    def swap(pack):
        return jnp.where(even, to_even(pack), to_odd(pack))

    def of_odd(a, b):
        return jnp.where(even, to_even(a), b)

    def of_even(a, b):
        return jnp.where(even, a, to_odd(b))

    def beside(field, cx, cy):
        total = cx * pltpu.roll(field, 1, 0) + pltpu.roll(cx * field, hx_rows - 1, 0)
        return total + cy * pltpu.roll(field, 2, 1) + pltpu.roll(cy * field, ny - 2, 1)

    def side_sum(cx, cy):
        return cx + pltpu.roll(cx, hx_rows - 1, 0) + cy + pltpu.roll(cy, ny - 2, 1)

    raw_part = restrict(inner(2) + inner(3), inner(4) + inner(5))
    coarse_x = lanes_sum(rows_even(gx[2] + gx[3]), rows_even(gx[4] + gx[5]))
    coarse_y = lanes_even(rows_sum(gy[2] + gy[3]), rows_sum(gy[4] + gy[5]))
    middle = rows_sum(gz[4])
    z_in = lanes_sum(middle, middle)
    part[0, 0] = of_odd(raw_part, z_in)
    part[0, 1] = of_odd(coarse_x, coarse_y)
    part[1, 0] = of_even(raw_part, z_in)
    part[1, 1] = of_even(coarse_x, coarse_y)
    send(edge_up, edge_low)
    send(u1_up, u1_low)
    side = side_sum(coarse_x, coarse_y)

    receive(near_up, near_low)
    h2, h6 = face_below(2), face_below(6)
    tmp[6] = h2
    tmp[7] = h6
    finish(2, dg[2] + h2)
    finish(5, dg[5] + h6)
    over(0, 2, lambda k: first_sweep(2 + 3 * k))
    over(3, 5, second_sweep)
    send(u2_up, u2_low)
    raw = raw_part + restrict(active(2) * h2, active(5) * h6)
    active1 = jnp.where(raw_part > 0.0, 1.0, 0.0)
    diag1 = raw + (1.0 - active1)
    weight = OMEGA * active1 / diag1
    z_out = restrict(gz[2], gz[6])
    outer = restrict(active(1) * h2, active(6) * h6)
    own_part, out_part, in_part = (1.0 - OMEGA) * active1 + weight * side, weight * z_out, weight * z_in
    spread[...] = in_part
    in_first, in_second = spread[pl.ds(0, hx_rows // 2, 2), :], spread[pl.ds(1, hx_rows // 2, 2), :]
    even_half = even[: hx_rows // 2]
    far_out[0, pl.ds(0, hx_rows)] = of_even(own_part, out_part)
    far_out[0, pl.ds(hx_rows, hx_rows // 2)] = jnp.where(even_half, in_first, to_odd(in_second))
    far_out[1, pl.ds(0, hx_rows)] = of_odd(own_part, out_part)
    far_out[1, pl.ds(hx_rows, hx_rows // 2)] = jnp.where(even_half, to_even(in_first), in_second)
    send(far_up, far_low)

    sub = lax.broadcasted_iota(jnp.int32, (8, ny), 0)
    sub_even = lax.broadcasted_iota(jnp.int32, (8, ny), 1) % 2 == 0

    def row_sum(pack):
        return jnp.sum(pack, axis=0, keepdims=True)

    def gather(out, everyone, slot, rows_of):
        tile = jnp.zeros((8, ny), jnp.float32)
        for row, values in enumerate(rows_of):
            tile = jnp.where(sub == row, values, tile)
        lower = jnp.sum(jnp.where(sub_even, tile, 0.0), axis=1, keepdims=True)
        upper = jnp.sum(jnp.where(sub_even, 0.0, tile), axis=1, keepdims=True)
        tile = jnp.where(sub_even, lower, upper)
        out[...] = tile
        everyone[me] = tile
        rows = pl.ds(0, len(rows_of))

        def one(step, carry):
            pltpu.make_async_remote_copy(
                src_ref=out.at[rows],
                dst_ref=everyone.at[me, rows],
                send_sem=gather_sem.at[0, slot],
                recv_sem=gather_sem.at[1, slot],
                device_id={"slab": lax.rem(me + step, n)},
                device_id_type=MESH,
            ).start()
            return carry

        lax.fori_loop(1, n, one, 0)

    def gather_wait(everyone, side, slot, count):
        rest = everyone.at[pl.ds(0, n - 1), pl.ds(0, count)]
        pltpu.make_async_copy(rest, rest, gather_sem.at[side, slot]).wait()

    gather(line_out, line_all, 0, (row_sum(raw - 2.0 * (coarse_x + coarse_y)), row_sum(jnp.where(even, z_out, z_in))))

    receive(next_up, next_low)
    finish(1, side_faces(1) + face_below(1) + tmp[6])
    finish(6, side_faces(6) + face_below(7) + tmp[7])
    receive(rhs_up, rhs_low)
    over(0, 2, lambda k: first_sweep(1 + 5 * k))
    over(0, 2, lambda k: second_sweep(2 + 3 * k))
    r3, r4 = residual(3), residual(4)

    def split(both):
        below, above = both
        return jnp.where(even, below, to_odd(above)), jnp.where(even, to_even(below), above)

    receive(edge_up, edge_low)
    edge_raw, edge_in = split((edge[0, 0], edge[1, 0]))
    edge_x, edge_y = split((edge[0, 1], edge[1, 1]))
    edge_side = side_sum(edge_x, edge_y)
    edge_diag = edge_raw + outer
    edge_active = edge_raw > 0.0
    edge_weight = jnp.where(edge_active, OMEGA / jnp.where(edge_active, edge_diag, 1.0), 0.0)
    own_1 = weight * (diag1 - side)
    edge_own_1, edge_out_1, edge_in_1 = edge_weight * (edge_diag - edge_side), edge_weight * z_out, edge_weight * edge_in
    to_out2 = out_part * edge_in_1
    to_out1 = (2.0 - OMEGA) * out_part + weight * beside(out_part, coarse_x, coarse_y) - out_part * edge_own_1
    to_own = 1.0 + (OMEGA - 2.0) * own_1 - weight * beside(own_1, coarse_x, coarse_y) + out_part * edge_out_1 + in_part * swap(in_part)
    to_in1 = (2.0 - OMEGA) * in_part + weight * beside(in_part, coarse_x, coarse_y) - in_part * swap(own_1)
    to_in2 = in_part * swap(out_part)
    edge_own_part = jnp.where(edge_active, 1.0 - OMEGA, 0.0) + edge_weight * edge_side

    receive(u1_up, u1_low)
    over(0, 2, lambda k: second_sweep(1 + 5 * k))
    b1 = restrict(residual(2) + r3, r4 + residual(5))

    row_even = even[:1]

    def row_swap(row):
        return jnp.where(row_even, to_even(row), to_odd(row))

    gather(
        row_out, row_all, 1,
        (
            row_sum(to_own * b1) + row_swap(row_sum(to_in1 * b1)),
            row_swap(row_sum(to_out1 * b1)) + row_sum(to_in2 * b1),
            row_sum(to_out2 * b1),
        ),
    )
    v1 = weight * b1
    begin[0] = jnp.where(even, to_even(b1), to_odd(v1))
    begin[1] = jnp.where(even, b1, v1)
    send(ends_up, ends_low)

    def own_sweep(own, beyond):
        total = beside(own, coarse_x, coarse_y) + z_out * beyond + z_in * swap(own)
        return (1.0 - OMEGA) * own + weight * (b1 + total)

    def edge_sweep(own, beyond, further):
        total = beside(beyond, edge_x, edge_y) + z_out * own + edge_in * further
        return (1.0 - OMEGA) * beyond + edge_weight * (edge_b1 + total)

    receive(ends_up, ends_low)
    edge_b1, far_v1 = split((ends[0], ends[1]))
    edge_v1 = edge_weight * edge_b1
    v2, edge_v2 = own_sweep(v1, edge_v1), edge_sweep(v1, edge_v1, far_v1)
    v3 = own_sweep(v2, edge_v2)
    vn[1] = v3
    send(vn_up, vn_low)

    receive(far_up, far_low)
    far_own_part, far_out_part = split((far[0, pl.ds(0, hx_rows)], far[1, pl.ds(0, hx_rows)]))
    below, above = far[0, pl.ds(hx_rows, hx_rows // 2)], far[1, pl.ds(hx_rows, hx_rows // 2)]
    spread[pl.ds(0, hx_rows // 2, 2), :] = jnp.where(even_half, below, to_odd(above))
    spread[pl.ds(1, hx_rows // 2, 2), :] = jnp.where(even_half, to_even(below), above)

    gather_wait(line_all, 1, 0, 2)

    line_even = lax.broadcasted_iota(jnp.int32, (n, ny), 1) % 2 == 0

    def line_row(everyone, row):
        return everyone.reshape(n * 8, ny)[pl.ds(row, n, 8), :]

    def apart(both):
        lower = jnp.where(line_even, both, pltpu.roll(both, 1, 1))
        return lower, jnp.where(line_even, pltpu.roll(both, ny - 1, 1), both)

    (de, do), (fe, fo) = apart(line_row(line_all, 0)), apart(line_row(line_all, 1))

    def back(x, s):
        return pltpu.roll(x, s % n, 0)

    def ahead(x, s):
        return pltpu.roll(x, (n - s) % n, 0)

    inv_odd = 1.0 / do
    to_low = fe * back(inv_odd, 1)
    to_up = fo * inv_odd
    fe_next = ahead(fe, 1)
    diag = de - fe * to_low - fo * to_up
    lower = -to_low * back(fo, 1)
    upper = -to_up * fe_next
    steps = []
    shift = 1
    while shift < n:
        alpha, gamma = lower / back(diag, shift), upper / ahead(diag, shift)
        steps.append((shift, alpha, gamma))
        diag = diag - alpha * back(upper, shift) - gamma * ahead(lower, shift)
        lower, upper = -alpha * back(lower, shift), -gamma * ahead(upper, shift)
        shift *= 2
    inv_diag = 1.0 / diag

    gather_wait(row_all, 1, 1, 3)
    one, two = line_row(row_all, 1), line_row(row_all, 2)
    sums = line_row(row_all, 0) + jnp.where(line_even, back(one, 1) + ahead(two, 1), ahead(one, 1) + back(two, 1))
    be, bo = apart(sums)
    reduced = be + to_low * back(bo, 1) + to_up * bo
    for shift, alpha, gamma in steps:
        reduced = reduced - alpha * back(reduced, shift) - gamma * ahead(reduced, shift)
    e_even = reduced * inv_diag
    e_odd = (bo + fo * e_even + fe_next * ahead(e_even, 1)) * inv_odd
    xs[0, pl.ds(8, n), :] = jnp.where(line_even, e_even, e_odd)
    xs[1, pl.ds(8, n), :] = jnp.where(line_even, e_odd, e_even)

    def line(side, distance):
        return jnp.broadcast_to(xs[side, pl.ds(me + 8 + distance, 1), :], (hx_rows, ny))

    def outward(side, distance):
        return jnp.where(even, line(side, -distance), line(side, distance))

    e_own, e_in = line(0, 0), line(1, 0)
    e_out, e_out2, e_out3 = outward(1, 1), outward(0, 1), outward(1, 2)
    receive(vn_up, vn_low)
    below, above = vn[0], vn[2]
    w2 = v3 + own_part * e_own + out_part * e_out + in_part * e_in
    edge_w2 = jnp.where(even, to_even(below), to_odd(above))
    edge_w2 = edge_w2 + edge_own_part * e_out + edge_out_1 * e_own + edge_in_1 * e_out2
    far_w2 = jnp.where(even, below, above) + far_own_part * e_out2 + spread[...] * e_out + far_out_part * e_out3
    w3, edge_w3 = own_sweep(w2, edge_w2), edge_sweep(w2, edge_w2, far_w2)

    def prolong(slot, plane):
        pro[slot, pl.ds(0, hx_rows, 2), :] = plane
        pro[slot, pl.ds(1, hx_rows, 2), :] = plane

    def lower_plane(pack):
        return jnp.where(even, pack, pltpu.roll(pack, 1, 1))

    def upper_plane(pack):
        return jnp.where(even, pltpu.roll(pack, ny - 1, 1), pack)

    prolong(0, lower_plane(edge_w3))
    prolong(1, lower_plane(w3))
    prolong(2, upper_plane(w3))
    prolong(3, upper_plane(edge_w3))

    receive(u2_up, u2_low)

    def correct(k):
        ua[k] = ub[k] + jnp.where(lab[k] > 0, pro[k // 2], 0.0)

    pl.when(has_up)(u1_up.wait_send)
    pl.when(has_low)(u1_low.wait_send)
    over(0, 8, correct)

    over(1, 7, sweep(ua, tmp))
    over(2, 6, sweep(tmp, out.at[0], 2))

    for upward, downward in (
        (near_up, near_low), (next_up, next_low), (rhs_up, rhs_low), (far_up, far_low), (ends_up, ends_low), (vn_up, vn_low),
        (u2_up, u2_low), (edge_up, edge_low),
    ):
        pl.when(has_up)(upward.wait_send)
        pl.when(has_low)(downward.wait_send)
    gather_wait(line_all, 0, 0, 2)
    gather_wait(row_all, 0, 1, 3)


def on_device(n, rhs, labels, sigma_table):
    planes, nx, ny = labels.shape
    fine = lambda count: pltpu.VMEM((count, nx, ny), jnp.float32)
    packs = lambda *counts: pltpu.VMEM((*counts, nx // 2, ny), jnp.float32)
    thirds = lambda *counts: pltpu.VMEM((*counts, nx // 2 + nx // 4, ny), jnp.float32)
    tiles = lambda *counts: pltpu.VMEM((*counts, 8, ny), jnp.float32)
    return pl.pallas_call(
        functools.partial(kernel, n),
        out_shape=pltpu.VMEM(rhs.shape, jnp.float32),
        in_specs=[
            pl.BlockSpec(memory_space=pl.ANY),
            pl.BlockSpec(memory_space=pl.ANY),
            pl.BlockSpec(memory_space=pl.ANY),
        ],
        out_specs=pl.BlockSpec(memory_space=pltpu.VMEM),
        scratch_shapes=[
            pltpu.VMEM((8, nx, ny), jnp.int32),
            fine(8), fine(8), fine(8), fine(8), fine(8), fine(8), fine(8), fine(8),
            fine(8), fine(4),
            packs(2, 2), packs(2, 2), thirds(2), thirds(2), packs(2), packs(2), packs(3), packs(),
            tiles(), tiles(n), tiles(), tiles(n),
            pltpu.VMEM((2, n + 16, ny), jnp.float32),
            pltpu.SMEM((3, LABELS), jnp.float32),
            pltpu.SemaphoreType.DMA((3,)),
            pltpu.SemaphoreType.DMA((2, 18)),
            pltpu.SemaphoreType.DMA((2, 2)),
        ],
        compiler_params=pltpu.CompilerParams(collective_id=0, has_side_effects=True),
    )(rhs, labels, sigma_table.T)


def solution(mesh):
    placed = (P("groups", "slab", None, None), P("slab", "groups", None), P())
    return jax.shard_map(
        functools.partial(on_device, mesh.shape["slab"]),
        mesh=mesh,
        in_specs=placed,
        out_specs=P("groups", "slab", None, None),
        check_vma=False,
    )
```

```python
import functools
import itertools

import jax
import jax.numpy as jnp
from jax import lax
from jax.experimental import pallas as pl
from jax.experimental.pallas import tpu as pltpu
from jax.sharding import PartitionSpec as P

OMEGA = 0.8
LABELS = 5
MESH = pl.DeviceIdType.MESH
REACH = 4


def copy_to(src, dst, sems, slot, target):
    return pltpu.make_async_remote_copy(
        src_ref=src,
        dst_ref=dst,
        send_sem=sems.at[0, slot],
        recv_sem=sems.at[1, slot],
        device_id={"slab": target},
        device_id_type=MESH,
    )


def kernel(
    n, rhs_hbm, lab_hbm, table_hbm, out,
    lab, rhs, gx, gy, gz, idf, dg, ua, ub, tmp, pro,
    part, edge, far_out, far, ends, begin, vn, spread, line_out, line_all, row_out, row_all, xs, table,
    load_sem, sems, gather_sem, tokens,
):
    me = lax.axis_index("slab")
    nx, ny = lab.shape[1:]
    hx_rows = nx // 2
    has_low, has_up = me > 0, me < n - 1

    load_table = pltpu.make_async_copy(table_hbm, table, load_sem.at[2])
    load_table.start()
    own_lab = pltpu.make_async_copy(lab_hbm, lab.at[pl.ds(2, 4)], load_sem.at[0])
    own_rhs = pltpu.make_async_copy(rhs_hbm.at[0], rhs.at[pl.ds(2, 4)], load_sem.at[1])
    own_lab.start()
    own_rhs.start()
    barrier = pltpu.get_barrier_semaphore()

    up, low = lax.rem(me + 1, n), lax.rem(me + n - 1, n)

    def signal(sem, distance):
        for near, other in ((me >= distance, me - distance), (me + distance < n, me + distance)):

            @pl.when(near)
            def _():
                pl.semaphore_signal(sem, inc=1, device_id={"slab": other}, device_id_type=MESH)

    for distance in range(1, min(REACH, n - 1) + 1):
        signal(barrier, distance)
    pl.semaphore_wait(barrier, jnp.minimum(me, REACH) + jnp.minimum(n - 1 - me, REACH))

    rounds = []
    while REACH * 2 ** len(rounds) < n - 1:
        rounds.append(REACH * 2 ** len(rounds))

    def round_start(r):
        if r < len(rounds):
            signal(tokens.at[r], rounds[r])

    def round_end(r):
        if r < len(rounds):
            distance = rounds[r]
            both = jnp.logical_and(me >= distance, me + distance < n)
            one = jnp.logical_xor(me >= distance, me + distance < n)
            pl.when(both)(lambda: pl.semaphore_wait(tokens.at[r], 2))
            pl.when(one)(lambda: pl.semaphore_wait(tokens.at[r], 1))

    near_up = copy_to(lab_hbm.at[3], lab.at[1], sems, 0, up)
    near_low = copy_to(lab_hbm.at[0], lab.at[6], sems, 1, low)
    next_up = copy_to(lab_hbm.at[2], lab.at[0], sems, 2, up)
    next_low = copy_to(lab_hbm.at[1], lab.at[7], sems, 3, low)
    rhs_up = copy_to(rhs_hbm.at[0, 3], rhs.at[1], sems, 4, up)
    rhs_low = copy_to(rhs_hbm.at[0, 0], rhs.at[6], sems, 5, low)
    u1_up = copy_to(ua.at[4], ua.at[0], sems, 6, up)
    u1_low = copy_to(ua.at[3], ua.at[7], sems, 7, low)
    far_up = copy_to(far_out.at[0], far.at[0], sems, 8, up)
    far_low = copy_to(far_out.at[1], far.at[1], sems, 9, low)
    ends_up = copy_to(begin.at[0], ends.at[0], sems, 10, up)
    ends_low = copy_to(begin.at[1], ends.at[1], sems, 11, low)
    u2_up = copy_to(ub.at[4], ub.at[0], sems, 12, up)
    u2_low = copy_to(ub.at[3], ub.at[7], sems, 13, low)
    vn_up = copy_to(vn.at[1], vn.at[0], sems, 14, up)
    vn_low = copy_to(vn.at[1], vn.at[2], sems, 15, low)
    edge_up = copy_to(part.at[0], edge.at[0], sems, 16, up)
    edge_low = copy_to(part.at[1], edge.at[1], sems, 17, low)

    def send(upward, downward):
        pl.when(has_up)(upward.start)
        pl.when(has_low)(downward.start)

    def receive(upward, downward):
        pl.when(has_low)(upward.wait_recv)
        pl.when(has_up)(downward.wait_recv)

    send(near_up, near_low)
    send(next_up, next_low)
    send(rhs_up, rhs_low)
    round_start(0)

    def clear(ref, first, count):
        for k in range(first, first + count):
            ref[k] = jnp.zeros(ref.shape[1:], ref.dtype)

    @pl.when(me == 0)
    def _():
        clear(lab, 0, 2)
        clear(rhs, 1, 1)
        clear(ua, 0, 1)
        clear(edge.at[0], 0, 2)
        clear(far, 0, 1)
        clear(ends, 0, 1)
        clear(ub, 0, 1)
        clear(vn, 0, 1)

    @pl.when(me == n - 1)
    def _():
        clear(lab, 6, 2)
        clear(rhs, 6, 1)
        clear(ua, 7, 1)
        clear(edge.at[1], 0, 2)
        clear(far, 1, 1)
        clear(ends, 1, 1)
        clear(ub, 7, 1)
        clear(vn, 2, 1)

    xs[...] = jnp.zeros(xs.shape, xs.dtype)

    fine_row = lax.broadcasted_iota(jnp.int32, (nx, ny), 0) % 2 == 1
    fine_lane = lax.broadcasted_iota(jnp.int32, (nx, ny), 1) % 2 == 1
    even = lax.broadcasted_iota(jnp.int32, (hx_rows, ny), 1) % 2 == 0

    def select(values, column):
        chosen = jnp.full(values.shape, table[column, 0], jnp.float32)
        for tissue in range(1, LABELS):
            chosen = jnp.where(values == tissue, table[column, tissue], chosen)
        return chosen

    def harmonic(a, b):
        return 2.0 * a * b / (a + b)

    def active(k):
        return (lab[k] > 0).astype(jnp.float32)

    def side_faces(k):
        here = lab[k]
        a = (here > 0).astype(jnp.float32)
        sx, sy = select(here, 0), select(here, 1)
        hx = harmonic(pltpu.roll(sx, 1, 0), sx)
        gx[k] = hx * a * pltpu.roll(a, 1, 0)
        hy = harmonic(pltpu.roll(sy, 1, 1), sy)
        gy[k] = hy * a * pltpu.roll(a, 1, 1)
        return hx + pltpu.roll(hx, nx - 1, 0) + hy + pltpu.roll(hy, ny - 1, 1)

    def face_below(k):
        h = harmonic(select(lab[k - 1], 2), select(lab[k], 2))
        gz[k] = h * active(k - 1) * active(k)
        return h

    def finish(k, faces):
        a = active(k)
        diagonal = a * faces + (1.0 - a)
        dg[k] = diagonal
        idf[k] = OMEGA * a / diagonal

    def over(first, last, body):
        for k in range(first, last):
            body(k)

    def first_sweep(k):
        ua[k] = idf[k] * rhs[k]

    def neighbours(field, k):
        u = field[k]
        cx, cy = gx[k], gy[k]
        total = cx * pltpu.roll(u, 1, 0) + pltpu.roll(cx * u, nx - 1, 0)
        total = total + cy * pltpu.roll(u, 1, 1) + pltpu.roll(cy * u, ny - 1, 1)
        return u, total + gz[k] * field[k - 1] + gz[k + 1] * field[k + 1]

    def sweep(src, dst, shift=0):
        def body(k):
            u, total = neighbours(src, k)
            dst[k - shift] = (1.0 - OMEGA) * u + idf[k] * (rhs[k] + total)

        return body

    def residual(k):
        u, total = neighbours(ub, k)
        return jnp.where(idf[k] > 0.0, rhs[k] - dg[k] * u + total, 0.0)

    second_sweep = sweep(ua, ub)

    load_table.wait()
    own_lab.wait()
    h3, h4, h5 = face_below(3), face_below(4), face_below(5)
    finish(3, side_faces(3) + h3 + h4)
    finish(4, side_faces(4) + h4 + h5)
    dg[2] = side_faces(2) + h3
    dg[5] = side_faces(5) + h5
    own_rhs.wait()
    over(3, 5, first_sweep)

    turn = itertools.count()

    def rows_apart(plane):
        slot = next(turn) % 6
        tmp[slot] = plane
        return tmp[slot, pl.ds(0, hx_rows, 2), :], tmp[slot, pl.ds(1, hx_rows, 2), :]

    def rows_even(plane):
        return rows_apart(plane)[0]

    def rows_sum(plane):
        first, second = rows_apart(plane)
        return first + second

    def lanes_sum(t0, t1):
        return jnp.where(even, t0 + pltpu.roll(t0, ny - 1, 1), t1 + pltpu.roll(t1, 1, 1))

    def lanes_even(t0, t1):
        return jnp.where(even, t0, pltpu.roll(t1, 1, 1))

    def restrict(p0, p1):
        return lanes_sum(rows_sum(p0), rows_sum(p1))

    def inner(k):
        doubled = jnp.where(fine_row, gx[k], 0.0) + jnp.where(fine_lane, gy[k], 0.0)
        if k % 2 == 1:
            doubled = doubled + gz[k]
        return active(k) * dg[k] - 2.0 * doubled

    def to_even(pack):
        return pltpu.roll(pack, ny - 1, 1)

    def to_odd(pack):
        return pltpu.roll(pack, 1, 1)

    def swap(pack):
        return jnp.where(even, to_even(pack), to_odd(pack))

    def of_odd(a, b):
        return jnp.where(even, to_even(a), b)

    def of_even(a, b):
        return jnp.where(even, a, to_odd(b))

    def beside(field, cx, cy):
        total = cx * pltpu.roll(field, 1, 0) + pltpu.roll(cx * field, hx_rows - 1, 0)
        return total + cy * pltpu.roll(field, 2, 1) + pltpu.roll(cy * field, ny - 2, 1)

    def side_sum(cx, cy):
        return cx + pltpu.roll(cx, hx_rows - 1, 0) + cy + pltpu.roll(cy, ny - 2, 1)

    raw_part = restrict(inner(2) + inner(3), inner(4) + inner(5))
    coarse_x = lanes_sum(rows_even(gx[2] + gx[3]), rows_even(gx[4] + gx[5]))
    coarse_y = lanes_even(rows_sum(gy[2] + gy[3]), rows_sum(gy[4] + gy[5]))
    middle = rows_sum(gz[4])
    z_in = lanes_sum(middle, middle)
    part[0, 0] = of_odd(raw_part, z_in)
    part[0, 1] = of_odd(coarse_x, coarse_y)
    part[1, 0] = of_even(raw_part, z_in)
    part[1, 1] = of_even(coarse_x, coarse_y)
    send(edge_up, edge_low)
    send(u1_up, u1_low)
    side = side_sum(coarse_x, coarse_y)

    round_end(0)
    round_start(1)
    receive(near_up, near_low)
    h2, h6 = face_below(2), face_below(6)
    tmp[6] = h2
    tmp[7] = h6
    finish(2, dg[2] + h2)
    finish(5, dg[5] + h6)
    over(0, 2, lambda k: first_sweep(2 + 3 * k))
    over(3, 5, second_sweep)
    raw = raw_part + restrict(active(2) * h2, active(5) * h6)
    active1 = jnp.where(raw_part > 0.0, 1.0, 0.0)
    diag1 = raw + (1.0 - active1)
    weight = OMEGA * active1 / diag1
    z_out = restrict(gz[2], gz[6])
    outer = restrict(active(1) * h2, active(6) * h6)
    own_part, out_part, in_part = (1.0 - OMEGA) * active1 + weight * side, weight * z_out, weight * z_in
    spread[...] = in_part
    in_first, in_second = spread[pl.ds(0, hx_rows // 2, 2), :], spread[pl.ds(1, hx_rows // 2, 2), :]
    even_half = even[: hx_rows // 2]
    far_out[0, pl.ds(0, hx_rows)] = of_even(own_part, out_part)
    far_out[0, pl.ds(hx_rows, hx_rows // 2)] = jnp.where(even_half, in_first, to_odd(in_second))
    far_out[1, pl.ds(0, hx_rows)] = of_odd(own_part, out_part)
    far_out[1, pl.ds(hx_rows, hx_rows // 2)] = jnp.where(even_half, to_even(in_first), in_second)
    send(far_up, far_low)

    sub = lax.broadcasted_iota(jnp.int32, (8, ny), 0)
    sub_even = lax.broadcasted_iota(jnp.int32, (8, ny), 1) % 2 == 0

    def row_sum(pack):
        return jnp.sum(pack, axis=0, keepdims=True)

    def gather(out, everyone, slot, rows_of):
        tile = jnp.zeros((8, ny), jnp.float32)
        for row, values in enumerate(rows_of):
            tile = jnp.where(sub == row, values, tile)
        lower = jnp.sum(jnp.where(sub_even, tile, 0.0), axis=1, keepdims=True)
        upper = jnp.sum(jnp.where(sub_even, 0.0, tile), axis=1, keepdims=True)
        tile = jnp.where(sub_even, lower, upper)
        out[...] = tile
        everyone[me] = tile
        rows = pl.ds(0, len(rows_of))

        def one(step, carry):
            pltpu.make_async_remote_copy(
                src_ref=out.at[rows],
                dst_ref=everyone.at[me, rows],
                send_sem=gather_sem.at[0, slot],
                recv_sem=gather_sem.at[1, slot],
                device_id={"slab": lax.rem(me + step, n)},
                device_id_type=MESH,
            ).start()
            return carry

        lax.fori_loop(1, n, one, 0)

    def gather_wait(everyone, side, slot, count):
        rest = everyone.at[pl.ds(0, n - 1), pl.ds(0, count)]
        pltpu.make_async_copy(rest, rest, gather_sem.at[side, slot]).wait()

    line_sums = (row_sum(raw - 2.0 * (coarse_x + coarse_y)), row_sum(jnp.where(even, z_out, z_in)))
    round_end(1)
    round_start(2)

    receive(next_up, next_low)
    finish(1, side_faces(1) + face_below(1) + tmp[6])
    finish(6, side_faces(6) + face_below(7) + tmp[7])
    receive(rhs_up, rhs_low)
    round_end(2)
    round_start(3)
    over(0, 2, lambda k: first_sweep(1 + 5 * k))
    over(0, 2, lambda k: second_sweep(2 + 3 * k))
    r3, r4 = residual(3), residual(4)

    def split(both):
        below, above = both
        return jnp.where(even, below, to_odd(above)), jnp.where(even, to_even(below), above)

    receive(edge_up, edge_low)
    edge_raw, edge_in = split((edge[0, 0], edge[1, 0]))
    edge_x, edge_y = split((edge[0, 1], edge[1, 1]))
    edge_side = side_sum(edge_x, edge_y)
    edge_diag = edge_raw + outer
    edge_active = edge_raw > 0.0
    edge_weight = jnp.where(edge_active, OMEGA / jnp.where(edge_active, edge_diag, 1.0), 0.0)
    own_1 = weight * (diag1 - side)
    edge_own_1, edge_out_1, edge_in_1 = edge_weight * (edge_diag - edge_side), edge_weight * z_out, edge_weight * edge_in
    to_out2 = out_part * edge_in_1
    to_out1 = (2.0 - OMEGA) * out_part + weight * beside(out_part, coarse_x, coarse_y) - out_part * edge_own_1
    to_own = 1.0 + (OMEGA - 2.0) * own_1 - weight * beside(own_1, coarse_x, coarse_y) + out_part * edge_out_1 + in_part * swap(in_part)
    to_in1 = (2.0 - OMEGA) * in_part + weight * beside(in_part, coarse_x, coarse_y) - in_part * swap(own_1)
    to_in2 = in_part * swap(out_part)
    edge_own_part = jnp.where(edge_active, 1.0 - OMEGA, 0.0) + edge_weight * edge_side

    for r in range(3, len(rounds)):
        round_end(r)
        round_start(r + 1)
    gather(line_out, line_all, 0, line_sums)

    receive(u1_up, u1_low)
    over(0, 2, lambda k: second_sweep(1 + 5 * k))
    b1 = restrict(residual(2) + r3, r4 + residual(5))

    row_even = even[:1]

    def row_swap(row):
        return jnp.where(row_even, to_even(row), to_odd(row))

    v1 = weight * b1
    begin[0] = jnp.where(even, to_even(b1), to_odd(v1))
    begin[1] = jnp.where(even, b1, v1)
    send(ends_up, ends_low)
    gather(
        row_out, row_all, 1,
        (
            row_sum(to_own * b1) + row_swap(row_sum(to_in1 * b1)),
            row_swap(row_sum(to_out1 * b1)) + row_sum(to_in2 * b1),
            row_sum(to_out2 * b1),
        ),
    )

    def own_sweep(own, beyond):
        total = beside(own, coarse_x, coarse_y) + z_out * beyond + z_in * swap(own)
        return (1.0 - OMEGA) * own + weight * (b1 + total)

    def edge_sweep(own, beyond, further):
        total = beside(beyond, edge_x, edge_y) + z_out * own + edge_in * further
        return (1.0 - OMEGA) * beyond + edge_weight * (edge_b1 + total)

    receive(ends_up, ends_low)
    edge_b1, far_v1 = split((ends[0], ends[1]))
    edge_v1 = edge_weight * edge_b1
    v2, edge_v2 = own_sweep(v1, edge_v1), edge_sweep(v1, edge_v1, far_v1)
    v3 = own_sweep(v2, edge_v2)
    vn[1] = v3
    send(vn_up, vn_low)
    send(u2_up, u2_low)

    receive(far_up, far_low)
    far_own_part, far_out_part = split((far[0, pl.ds(0, hx_rows)], far[1, pl.ds(0, hx_rows)]))
    below, above = far[0, pl.ds(hx_rows, hx_rows // 2)], far[1, pl.ds(hx_rows, hx_rows // 2)]
    spread[pl.ds(0, hx_rows // 2, 2), :] = jnp.where(even_half, below, to_odd(above))
    spread[pl.ds(1, hx_rows // 2, 2), :] = jnp.where(even_half, to_even(below), above)

    gather_wait(line_all, 1, 0, 2)

    line_even = lax.broadcasted_iota(jnp.int32, (n, ny), 1) % 2 == 0

    def line_row(everyone, row):
        return everyone.reshape(n * 8, ny)[pl.ds(row, n, 8), :]

    def apart(both):
        lower = jnp.where(line_even, both, pltpu.roll(both, 1, 1))
        return lower, jnp.where(line_even, pltpu.roll(both, ny - 1, 1), both)

    (de, do), (fe, fo) = apart(line_row(line_all, 0)), apart(line_row(line_all, 1))

    def back(x, s):
        return pltpu.roll(x, s % n, 0)

    def ahead(x, s):
        return pltpu.roll(x, (n - s) % n, 0)

    inv_odd = 1.0 / do
    to_low = fe * back(inv_odd, 1)
    to_up = fo * inv_odd
    fe_next = ahead(fe, 1)
    diag = de - fe * to_low - fo * to_up
    lower = -to_low * back(fo, 1)
    upper = -to_up * fe_next
    steps = []
    shift = 1
    while shift < n:
        alpha, gamma = lower / back(diag, shift), upper / ahead(diag, shift)
        steps.append((shift, alpha, gamma))
        diag = diag - alpha * back(upper, shift) - gamma * ahead(lower, shift)
        lower, upper = -alpha * back(lower, shift), -gamma * ahead(upper, shift)
        shift *= 2
    inv_diag = 1.0 / diag

    gather_wait(row_all, 1, 1, 3)
    one, two = line_row(row_all, 1), line_row(row_all, 2)
    sums = line_row(row_all, 0) + jnp.where(line_even, back(one, 1) + ahead(two, 1), ahead(one, 1) + back(two, 1))
    be, bo = apart(sums)
    reduced = be + to_low * back(bo, 1) + to_up * bo
    for shift, alpha, gamma in steps:
        reduced = reduced - alpha * back(reduced, shift) - gamma * ahead(reduced, shift)
    e_even = reduced * inv_diag
    e_odd = (bo + fo * e_even + fe_next * ahead(e_even, 1)) * inv_odd
    xs[0, pl.ds(8, n), :] = jnp.where(line_even, e_even, e_odd)
    xs[1, pl.ds(8, n), :] = jnp.where(line_even, e_odd, e_even)

    def line(side, distance):
        return jnp.broadcast_to(xs[side, pl.ds(me + 8 + distance, 1), :], (hx_rows, ny))

    def outward(side, distance):
        return jnp.where(even, line(side, -distance), line(side, distance))

    e_own, e_in = line(0, 0), line(1, 0)
    e_out, e_out2, e_out3 = outward(1, 1), outward(0, 1), outward(1, 2)
    receive(vn_up, vn_low)
    below, above = vn[0], vn[2]
    w2 = v3 + own_part * e_own + out_part * e_out + in_part * e_in
    edge_w2 = jnp.where(even, to_even(below), to_odd(above))
    edge_w2 = edge_w2 + edge_own_part * e_out + edge_out_1 * e_own + edge_in_1 * e_out2
    far_w2 = jnp.where(even, below, above) + far_own_part * e_out2 + spread[...] * e_out + far_out_part * e_out3
    w3, edge_w3 = own_sweep(w2, edge_w2), edge_sweep(w2, edge_w2, far_w2)

    def prolong(slot, plane):
        pro[slot, pl.ds(0, hx_rows, 2), :] = plane
        pro[slot, pl.ds(1, hx_rows, 2), :] = plane

    def lower_plane(pack):
        return jnp.where(even, pack, pltpu.roll(pack, 1, 1))

    def upper_plane(pack):
        return jnp.where(even, pltpu.roll(pack, ny - 1, 1), pack)

    prolong(0, lower_plane(edge_w3))
    prolong(1, lower_plane(w3))
    prolong(2, upper_plane(w3))
    prolong(3, upper_plane(edge_w3))

    receive(u2_up, u2_low)

    def correct(k):
        ua[k] = ub[k] + jnp.where(lab[k] > 0, pro[k // 2], 0.0)

    pl.when(has_up)(u1_up.wait_send)
    pl.when(has_low)(u1_low.wait_send)
    over(0, 8, correct)

    over(1, 7, sweep(ua, tmp))
    over(2, 6, sweep(tmp, out.at[0], 2))

    for upward, downward in (
        (near_up, near_low), (next_up, next_low), (rhs_up, rhs_low), (far_up, far_low), (ends_up, ends_low), (vn_up, vn_low),
        (u2_up, u2_low), (edge_up, edge_low),
    ):
        pl.when(has_up)(upward.wait_send)
        pl.when(has_low)(downward.wait_send)
    gather_wait(line_all, 0, 0, 2)
    gather_wait(row_all, 0, 1, 3)


def on_device(n, rhs, labels, sigma_table):
    planes, nx, ny = labels.shape
    fine = lambda count: pltpu.VMEM((count, nx, ny), jnp.float32)
    packs = lambda *counts: pltpu.VMEM((*counts, nx // 2, ny), jnp.float32)
    thirds = lambda *counts: pltpu.VMEM((*counts, nx // 2 + nx // 4, ny), jnp.float32)
    tiles = lambda *counts: pltpu.VMEM((*counts, 8, ny), jnp.float32)
    return pl.pallas_call(
        functools.partial(kernel, n),
        out_shape=pltpu.VMEM(rhs.shape, jnp.float32),
        in_specs=[
            pl.BlockSpec(memory_space=pl.ANY),
            pl.BlockSpec(memory_space=pl.ANY),
            pl.BlockSpec(memory_space=pl.ANY),
        ],
        out_specs=pl.BlockSpec(memory_space=pltpu.VMEM),
        scratch_shapes=[
            pltpu.VMEM((8, nx, ny), jnp.int32),
            fine(8), fine(8), fine(8), fine(8), fine(8), fine(8), fine(8), fine(8),
            fine(8), fine(4),
            packs(2, 2), packs(2, 2), thirds(2), thirds(2), packs(2), packs(2), packs(3), packs(),
            tiles(), tiles(n), tiles(), tiles(n),
            pltpu.VMEM((2, n + 16, ny), jnp.float32),
            pltpu.SMEM((3, LABELS), jnp.float32),
            pltpu.SemaphoreType.DMA((3,)),
            pltpu.SemaphoreType.DMA((2, 18)),
            pltpu.SemaphoreType.DMA((2, 2)),
            pltpu.SemaphoreType.REGULAR((n.bit_length(),)),
        ],
        compiler_params=pltpu.CompilerParams(collective_id=0, has_side_effects=True),
    )(rhs, labels, sigma_table.T)


def solution(mesh):
    placed = (P("groups", "slab", None, None), P("slab", "groups", None), P())
    return jax.shard_map(
        functools.partial(on_device, mesh.shape["slab"]),
        mesh=mesh,
        in_specs=placed,
        out_specs=P("groups", "slab", None, None),
        check_vma=False,
    )
```

```python
import functools
import itertools

import jax
import jax.numpy as jnp
import numpy as np
from jax import lax
from jax.experimental import pallas as pl
from jax.experimental.pallas import tpu as pltpu
from jax.sharding import PartitionSpec as P

OMEGA = 0.8
LABELS = 5
MESH = pl.DeviceIdType.MESH
REACH = 4


def copy_to(src, dst, sems, slot, target):
    return pltpu.make_async_remote_copy(
        src_ref=src,
        dst_ref=dst,
        send_sem=sems.at[0, slot],
        recv_sem=sems.at[1, slot],
        device_id={"slab": target},
        device_id_type=MESH,
    )


def near_axis(row, lane, nx, ny):
    across, along = 2 * row + 1 - nx, 2 * lane + 1 - ny
    return (across * across + along * along) * 1000 <= 813 * nx * nx


def folds(nx, ny):
    tiles = nx // 8
    pairs = ((2, tiles - 2), (4, 0), (tiles - 5, tiles - 1), (tiles - 3, 1))
    if nx != ny or nx < 128 or nx % 8:
        return ()
    inside = near_axis(np.arange(nx)[:, None], np.arange(ny)[None], nx, ny).reshape(tiles, 8, ny)
    if any((inside[kept] & np.roll(inside[folded], ny // 2, 1)).any() for kept, folded in pairs):
        return ()
    return pairs


def kernel(
    n, pairs, rhs_hbm, lab_hbm, table_hbm, out,
    lab, rhs, gx, gy, gz, idf, dg, ua, ub, tmp, pro,
    lab_out, fine_out, part, edge, far_out, far, ends, begin, vn, spread, line_out, line_all, row_out, row_all, xs, table,
    load_sem, sems, gather_sem, tokens,
):
    me = lax.axis_index("slab")
    nx, ny = lab.shape[1:]
    hx_rows = nx // 2
    has_low, has_up = me > 0, me < n - 1

    load_table = pltpu.make_async_copy(table_hbm, table, load_sem.at[2])
    load_table.start()
    own_lab = pltpu.make_async_copy(lab_hbm, lab.at[pl.ds(2, 4)], load_sem.at[0])
    own_rhs = pltpu.make_async_copy(rhs_hbm.at[0], rhs.at[pl.ds(2, 4)], load_sem.at[1])
    own_lab.start()
    own_rhs.start()
    barrier = pltpu.get_barrier_semaphore()

    up, low = lax.rem(me + 1, n), lax.rem(me + n - 1, n)

    def signal(sem, distance):
        for near, other in ((me >= distance, me - distance), (me + distance < n, me + distance)):

            @pl.when(near)
            def _():
                pl.semaphore_signal(sem, inc=1, device_id={"slab": other}, device_id_type=MESH)

    for distance in range(1, min(REACH, n - 1) + 1):
        signal(barrier, distance)
    pl.semaphore_wait(barrier, jnp.minimum(me, REACH) + jnp.minimum(n - 1 - me, REACH))

    rounds = []
    while REACH * 2 ** len(rounds) < n - 1:
        rounds.append(REACH * 2 ** len(rounds))

    def round_start(r):
        if r < len(rounds):
            signal(tokens.at[r], rounds[r])

    def round_end(r):
        if r < len(rounds):
            distance = rounds[r]
            both = jnp.logical_and(me >= distance, me + distance < n)
            one = jnp.logical_xor(me >= distance, me + distance < n)
            pl.when(both)(lambda: pl.semaphore_wait(tokens.at[r], 2))
            pl.when(one)(lambda: pl.semaphore_wait(tokens.at[r], 1))

    sent = pl.ds(16, nx - 32) if pairs else pl.ds(0, nx)
    near_up = copy_to(lab_out.at[0, 0], lab.at[1, sent], sems, 0, up)
    near_low = copy_to(lab_out.at[1, 0], lab.at[6, sent], sems, 1, low)
    next_up = copy_to(lab_out.at[0, 1], lab.at[0, sent], sems, 2, up)
    next_low = copy_to(lab_out.at[1, 1], lab.at[7, sent], sems, 3, low)
    rhs_up = copy_to(fine_out.at[0, 0], rhs.at[1, sent], sems, 4, up)
    rhs_low = copy_to(fine_out.at[1, 0], rhs.at[6, sent], sems, 5, low)
    u1_up = copy_to(fine_out.at[0, 1], ua.at[0, sent], sems, 6, up)
    u1_low = copy_to(fine_out.at[1, 1], ua.at[7, sent], sems, 7, low)
    far_up = copy_to(far_out.at[0], far.at[0], sems, 8, up)
    far_low = copy_to(far_out.at[1], far.at[1], sems, 9, low)
    ends_up = copy_to(begin.at[0], ends.at[0], sems, 10, up)
    ends_low = copy_to(begin.at[1], ends.at[1], sems, 11, low)
    u2_up = copy_to(fine_out.at[0, 2], ub.at[0, sent], sems, 12, up)
    u2_low = copy_to(fine_out.at[1, 2], ub.at[7, sent], sems, 13, low)
    vn_up = copy_to(vn.at[1], vn.at[0], sems, 14, up)
    vn_low = copy_to(vn.at[1], vn.at[2], sems, 15, low)
    edge_up = copy_to(part.at[0], edge.at[0], sems, 16, up)
    edge_low = copy_to(part.at[1], edge.at[1], sems, 17, low)

    def send(upward, downward):
        pl.when(has_up)(upward.start)
        pl.when(has_low)(downward.start)

    def receive(upward, downward):
        pl.when(has_low)(upward.wait_recv)
        pl.when(has_up)(downward.wait_recv)

    tile_row = lax.broadcasted_iota(jnp.int32, (8, ny), 0)
    tile_lane = lax.broadcasted_iota(jnp.int32, (8, ny), 1)

    def tile(t):
        return pl.ds(8 * t, 8)

    def inside(t):
        return near_axis(tile_row + 8 * t, tile_lane, nx, ny)

    def half_turn(values):
        return pltpu.roll(values, ny // 2, 1)

    def fold(field, k, out_ref):
        out_ref[...] = field[k, sent]
        for kept, folded in pairs:
            out_ref[tile(kept - 2)] = jnp.where(inside(kept), field[k, tile(kept)], half_turn(field[k, tile(folded)]))

    def unfold(field, k):
        for kept, folded in pairs:
            both = field[k, tile(kept)]
            zero_tile = jnp.zeros_like(both)
            field[k, tile(folded)] = jnp.where(inside(folded), half_turn(both), zero_tile)
            field[k, tile(kept)] = jnp.where(inside(kept), both, zero_tile)

    round_start(0)
    own_lab.wait()
    fold(lab, 5, lab_out.at[0, 0])
    fold(lab, 2, lab_out.at[1, 0])
    send(near_up, near_low)
    fold(lab, 4, lab_out.at[0, 1])
    fold(lab, 3, lab_out.at[1, 1])
    send(next_up, next_low)
    own_rhs.wait()
    fold(rhs, 5, fine_out.at[0, 0])
    fold(rhs, 2, fine_out.at[1, 0])
    send(rhs_up, rhs_low)

    def clear(ref, first, count):
        for k in range(first, first + count):
            ref[k] = jnp.zeros(ref.shape[1:], ref.dtype)

    @pl.when(me == 0)
    def _():
        clear(lab, 0, 2)
        clear(rhs, 1, 1)
        clear(ua, 0, 1)
        clear(edge.at[0], 0, 2)
        clear(far, 0, 1)
        clear(ends, 0, 1)
        clear(ub, 0, 1)
        clear(vn, 0, 1)

    @pl.when(me == n - 1)
    def _():
        clear(lab, 6, 2)
        clear(rhs, 6, 1)
        clear(ua, 7, 1)
        clear(edge.at[1], 0, 2)
        clear(far, 1, 1)
        clear(ends, 1, 1)
        clear(ub, 7, 1)
        clear(vn, 2, 1)

    xs[...] = jnp.zeros(xs.shape, xs.dtype)

    fine_row = lax.broadcasted_iota(jnp.int32, (nx, ny), 0) % 2 == 1
    fine_lane = lax.broadcasted_iota(jnp.int32, (nx, ny), 1) % 2 == 1
    even = lax.broadcasted_iota(jnp.int32, (hx_rows, ny), 1) % 2 == 0

    def select(values, column):
        chosen = jnp.full(values.shape, table[column, 0], jnp.float32)
        for tissue in range(1, LABELS):
            chosen = jnp.where(values == tissue, table[column, tissue], chosen)
        return chosen

    def harmonic(a, b):
        return 2.0 * a * b / (a + b)

    def active(k):
        return (lab[k] > 0).astype(jnp.float32)

    def side_faces(k):
        here = lab[k]
        a = (here > 0).astype(jnp.float32)
        sx, sy = select(here, 0), select(here, 1)
        hx = harmonic(pltpu.roll(sx, 1, 0), sx)
        gx[k] = hx * a * pltpu.roll(a, 1, 0)
        hy = harmonic(pltpu.roll(sy, 1, 1), sy)
        gy[k] = hy * a * pltpu.roll(a, 1, 1)
        return hx + pltpu.roll(hx, nx - 1, 0) + hy + pltpu.roll(hy, ny - 1, 1)

    def face_below(k):
        h = harmonic(select(lab[k - 1], 2), select(lab[k], 2))
        gz[k] = h * active(k - 1) * active(k)
        return h

    def finish(k, faces):
        a = active(k)
        diagonal = a * faces + (1.0 - a)
        dg[k] = diagonal
        idf[k] = OMEGA * a / diagonal

    def over(first, last, body):
        for k in range(first, last):
            body(k)

    def first_sweep(k):
        ua[k] = idf[k] * rhs[k]

    def neighbours(field, k):
        u = field[k]
        cx, cy = gx[k], gy[k]
        total = cx * pltpu.roll(u, 1, 0) + pltpu.roll(cx * u, nx - 1, 0)
        total = total + cy * pltpu.roll(u, 1, 1) + pltpu.roll(cy * u, ny - 1, 1)
        return u, total + gz[k] * field[k - 1] + gz[k + 1] * field[k + 1]

    def sweep(src, dst, shift=0):
        def body(k):
            u, total = neighbours(src, k)
            dst[k - shift] = (1.0 - OMEGA) * u + idf[k] * (rhs[k] + total)

        return body

    def residual(k):
        u, total = neighbours(ub, k)
        return jnp.where(idf[k] > 0.0, rhs[k] - dg[k] * u + total, 0.0)

    second_sweep = sweep(ua, ub)

    load_table.wait()
    h3, h4, h5 = face_below(3), face_below(4), face_below(5)
    finish(3, side_faces(3) + h3 + h4)
    finish(4, side_faces(4) + h4 + h5)
    dg[2] = side_faces(2) + h3
    dg[5] = side_faces(5) + h5
    over(3, 5, first_sweep)
    fold(ua, 4, fine_out.at[0, 1])
    fold(ua, 3, fine_out.at[1, 1])

    turn = itertools.count()

    def rows_apart(plane):
        slot = next(turn) % 6
        tmp[slot] = plane
        return tmp[slot, pl.ds(0, hx_rows, 2), :], tmp[slot, pl.ds(1, hx_rows, 2), :]

    def rows_even(plane):
        return rows_apart(plane)[0]

    def rows_sum(plane):
        first, second = rows_apart(plane)
        return first + second

    def lanes_sum(t0, t1):
        return jnp.where(even, t0 + pltpu.roll(t0, ny - 1, 1), t1 + pltpu.roll(t1, 1, 1))

    def lanes_even(t0, t1):
        return jnp.where(even, t0, pltpu.roll(t1, 1, 1))

    def restrict(p0, p1):
        return lanes_sum(rows_sum(p0), rows_sum(p1))

    def inner(k):
        doubled = jnp.where(fine_row, gx[k], 0.0) + jnp.where(fine_lane, gy[k], 0.0)
        if k % 2 == 1:
            doubled = doubled + gz[k]
        return active(k) * dg[k] - 2.0 * doubled

    def to_even(pack):
        return pltpu.roll(pack, ny - 1, 1)

    def to_odd(pack):
        return pltpu.roll(pack, 1, 1)

    def swap(pack):
        return jnp.where(even, to_even(pack), to_odd(pack))

    def of_odd(a, b):
        return jnp.where(even, to_even(a), b)

    def of_even(a, b):
        return jnp.where(even, a, to_odd(b))

    def beside(field, cx, cy):
        total = cx * pltpu.roll(field, 1, 0) + pltpu.roll(cx * field, hx_rows - 1, 0)
        return total + cy * pltpu.roll(field, 2, 1) + pltpu.roll(cy * field, ny - 2, 1)

    def side_sum(cx, cy):
        return cx + pltpu.roll(cx, hx_rows - 1, 0) + cy + pltpu.roll(cy, ny - 2, 1)

    raw_part = restrict(inner(2) + inner(3), inner(4) + inner(5))
    coarse_x = lanes_sum(rows_even(gx[2] + gx[3]), rows_even(gx[4] + gx[5]))
    coarse_y = lanes_even(rows_sum(gy[2] + gy[3]), rows_sum(gy[4] + gy[5]))
    middle = rows_sum(gz[4])
    z_in = lanes_sum(middle, middle)
    part[0, 0] = of_odd(raw_part, z_in)
    part[0, 1] = of_odd(coarse_x, coarse_y)
    part[1, 0] = of_even(raw_part, z_in)
    part[1, 1] = of_even(coarse_x, coarse_y)
    send(edge_up, edge_low)
    send(u1_up, u1_low)
    side = side_sum(coarse_x, coarse_y)

    round_end(0)
    round_start(1)
    receive(near_up, near_low)
    unfold(lab, 1)
    unfold(lab, 6)
    h2, h6 = face_below(2), face_below(6)
    tmp[6] = h2
    tmp[7] = h6
    finish(2, dg[2] + h2)
    finish(5, dg[5] + h6)
    over(0, 2, lambda k: first_sweep(2 + 3 * k))
    over(3, 5, second_sweep)
    fold(ub, 4, fine_out.at[0, 2])
    fold(ub, 3, fine_out.at[1, 2])
    raw = raw_part + restrict(active(2) * h2, active(5) * h6)
    active1 = jnp.where(raw_part > 0.0, 1.0, 0.0)
    diag1 = raw + (1.0 - active1)
    weight = OMEGA * active1 / diag1
    z_out = restrict(gz[2], gz[6])
    outer = restrict(active(1) * h2, active(6) * h6)
    own_part, out_part, in_part = (1.0 - OMEGA) * active1 + weight * side, weight * z_out, weight * z_in
    spread[...] = in_part
    in_first, in_second = spread[pl.ds(0, hx_rows // 2, 2), :], spread[pl.ds(1, hx_rows // 2, 2), :]
    even_half = even[: hx_rows // 2]
    far_out[0, pl.ds(0, hx_rows)] = of_even(own_part, out_part)
    far_out[0, pl.ds(hx_rows, hx_rows // 2)] = jnp.where(even_half, in_first, to_odd(in_second))
    far_out[1, pl.ds(0, hx_rows)] = of_odd(own_part, out_part)
    far_out[1, pl.ds(hx_rows, hx_rows // 2)] = jnp.where(even_half, to_even(in_first), in_second)
    send(far_up, far_low)

    sub = lax.broadcasted_iota(jnp.int32, (8, ny), 0)
    sub_even = lax.broadcasted_iota(jnp.int32, (8, ny), 1) % 2 == 0

    def row_sum(pack):
        return jnp.sum(pack, axis=0, keepdims=True)

    def gather(out, everyone, slot, rows_of):
        tile = jnp.zeros((8, ny), jnp.float32)
        for row, values in enumerate(rows_of):
            tile = jnp.where(sub == row, values, tile)
        lower = jnp.sum(jnp.where(sub_even, tile, 0.0), axis=1, keepdims=True)
        upper = jnp.sum(jnp.where(sub_even, 0.0, tile), axis=1, keepdims=True)
        tile = jnp.where(sub_even, lower, upper)
        out[...] = tile
        everyone[me] = tile
        rows = pl.ds(0, len(rows_of))

        def one(step, carry):
            pltpu.make_async_remote_copy(
                src_ref=out.at[rows],
                dst_ref=everyone.at[me, rows],
                send_sem=gather_sem.at[0, slot],
                recv_sem=gather_sem.at[1, slot],
                device_id={"slab": lax.rem(me + step, n)},
                device_id_type=MESH,
            ).start()
            return carry

        lax.fori_loop(1, n, one, 0)

    def gather_wait(everyone, side, slot, count):
        rest = everyone.at[pl.ds(0, n - 1), pl.ds(0, count)]
        pltpu.make_async_copy(rest, rest, gather_sem.at[side, slot]).wait()

    line_sums = (row_sum(raw - 2.0 * (coarse_x + coarse_y)), row_sum(jnp.where(even, z_out, z_in)))
    round_end(1)
    round_start(2)

    receive(next_up, next_low)
    unfold(lab, 0)
    unfold(lab, 7)
    finish(1, side_faces(1) + face_below(1) + tmp[6])
    finish(6, side_faces(6) + face_below(7) + tmp[7])
    receive(rhs_up, rhs_low)
    unfold(rhs, 1)
    unfold(rhs, 6)
    round_end(2)
    round_start(3)
    over(0, 2, lambda k: first_sweep(1 + 5 * k))
    over(0, 2, lambda k: second_sweep(2 + 3 * k))
    r3, r4 = residual(3), residual(4)

    def split(both):
        below, above = both
        return jnp.where(even, below, to_odd(above)), jnp.where(even, to_even(below), above)

    receive(edge_up, edge_low)
    edge_raw, edge_in = split((edge[0, 0], edge[1, 0]))
    edge_x, edge_y = split((edge[0, 1], edge[1, 1]))
    edge_side = side_sum(edge_x, edge_y)
    edge_diag = edge_raw + outer
    edge_active = edge_raw > 0.0
    edge_weight = jnp.where(edge_active, OMEGA / jnp.where(edge_active, edge_diag, 1.0), 0.0)
    own_1 = weight * (diag1 - side)
    edge_own_1, edge_out_1, edge_in_1 = edge_weight * (edge_diag - edge_side), edge_weight * z_out, edge_weight * edge_in
    to_out2 = out_part * edge_in_1
    to_out1 = (2.0 - OMEGA) * out_part + weight * beside(out_part, coarse_x, coarse_y) - out_part * edge_own_1
    to_own = 1.0 + (OMEGA - 2.0) * own_1 - weight * beside(own_1, coarse_x, coarse_y) + out_part * edge_out_1 + in_part * swap(in_part)
    to_in1 = (2.0 - OMEGA) * in_part + weight * beside(in_part, coarse_x, coarse_y) - in_part * swap(own_1)
    to_in2 = in_part * swap(out_part)
    edge_own_part = jnp.where(edge_active, 1.0 - OMEGA, 0.0) + edge_weight * edge_side

    for r in range(3, len(rounds)):
        round_end(r)
        round_start(r + 1)
    gather(line_out, line_all, 0, line_sums)

    receive(u1_up, u1_low)
    unfold(ua, 0)
    unfold(ua, 7)
    over(0, 2, lambda k: second_sweep(1 + 5 * k))
    b1 = restrict(residual(2) + r3, r4 + residual(5))

    row_even = even[:1]

    def row_swap(row):
        return jnp.where(row_even, to_even(row), to_odd(row))

    v1 = weight * b1
    begin[0] = jnp.where(even, to_even(b1), to_odd(v1))
    begin[1] = jnp.where(even, b1, v1)
    send(ends_up, ends_low)
    gather(
        row_out, row_all, 1,
        (
            row_sum(to_own * b1) + row_swap(row_sum(to_in1 * b1)),
            row_swap(row_sum(to_out1 * b1)) + row_sum(to_in2 * b1),
            row_sum(to_out2 * b1),
        ),
    )

    def own_sweep(own, beyond):
        total = beside(own, coarse_x, coarse_y) + z_out * beyond + z_in * swap(own)
        return (1.0 - OMEGA) * own + weight * (b1 + total)

    def edge_sweep(own, beyond, further):
        total = beside(beyond, edge_x, edge_y) + z_out * own + edge_in * further
        return (1.0 - OMEGA) * beyond + edge_weight * (edge_b1 + total)

    receive(ends_up, ends_low)
    edge_b1, far_v1 = split((ends[0], ends[1]))
    edge_v1 = edge_weight * edge_b1
    v2, edge_v2 = own_sweep(v1, edge_v1), edge_sweep(v1, edge_v1, far_v1)
    v3 = own_sweep(v2, edge_v2)
    vn[1] = v3
    send(vn_up, vn_low)
    send(u2_up, u2_low)

    receive(far_up, far_low)
    far_own_part, far_out_part = split((far[0, pl.ds(0, hx_rows)], far[1, pl.ds(0, hx_rows)]))
    below, above = far[0, pl.ds(hx_rows, hx_rows // 2)], far[1, pl.ds(hx_rows, hx_rows // 2)]
    spread[pl.ds(0, hx_rows // 2, 2), :] = jnp.where(even_half, below, to_odd(above))
    spread[pl.ds(1, hx_rows // 2, 2), :] = jnp.where(even_half, to_even(below), above)

    gather_wait(line_all, 1, 0, 2)

    line_even = lax.broadcasted_iota(jnp.int32, (n, ny), 1) % 2 == 0

    def line_row(everyone, row):
        return everyone.reshape(n * 8, ny)[pl.ds(row, n, 8), :]

    def apart(both):
        lower = jnp.where(line_even, both, pltpu.roll(both, 1, 1))
        return lower, jnp.where(line_even, pltpu.roll(both, ny - 1, 1), both)

    (de, do), (fe, fo) = apart(line_row(line_all, 0)), apart(line_row(line_all, 1))

    def back(x, s):
        return pltpu.roll(x, s % n, 0)

    def ahead(x, s):
        return pltpu.roll(x, (n - s) % n, 0)

    inv_odd = 1.0 / do
    to_low = fe * back(inv_odd, 1)
    to_up = fo * inv_odd
    fe_next = ahead(fe, 1)
    diag = de - fe * to_low - fo * to_up
    lower = -to_low * back(fo, 1)
    upper = -to_up * fe_next
    steps = []
    shift = 1
    while shift < n:
        alpha, gamma = lower / back(diag, shift), upper / ahead(diag, shift)
        steps.append((shift, alpha, gamma))
        diag = diag - alpha * back(upper, shift) - gamma * ahead(lower, shift)
        lower, upper = -alpha * back(lower, shift), -gamma * ahead(upper, shift)
        shift *= 2
    inv_diag = 1.0 / diag

    gather_wait(row_all, 1, 1, 3)
    one, two = line_row(row_all, 1), line_row(row_all, 2)
    sums = line_row(row_all, 0) + jnp.where(line_even, back(one, 1) + ahead(two, 1), ahead(one, 1) + back(two, 1))
    be, bo = apart(sums)
    reduced = be + to_low * back(bo, 1) + to_up * bo
    for shift, alpha, gamma in steps:
        reduced = reduced - alpha * back(reduced, shift) - gamma * ahead(reduced, shift)
    e_even = reduced * inv_diag
    e_odd = (bo + fo * e_even + fe_next * ahead(e_even, 1)) * inv_odd
    xs[0, pl.ds(8, n), :] = jnp.where(line_even, e_even, e_odd)
    xs[1, pl.ds(8, n), :] = jnp.where(line_even, e_odd, e_even)

    def line(side, distance):
        return jnp.broadcast_to(xs[side, pl.ds(me + 8 + distance, 1), :], (hx_rows, ny))

    def outward(side, distance):
        return jnp.where(even, line(side, -distance), line(side, distance))

    e_own, e_in = line(0, 0), line(1, 0)
    e_out, e_out2, e_out3 = outward(1, 1), outward(0, 1), outward(1, 2)
    receive(vn_up, vn_low)
    below, above = vn[0], vn[2]
    w2 = v3 + own_part * e_own + out_part * e_out + in_part * e_in
    edge_w2 = jnp.where(even, to_even(below), to_odd(above))
    edge_w2 = edge_w2 + edge_own_part * e_out + edge_out_1 * e_own + edge_in_1 * e_out2
    far_w2 = jnp.where(even, below, above) + far_own_part * e_out2 + spread[...] * e_out + far_out_part * e_out3
    w3, edge_w3 = own_sweep(w2, edge_w2), edge_sweep(w2, edge_w2, far_w2)

    def prolong(slot, plane):
        pro[slot, pl.ds(0, hx_rows, 2), :] = plane
        pro[slot, pl.ds(1, hx_rows, 2), :] = plane

    def lower_plane(pack):
        return jnp.where(even, pack, pltpu.roll(pack, 1, 1))

    def upper_plane(pack):
        return jnp.where(even, pltpu.roll(pack, ny - 1, 1), pack)

    prolong(0, lower_plane(edge_w3))
    prolong(1, lower_plane(w3))
    prolong(2, upper_plane(w3))
    prolong(3, upper_plane(edge_w3))

    receive(u2_up, u2_low)
    unfold(ub, 0)
    unfold(ub, 7)

    def correct(k):
        ua[k] = ub[k] + jnp.where(lab[k] > 0, pro[k // 2], 0.0)

    over(0, 8, correct)

    over(1, 7, sweep(ua, tmp))
    over(2, 6, sweep(tmp, out.at[0], 2))

    for upward, downward in (
        (near_up, near_low), (next_up, next_low), (rhs_up, rhs_low), (far_up, far_low), (ends_up, ends_low), (vn_up, vn_low),
        (u2_up, u2_low), (edge_up, edge_low), (u1_up, u1_low),
    ):
        pl.when(has_up)(upward.wait_send)
        pl.when(has_low)(downward.wait_send)
    gather_wait(line_all, 0, 0, 2)
    gather_wait(row_all, 0, 1, 3)


def on_device(n, rhs, labels, sigma_table):
    planes, nx, ny = labels.shape
    pairs = folds(nx, ny)
    kept = nx - 32 if pairs else nx
    fine = lambda count: pltpu.VMEM((count, nx, ny), jnp.float32)
    packs = lambda *counts: pltpu.VMEM((*counts, nx // 2, ny), jnp.float32)
    thirds = lambda *counts: pltpu.VMEM((*counts, nx // 2 + nx // 4, ny), jnp.float32)
    tiles = lambda *counts: pltpu.VMEM((*counts, 8, ny), jnp.float32)
    return pl.pallas_call(
        functools.partial(kernel, n, pairs),
        out_shape=pltpu.VMEM(rhs.shape, jnp.float32),
        in_specs=[
            pl.BlockSpec(memory_space=pl.ANY),
            pl.BlockSpec(memory_space=pl.ANY),
            pl.BlockSpec(memory_space=pl.ANY),
        ],
        out_specs=pl.BlockSpec(memory_space=pltpu.VMEM),
        scratch_shapes=[
            pltpu.VMEM((8, nx, ny), jnp.int32),
            fine(8), fine(8), fine(8), fine(8), fine(8), fine(8), fine(8), fine(8),
            fine(8), fine(4),
            pltpu.VMEM((2, 2, kept, ny), jnp.int32), pltpu.VMEM((2, 3, kept, ny), jnp.float32),
            packs(2, 2), packs(2, 2), thirds(2), thirds(2), packs(2), packs(2), packs(3), packs(),
            tiles(), tiles(n), tiles(), tiles(n),
            pltpu.VMEM((2, n + 16, ny), jnp.float32),
            pltpu.SMEM((3, LABELS), jnp.float32),
            pltpu.SemaphoreType.DMA((3,)),
            pltpu.SemaphoreType.DMA((2, 18)),
            pltpu.SemaphoreType.DMA((2, 2)),
            pltpu.SemaphoreType.REGULAR((n.bit_length(),)),
        ],
        compiler_params=pltpu.CompilerParams(collective_id=0, has_side_effects=True),
    )(rhs, labels, sigma_table.T)


def solution(mesh):
    placed = (P("groups", "slab", None, None), P("slab", "groups", None), P())
    return jax.shard_map(
        functools.partial(on_device, mesh.shape["slab"]),
        mesh=mesh,
        in_specs=placed,
        out_specs=P("groups", "slab", None, None),
        check_vma=False,
    )
```

```python
import functools
import itertools

import jax
import jax.numpy as jnp
import numpy as np
from jax import lax
from jax.experimental import pallas as pl
from jax.experimental.pallas import tpu as pltpu
from jax.sharding import PartitionSpec as P

OMEGA = 0.8
LABELS = 5
MESH = pl.DeviceIdType.MESH
REACH = 4


def copy_to(src, dst, sems, slot, target):
    return pltpu.make_async_remote_copy(
        src_ref=src,
        dst_ref=dst,
        send_sem=sems.at[0, slot],
        recv_sem=sems.at[1, slot],
        device_id={"slab": target},
        device_id_type=MESH,
    )


def near_axis(row, lane, nx, ny):
    across, along = 2 * row + 1 - nx, 2 * lane + 1 - ny
    return (across * across + along * along) * 1000 <= 813 * nx * nx


def folds(nx, ny):
    tiles = nx // 8
    pairs = ((2, tiles - 2), (4, 0), (tiles - 5, tiles - 1), (tiles - 3, 1))
    if nx != ny or nx < 128 or nx % 8:
        return ()
    inside = near_axis(np.arange(nx)[:, None], np.arange(ny)[None], nx, ny).reshape(tiles, 8, ny)
    if any((inside[kept] & np.roll(inside[folded], ny // 2, 1)).any() for kept, folded in pairs):
        return ()
    return pairs


def kernel(
    n, pairs, rhs_hbm, lab_hbm, table_hbm, out,
    lab, rhs, gx, gy, gz, idf, dg, ua, ub, tmp, pro,
    lab_out, fine_out, part, edge, far_out, far, ends, begin, vn, spread, line_out, line_all, row_out, row_all, xs, table,
    load_sem, sems, gather_sem, tokens,
):
    me = lax.axis_index("slab")
    nx, ny = lab.shape[1:]
    hx_rows = nx // 2
    has_low, has_up = me > 0, me < n - 1

    load_table = pltpu.make_async_copy(table_hbm, table, load_sem.at[2])
    load_table.start()
    own_lab = pltpu.make_async_copy(lab_hbm, lab.at[pl.ds(2, 4)], load_sem.at[0])
    own_rhs = pltpu.make_async_copy(rhs_hbm.at[0], rhs.at[pl.ds(2, 4)], load_sem.at[1])
    own_lab.start()
    own_rhs.start()
    barrier = pltpu.get_barrier_semaphore()

    up, low = lax.rem(me + 1, n), lax.rem(me + n - 1, n)

    def signal(sem, distance):
        for near, other in ((me >= distance, me - distance), (me + distance < n, me + distance)):

            @pl.when(near)
            def _():
                pl.semaphore_signal(sem, inc=1, device_id={"slab": other}, device_id_type=MESH)

    for distance in range(1, min(REACH, n - 1) + 1):
        signal(barrier, distance)
    pl.semaphore_wait(barrier, jnp.minimum(me, REACH) + jnp.minimum(n - 1 - me, REACH))

    rounds = []
    while REACH * 2 ** len(rounds) < n - 1:
        rounds.append(REACH * 2 ** len(rounds))

    def round_start(r):
        if r < len(rounds):
            signal(tokens.at[r], rounds[r])

    def round_end(r):
        if r < len(rounds):
            distance = rounds[r]
            both = jnp.logical_and(me >= distance, me + distance < n)
            one = jnp.logical_xor(me >= distance, me + distance < n)
            pl.when(both)(lambda: pl.semaphore_wait(tokens.at[r], 2))
            pl.when(one)(lambda: pl.semaphore_wait(tokens.at[r], 1))

    sent = pl.ds(16, nx - 32) if pairs else pl.ds(0, nx)
    near_up = copy_to(lab_out.at[0, 0], lab.at[1, sent], sems, 0, up)
    near_low = copy_to(lab_out.at[1, 0], lab.at[6, sent], sems, 1, low)
    next_up = copy_to(lab_out.at[0, 1], lab.at[0, sent], sems, 2, up)
    next_low = copy_to(lab_out.at[1, 1], lab.at[7, sent], sems, 3, low)
    rhs_up = copy_to(fine_out.at[0, 0], rhs.at[1, sent], sems, 4, up)
    rhs_low = copy_to(fine_out.at[1, 0], rhs.at[6, sent], sems, 5, low)
    u1_up = copy_to(fine_out.at[0, 1], ua.at[0, sent], sems, 6, up)
    u1_low = copy_to(fine_out.at[1, 1], ua.at[7, sent], sems, 7, low)
    far_up = copy_to(far_out.at[0], far.at[0], sems, 8, up)
    far_low = copy_to(far_out.at[1], far.at[1], sems, 9, low)
    ends_up = copy_to(begin.at[0], ends.at[0], sems, 10, up)
    ends_low = copy_to(begin.at[1], ends.at[1], sems, 11, low)
    u2_up = copy_to(fine_out.at[0, 2], ub.at[0, sent], sems, 12, up)
    u2_low = copy_to(fine_out.at[1, 2], ub.at[7, sent], sems, 13, low)
    vn_up = copy_to(vn.at[1], vn.at[0], sems, 14, up)
    vn_low = copy_to(vn.at[1], vn.at[2], sems, 15, low)
    edge_up = copy_to(part.at[0], edge.at[0], sems, 16, up)
    edge_low = copy_to(part.at[1], edge.at[1], sems, 17, low)

    def send(upward, downward):
        pl.when(has_up)(upward.start)
        pl.when(has_low)(downward.start)

    def receive(upward, downward):
        pl.when(has_low)(upward.wait_recv)
        pl.when(has_up)(downward.wait_recv)

    tile_row = lax.broadcasted_iota(jnp.int32, (8, ny), 0)
    tile_lane = lax.broadcasted_iota(jnp.int32, (8, ny), 1)

    def tile(t):
        return pl.ds(8 * t, 8)

    def inside(t):
        return near_axis(tile_row + 8 * t, tile_lane, nx, ny)

    def half_turn(values):
        return pltpu.roll(values, ny // 2, 1)

    def fold(field, k, out_ref):
        out_ref[...] = field[k, sent]
        for kept, folded in pairs:
            out_ref[tile(kept - 2)] = jnp.where(inside(kept), field[k, tile(kept)], half_turn(field[k, tile(folded)]))

    def unfold(field, k):
        for kept, folded in pairs:
            both = field[k, tile(kept)]
            zero_tile = jnp.zeros_like(both)
            field[k, tile(folded)] = jnp.where(inside(folded), half_turn(both), zero_tile)
            field[k, tile(kept)] = jnp.where(inside(kept), both, zero_tile)

    round_start(0)
    own_lab.wait()
    fold(lab, 5, lab_out.at[0, 0])
    fold(lab, 2, lab_out.at[1, 0])
    send(near_up, near_low)
    fold(lab, 4, lab_out.at[0, 1])
    fold(lab, 3, lab_out.at[1, 1])
    send(next_up, next_low)
    own_rhs.wait()
    fold(rhs, 5, fine_out.at[0, 0])
    fold(rhs, 2, fine_out.at[1, 0])
    send(rhs_up, rhs_low)

    def clear(ref, first, count):
        for k in range(first, first + count):
            ref[k] = jnp.zeros(ref.shape[1:], ref.dtype)

    @pl.when(me == 0)
    def _():
        clear(lab, 0, 2)
        clear(rhs, 1, 1)
        clear(ua, 0, 1)
        clear(edge, 0, 1)
        clear(far, 0, 1)
        clear(ends, 0, 1)
        clear(ub, 0, 1)
        clear(vn, 0, 1)

    @pl.when(me == n - 1)
    def _():
        clear(lab, 6, 2)
        clear(rhs, 6, 1)
        clear(ua, 7, 1)
        clear(edge, 1, 1)
        clear(far, 1, 1)
        clear(ends, 1, 1)
        clear(ub, 7, 1)
        clear(vn, 2, 1)

    xs[...] = jnp.zeros(xs.shape, xs.dtype)

    fine_row = lax.broadcasted_iota(jnp.int32, (nx, ny), 0) % 2 == 1
    fine_lane = lax.broadcasted_iota(jnp.int32, (nx, ny), 1) % 2 == 1
    even = lax.broadcasted_iota(jnp.int32, (hx_rows, ny), 1) % 2 == 0

    def select(values, column):
        chosen = jnp.full(values.shape, table[column, 0], jnp.float32)
        for tissue in range(1, LABELS):
            chosen = jnp.where(values == tissue, table[column, tissue], chosen)
        return chosen

    def harmonic(a, b):
        return 2.0 * a * b / (a + b)

    def active(k):
        return (lab[k] > 0).astype(jnp.float32)

    def side_faces(k):
        here = lab[k]
        a = (here > 0).astype(jnp.float32)
        sx, sy = select(here, 0), select(here, 1)
        hx = harmonic(pltpu.roll(sx, 1, 0), sx)
        gx[k] = hx * a * pltpu.roll(a, 1, 0)
        hy = harmonic(pltpu.roll(sy, 1, 1), sy)
        gy[k] = hy * a * pltpu.roll(a, 1, 1)
        return hx + pltpu.roll(hx, nx - 1, 0) + hy + pltpu.roll(hy, ny - 1, 1)

    def face_below(k):
        h = harmonic(select(lab[k - 1], 2), select(lab[k], 2))
        gz[k] = h * active(k - 1) * active(k)
        return h

    def finish(k, faces):
        a = active(k)
        diagonal = a * faces + (1.0 - a)
        dg[k] = diagonal
        idf[k] = OMEGA * a / diagonal

    def over(first, last, body):
        for k in range(first, last):
            body(k)

    def first_sweep(k):
        ua[k] = idf[k] * rhs[k]

    def neighbours(field, k):
        u = field[k]
        cx, cy = gx[k], gy[k]
        total = cx * pltpu.roll(u, 1, 0) + pltpu.roll(cx * u, nx - 1, 0)
        total = total + cy * pltpu.roll(u, 1, 1) + pltpu.roll(cy * u, ny - 1, 1)
        return u, total + gz[k] * field[k - 1] + gz[k + 1] * field[k + 1]

    def sweep(src, dst, shift=0):
        def body(k):
            u, total = neighbours(src, k)
            dst[k - shift] = (1.0 - OMEGA) * u + idf[k] * (rhs[k] + total)

        return body

    def residual(k):
        u, total = neighbours(ub, k)
        return jnp.where(idf[k] > 0.0, rhs[k] - dg[k] * u + total, 0.0)

    second_sweep = sweep(ua, ub)

    load_table.wait()
    h3, h4, h5 = face_below(3), face_below(4), face_below(5)
    finish(3, side_faces(3) + h3 + h4)
    finish(4, side_faces(4) + h4 + h5)
    dg[2] = side_faces(2) + h3
    dg[5] = side_faces(5) + h5
    over(3, 5, first_sweep)
    fold(ua, 4, fine_out.at[0, 1])
    fold(ua, 3, fine_out.at[1, 1])

    turn = itertools.count()

    def rows_apart(plane):
        slot = next(turn) % 6
        tmp[slot] = plane
        return tmp[slot, pl.ds(0, hx_rows, 2), :], tmp[slot, pl.ds(1, hx_rows, 2), :]

    def rows_even(plane):
        return rows_apart(plane)[0]

    def rows_sum(plane):
        first, second = rows_apart(plane)
        return first + second

    def lanes_sum(t0, t1):
        return jnp.where(even, t0 + pltpu.roll(t0, ny - 1, 1), t1 + pltpu.roll(t1, 1, 1))

    def lanes_even(t0, t1):
        return jnp.where(even, t0, pltpu.roll(t1, 1, 1))

    def restrict(p0, p1):
        return lanes_sum(rows_sum(p0), rows_sum(p1))

    def inner(k):
        doubled = jnp.where(fine_row, gx[k], 0.0) + jnp.where(fine_lane, gy[k], 0.0)
        if k % 2 == 1:
            doubled = doubled + gz[k]
        return active(k) * dg[k] - 2.0 * doubled

    def to_even(pack):
        return pltpu.roll(pack, ny - 1, 1)

    def to_odd(pack):
        return pltpu.roll(pack, 1, 1)

    def swap(pack):
        return jnp.where(even, to_even(pack), to_odd(pack))

    def of_odd(a, b):
        return jnp.where(even, to_even(a), b)

    def of_even(a, b):
        return jnp.where(even, a, to_odd(b))

    def beside(field, cx, cy):
        total = cx * pltpu.roll(field, 1, 0) + pltpu.roll(cx * field, hx_rows - 1, 0)
        return total + cy * pltpu.roll(field, 2, 1) + pltpu.roll(cy * field, ny - 2, 1)

    def side_sum(cx, cy):
        return cx + pltpu.roll(cx, hx_rows - 1, 0) + cy + pltpu.roll(cy, ny - 2, 1)

    h4_low, h4_up = rows_sum(active(3) * h4), rows_sum(active(4) * h4)
    middle = rows_sum(gz[4])
    z_in = lanes_sum(middle, middle)
    part[0] = jnp.where(even, h4_up + to_even(h4_up), z_in)
    part[1] = jnp.where(even, h4_low + to_even(h4_low), z_in)
    send(edge_up, edge_low)
    send(u1_up, u1_low)

    def coarse_pack(k0, k1, k2, k3):
        raw = restrict(inner(k0) + inner(k1), inner(k2) + inner(k3))
        x = lanes_sum(rows_even(gx[k0] + gx[k1]), rows_even(gx[k2] + gx[k3]))
        y = lanes_even(rows_sum(gy[k0] + gy[k1]), rows_sum(gy[k2] + gy[k3]))
        return raw, x, y

    round_end(0)
    round_start(1)
    receive(near_up, near_low)
    unfold(lab, 1)
    unfold(lab, 6)
    h2, h6 = face_below(2), face_below(6)
    tmp[6] = h2
    tmp[7] = h6
    finish(2, dg[2] + h2)
    finish(5, dg[5] + h6)
    over(0, 2, lambda k: first_sweep(2 + 3 * k))
    over(3, 5, second_sweep)
    fold(ub, 4, fine_out.at[0, 2])
    fold(ub, 3, fine_out.at[1, 2])
    raw, coarse_x, coarse_y = coarse_pack(2, 3, 4, 5)
    side = side_sum(coarse_x, coarse_y)
    active1 = jnp.where(raw > 0.0, 1.0, 0.0)
    diag1 = raw + (1.0 - active1)
    weight = OMEGA * active1 / diag1
    z_out = restrict(gz[2], gz[6])
    own_part, out_part, in_part = (1.0 - OMEGA) * active1 + weight * side, weight * z_out, weight * z_in
    spread[...] = in_part
    in_first, in_second = spread[pl.ds(0, hx_rows // 2, 2), :], spread[pl.ds(1, hx_rows // 2, 2), :]
    even_half = even[: hx_rows // 2]
    far_out[0, pl.ds(0, hx_rows)] = of_even(own_part, out_part)
    far_out[0, pl.ds(hx_rows, hx_rows // 2)] = jnp.where(even_half, in_first, to_odd(in_second))
    far_out[1, pl.ds(0, hx_rows)] = of_odd(own_part, out_part)
    far_out[1, pl.ds(hx_rows, hx_rows // 2)] = jnp.where(even_half, to_even(in_first), in_second)
    send(far_up, far_low)

    sub = lax.broadcasted_iota(jnp.int32, (8, ny), 0)
    sub_even = lax.broadcasted_iota(jnp.int32, (8, ny), 1) % 2 == 0

    def row_sum(pack):
        return jnp.sum(pack, axis=0, keepdims=True)

    def gather(out, everyone, slot, rows_of):
        tile = jnp.zeros((8, ny), jnp.float32)
        for row, values in enumerate(rows_of):
            tile = jnp.where(sub == row, values, tile)
        lower = jnp.sum(jnp.where(sub_even, tile, 0.0), axis=1, keepdims=True)
        upper = jnp.sum(jnp.where(sub_even, 0.0, tile), axis=1, keepdims=True)
        tile = jnp.where(sub_even, lower, upper)
        out[...] = tile
        everyone[me] = tile
        rows = pl.ds(0, len(rows_of))

        def one(step, carry):
            pltpu.make_async_remote_copy(
                src_ref=out.at[rows],
                dst_ref=everyone.at[me, rows],
                send_sem=gather_sem.at[0, slot],
                recv_sem=gather_sem.at[1, slot],
                device_id={"slab": lax.rem(me + step, n)},
                device_id_type=MESH,
            ).start()
            return carry

        lax.fori_loop(1, n, one, 0)

    def gather_wait(everyone, side, slot, count):
        rest = everyone.at[pl.ds(0, n - 1), pl.ds(0, count)]
        pltpu.make_async_copy(rest, rest, gather_sem.at[side, slot]).wait()

    line_sums = (row_sum(raw - 2.0 * (coarse_x + coarse_y)), row_sum(jnp.where(even, z_out, z_in)))
    round_end(1)
    round_start(2)

    receive(next_up, next_low)
    unfold(lab, 0)
    unfold(lab, 7)
    h1, h7 = face_below(1), face_below(7)
    finish(1, side_faces(1) + h1 + tmp[6])
    finish(6, side_faces(6) + h7 + tmp[7])
    dg[0] = side_faces(0) + h1
    dg[7] = side_faces(7) + h7
    receive(rhs_up, rhs_low)
    unfold(rhs, 1)
    unfold(rhs, 6)
    round_end(2)
    round_start(3)
    over(0, 2, lambda k: first_sweep(1 + 5 * k))
    over(0, 2, lambda k: second_sweep(2 + 3 * k))
    r3, r4 = residual(3), residual(4)
    edge_raw, edge_x, edge_y = coarse_pack(0, 1, 6, 7)
    edge_side = side_sum(edge_x, edge_y)

    def split(both):
        below, above = both
        return jnp.where(even, below, to_odd(above)), jnp.where(even, to_even(below), above)

    receive(edge_up, edge_low)
    edge_face, edge_in = split((edge[0], edge[1]))
    edge_diag = edge_raw + edge_face
    edge_active = edge_diag > 0.0
    edge_weight = jnp.where(edge_active, OMEGA / jnp.where(edge_active, edge_diag, 1.0), 0.0)
    own_1 = weight * (diag1 - side)
    edge_own_1, edge_out_1, edge_in_1 = edge_weight * (edge_diag - edge_side), edge_weight * z_out, edge_weight * edge_in
    to_out2 = out_part * edge_in_1
    to_out1 = (2.0 - OMEGA) * out_part + weight * beside(out_part, coarse_x, coarse_y) - out_part * edge_own_1
    to_own = 1.0 + (OMEGA - 2.0) * own_1 - weight * beside(own_1, coarse_x, coarse_y) + out_part * edge_out_1 + in_part * swap(in_part)
    to_in1 = (2.0 - OMEGA) * in_part + weight * beside(in_part, coarse_x, coarse_y) - in_part * swap(own_1)
    to_in2 = in_part * swap(out_part)
    edge_own_part = jnp.where(edge_active, 1.0 - OMEGA, 0.0) + edge_weight * edge_side

    for r in range(3, len(rounds)):
        round_end(r)
        round_start(r + 1)
    gather(line_out, line_all, 0, line_sums)

    def partial_sweep(k, beside_k, face):
        u, cx, cy = ua[k], gx[k], gy[k]
        total = cx * pltpu.roll(u, 1, 0) + pltpu.roll(cx * u, nx - 1, 0)
        total = total + cy * pltpu.roll(u, 1, 1) + pltpu.roll(cy * u, ny - 1, 1)
        ub[k] = (1.0 - OMEGA) * u + idf[k] * (rhs[k] + total + gz[face] * ua[beside_k])

    partial_sweep(1, 2, 2)
    partial_sweep(6, 5, 6)
    b1_part = restrict(residual(2) + r3, r4 + residual(5))
    tmp[6] = idf[1] * gz[1]
    tmp[7] = idf[6] * gz[7]
    pro[0] = gz[2] * tmp[6]
    pro[1] = gz[6] * tmp[7]

    receive(u1_up, u1_low)
    unfold(ua, 0)
    unfold(ua, 7)
    b1 = b1_part + restrict(pro[0] * ua[0], pro[1] * ua[7])

    row_even = even[:1]

    def row_swap(row):
        return jnp.where(row_even, to_even(row), to_odd(row))

    v1 = weight * b1
    begin[0] = jnp.where(even, to_even(b1), to_odd(v1))
    begin[1] = jnp.where(even, b1, v1)
    send(ends_up, ends_low)
    ub[1] = ub[1] + tmp[6] * ua[0]
    ub[6] = ub[6] + tmp[7] * ua[7]
    gather(
        row_out, row_all, 1,
        (
            row_sum(to_own * b1) + row_swap(row_sum(to_in1 * b1)),
            row_swap(row_sum(to_out1 * b1)) + row_sum(to_in2 * b1),
            row_sum(to_out2 * b1),
        ),
    )

    def own_sweep(own, beyond):
        total = beside(own, coarse_x, coarse_y) + z_out * beyond + z_in * swap(own)
        return (1.0 - OMEGA) * own + weight * (b1 + total)

    def edge_sweep(own, beyond, further):
        total = beside(beyond, edge_x, edge_y) + z_out * own + edge_in * further
        return (1.0 - OMEGA) * beyond + edge_weight * (edge_b1 + total)

    receive(ends_up, ends_low)
    edge_b1, far_v1 = split((ends[0], ends[1]))
    edge_v1 = edge_weight * edge_b1
    v2, edge_v2 = own_sweep(v1, edge_v1), edge_sweep(v1, edge_v1, far_v1)
    v3 = own_sweep(v2, edge_v2)
    vn[1] = v3
    send(vn_up, vn_low)
    send(u2_up, u2_low)

    receive(far_up, far_low)
    far_own_part, far_out_part = split((far[0, pl.ds(0, hx_rows)], far[1, pl.ds(0, hx_rows)]))
    below, above = far[0, pl.ds(hx_rows, hx_rows // 2)], far[1, pl.ds(hx_rows, hx_rows // 2)]
    spread[pl.ds(0, hx_rows // 2, 2), :] = jnp.where(even_half, below, to_odd(above))
    spread[pl.ds(1, hx_rows // 2, 2), :] = jnp.where(even_half, to_even(below), above)

    gather_wait(line_all, 1, 0, 2)

    line_even = lax.broadcasted_iota(jnp.int32, (n, ny), 1) % 2 == 0

    def line_row(everyone, row):
        return everyone.reshape(n * 8, ny)[pl.ds(row, n, 8), :]

    def apart(both):
        lower = jnp.where(line_even, both, pltpu.roll(both, 1, 1))
        return lower, jnp.where(line_even, pltpu.roll(both, ny - 1, 1), both)

    (de, do), (fe, fo) = apart(line_row(line_all, 0)), apart(line_row(line_all, 1))

    def back(x, s):
        return pltpu.roll(x, s % n, 0)

    def ahead(x, s):
        return pltpu.roll(x, (n - s) % n, 0)

    inv_odd = 1.0 / do
    to_low = fe * back(inv_odd, 1)
    to_up = fo * inv_odd
    fe_next = ahead(fe, 1)
    diag = de - fe * to_low - fo * to_up
    lower = -to_low * back(fo, 1)
    upper = -to_up * fe_next
    steps = []
    shift = 1
    while shift < n:
        alpha, gamma = lower / back(diag, shift), upper / ahead(diag, shift)
        steps.append((shift, alpha, gamma))
        diag = diag - alpha * back(upper, shift) - gamma * ahead(lower, shift)
        lower, upper = -alpha * back(lower, shift), -gamma * ahead(upper, shift)
        shift *= 2
    inv_diag = 1.0 / diag

    gather_wait(row_all, 1, 1, 3)
    one, two = line_row(row_all, 1), line_row(row_all, 2)
    sums = line_row(row_all, 0) + jnp.where(line_even, back(one, 1) + ahead(two, 1), ahead(one, 1) + back(two, 1))
    be, bo = apart(sums)
    reduced = be + to_low * back(bo, 1) + to_up * bo
    for shift, alpha, gamma in steps:
        reduced = reduced - alpha * back(reduced, shift) - gamma * ahead(reduced, shift)
    e_even = reduced * inv_diag
    e_odd = (bo + fo * e_even + fe_next * ahead(e_even, 1)) * inv_odd
    xs[0, pl.ds(8, n), :] = jnp.where(line_even, e_even, e_odd)
    xs[1, pl.ds(8, n), :] = jnp.where(line_even, e_odd, e_even)

    def line(side, distance):
        return jnp.broadcast_to(xs[side, pl.ds(me + 8 + distance, 1), :], (hx_rows, ny))

    def outward(side, distance):
        return jnp.where(even, line(side, -distance), line(side, distance))

    e_own, e_in = line(0, 0), line(1, 0)
    e_out, e_out2, e_out3 = outward(1, 1), outward(0, 1), outward(1, 2)
    receive(vn_up, vn_low)
    below, above = vn[0], vn[2]
    w2 = v3 + own_part * e_own + out_part * e_out + in_part * e_in
    edge_w2 = jnp.where(even, to_even(below), to_odd(above))
    edge_w2 = edge_w2 + edge_own_part * e_out + edge_out_1 * e_own + edge_in_1 * e_out2
    far_w2 = jnp.where(even, below, above) + far_own_part * e_out2 + spread[...] * e_out + far_out_part * e_out3
    w3, edge_w3 = own_sweep(w2, edge_w2), edge_sweep(w2, edge_w2, far_w2)

    def prolong(slot, plane):
        pro[slot, pl.ds(0, hx_rows, 2), :] = plane
        pro[slot, pl.ds(1, hx_rows, 2), :] = plane

    def lower_plane(pack):
        return jnp.where(even, pack, pltpu.roll(pack, 1, 1))

    def upper_plane(pack):
        return jnp.where(even, pltpu.roll(pack, ny - 1, 1), pack)

    prolong(0, lower_plane(edge_w3))
    prolong(1, lower_plane(w3))
    prolong(2, upper_plane(w3))
    prolong(3, upper_plane(edge_w3))

    receive(u2_up, u2_low)
    unfold(ub, 0)
    unfold(ub, 7)

    def correct(k):
        ua[k] = ub[k] + jnp.where(lab[k] > 0, pro[k // 2], 0.0)

    over(0, 8, correct)

    over(1, 7, sweep(ua, tmp))
    over(2, 6, sweep(tmp, out.at[0], 2))

    for upward, downward in (
        (near_up, near_low), (next_up, next_low), (rhs_up, rhs_low), (far_up, far_low), (ends_up, ends_low), (vn_up, vn_low),
        (u2_up, u2_low), (edge_up, edge_low), (u1_up, u1_low),
    ):
        pl.when(has_up)(upward.wait_send)
        pl.when(has_low)(downward.wait_send)
    gather_wait(line_all, 0, 0, 2)
    gather_wait(row_all, 0, 1, 3)


def on_device(n, rhs, labels, sigma_table):
    planes, nx, ny = labels.shape
    pairs = folds(nx, ny)
    kept = nx - 32 if pairs else nx
    fine = lambda count: pltpu.VMEM((count, nx, ny), jnp.float32)
    packs = lambda *counts: pltpu.VMEM((*counts, nx // 2, ny), jnp.float32)
    thirds = lambda *counts: pltpu.VMEM((*counts, nx // 2 + nx // 4, ny), jnp.float32)
    tiles = lambda *counts: pltpu.VMEM((*counts, 8, ny), jnp.float32)
    return pl.pallas_call(
        functools.partial(kernel, n, pairs),
        out_shape=pltpu.VMEM(rhs.shape, jnp.float32),
        in_specs=[
            pl.BlockSpec(memory_space=pl.ANY),
            pl.BlockSpec(memory_space=pl.ANY),
            pl.BlockSpec(memory_space=pl.ANY),
        ],
        out_specs=pl.BlockSpec(memory_space=pltpu.VMEM),
        scratch_shapes=[
            pltpu.VMEM((8, nx, ny), jnp.int32),
            fine(8), fine(8), fine(8), fine(8), fine(8), fine(8), fine(8), fine(8),
            fine(8), fine(4),
            pltpu.VMEM((2, 2, kept, ny), jnp.int32), pltpu.VMEM((2, 3, kept, ny), jnp.float32),
            packs(2), packs(2), thirds(2), thirds(2), packs(2), packs(2), packs(3), packs(),
            tiles(), tiles(n), tiles(), tiles(n),
            pltpu.VMEM((2, n + 16, ny), jnp.float32),
            pltpu.SMEM((3, LABELS), jnp.float32),
            pltpu.SemaphoreType.DMA((3,)),
            pltpu.SemaphoreType.DMA((2, 18)),
            pltpu.SemaphoreType.DMA((2, 2)),
            pltpu.SemaphoreType.REGULAR((n.bit_length(),)),
        ],
        compiler_params=pltpu.CompilerParams(collective_id=0, has_side_effects=True),
    )(rhs, labels, sigma_table.T)


def solution(mesh):
    placed = (P("groups", "slab", None, None), P("slab", "groups", None), P())
    return jax.shard_map(
        functools.partial(on_device, mesh.shape["slab"]),
        mesh=mesh,
        in_specs=placed,
        out_specs=P("groups", "slab", None, None),
        check_vma=False,
    )
```

```python
import functools
import itertools

import jax
import jax.numpy as jnp
import numpy as np
from jax import lax
from jax.experimental import pallas as pl
from jax.experimental.pallas import tpu as pltpu
from jax.sharding import PartitionSpec as P

OMEGA = 0.8
LABELS = 5
MESH = pl.DeviceIdType.MESH
REACH = 4


def copy_to(src, dst, sems, slot, target):
    return pltpu.make_async_remote_copy(
        src_ref=src,
        dst_ref=dst,
        send_sem=sems.at[0, slot],
        recv_sem=sems.at[1, slot],
        device_id={"slab": target},
        device_id_type=MESH,
    )


def near_axis(row, lane, nx, ny, bound):
    across, along = 2 * row + 1 - nx, 2 * lane + 1 - ny
    return (across * across + along * along) * 1000 <= bound


def folds(n, nx, ny):
    tiles = nx // 8
    whole = (0, tiles, (), 4 * 1000 * nx * nx)
    if nx != ny or nx < 128 or nx % 8:
        return whole, whole, n

    def fits(pairs, bound, first, count):
        inside = near_axis(np.arange(nx)[:, None], np.arange(ny)[None], nx, ny, bound).reshape(tiles, 8, ny)
        sent = set(range(first, first + count)) | {folded for _, folded in pairs}
        lost = any(inside[t].any() for t in range(tiles) if t not in sent)
        return not lost and not any((inside[kept] & np.roll(inside[folded], ny // 2, 1)).any() for kept, folded in pairs)

    pairs = ((2, tiles - 2), (4, 0), (tiles - 5, tiles - 1), (tiles - 3, 1))
    middle = (2, tiles - 4, pairs, 813 * nx * nx)
    if not fits(pairs, middle[3], 2, tiles - 4):
        return whole, whole, n
    pairs = ((4, tiles - 4), (tiles - 5, 3), (5, tiles - 3), (tiles - 6, 2))
    outer, rim = middle, n
    for slab in range(n - 1, n // 2, -1):
        away = (4 * slab + 0.5 - 2 * n) / (0.55 * 4 * n)
        bound = int((0.813 - 0.81 * away * away) * 1000 * nx * nx)
        if not fits(pairs, bound, 4, tiles - 8):
            break
        outer, rim = (4, tiles - 8, pairs, bound), slab
    return middle, outer, rim


def kernel(
    n, ways, rhs_hbm, lab_hbm, table_hbm, out,
    lab, rhs, gx, gy, gz, idf, dg, ua, ub, tmp, pro,
    lab_out, fine_out, part, edge, far_out, far, ends, begin, vn, spread, line_out, line_all, row_out, row_all, xs, table,
    load_sem, sems, gather_sem, tokens,
):
    me = lax.axis_index("slab")
    nx, ny = lab.shape[1:]
    hx_rows = nx // 2
    has_low, has_up = me > 0, me < n - 1

    load_table = pltpu.make_async_copy(table_hbm, table, load_sem.at[2])
    load_table.start()
    own_lab = pltpu.make_async_copy(lab_hbm, lab.at[pl.ds(2, 4)], load_sem.at[0])
    own_rhs = pltpu.make_async_copy(rhs_hbm.at[0], rhs.at[pl.ds(2, 4)], load_sem.at[1])
    own_lab.start()
    own_rhs.start()
    barrier = pltpu.get_barrier_semaphore()

    up, low = lax.rem(me + 1, n), lax.rem(me + n - 1, n)

    def signal(sem, distance):
        for near, other in ((me >= distance, me - distance), (me + distance < n, me + distance)):

            @pl.when(near)
            def _():
                pl.semaphore_signal(sem, inc=1, device_id={"slab": other}, device_id_type=MESH)

    for distance in range(1, min(REACH, n - 1) + 1):
        signal(barrier, distance)
    pl.semaphore_wait(barrier, jnp.minimum(me, REACH) + jnp.minimum(n - 1 - me, REACH))

    rounds = []
    while REACH * 2 ** len(rounds) < n - 1:
        rounds.append(REACH * 2 ** len(rounds))

    def round_start(r):
        if r < len(rounds):
            signal(tokens.at[r], rounds[r])

    def round_end(r):
        if r < len(rounds):
            distance = rounds[r]
            both = jnp.logical_and(me >= distance, me + distance < n)
            one = jnp.logical_xor(me >= distance, me + distance < n)
            pl.when(both)(lambda: pl.semaphore_wait(tokens.at[r], 2))
            pl.when(one)(lambda: pl.semaphore_wait(tokens.at[r], 1))

    middle, outer, rim = ways

    def plane_copies(out_ref, field, plane, slot, target):
        return tuple(
            copy_to(out_ref.at[pl.ds(0, 8 * count)], field.at[plane, pl.ds(8 * first, 8 * count)], sems, slot, target)
            for first, count, _, _ in (middle, outer)
        )

    near_up = plane_copies(lab_out.at[0, 0], lab, 1, 0, up)
    near_low = plane_copies(lab_out.at[1, 0], lab, 6, 1, low)
    next_up = plane_copies(lab_out.at[0, 1], lab, 0, 2, up)
    next_low = plane_copies(lab_out.at[1, 1], lab, 7, 3, low)
    rhs_up = plane_copies(fine_out.at[0, 0], rhs, 1, 4, up)
    rhs_low = plane_copies(fine_out.at[1, 0], rhs, 6, 5, low)
    u1_up = plane_copies(fine_out.at[0, 1], ua, 0, 6, up)
    u1_low = plane_copies(fine_out.at[1, 1], ua, 7, 7, low)
    far_up = copy_to(far_out.at[0], far.at[0], sems, 8, up)
    far_low = copy_to(far_out.at[1], far.at[1], sems, 9, low)
    ends_up = copy_to(begin.at[0], ends.at[0], sems, 10, up)
    ends_low = copy_to(begin.at[1], ends.at[1], sems, 11, low)
    u2_up = plane_copies(fine_out.at[0, 2], ub, 0, 12, up)
    u2_low = plane_copies(fine_out.at[1, 2], ub, 7, 13, low)
    vn_up = copy_to(vn.at[1], vn.at[0], sems, 14, up)
    vn_low = copy_to(vn.at[1], vn.at[2], sems, 15, low)
    edge_up = copy_to(part.at[0], edge.at[0], sems, 16, up)
    edge_low = copy_to(part.at[1], edge.at[1], sems, 17, low)

    def send(upward, downward):
        pl.when(has_up)(upward.start)
        pl.when(has_low)(downward.start)

    def receive(upward, downward):
        pl.when(has_low)(upward.wait_recv)
        pl.when(has_up)(downward.wait_recv)

    tile_row = lax.broadcasted_iota(jnp.int32, (8, ny), 0)
    tile_lane = lax.broadcasted_iota(jnp.int32, (8, ny), 1)

    def tile(t):
        return pl.ds(8 * t, 8)

    def inside(t, bound):
        return near_axis(tile_row + 8 * t, tile_lane, nx, ny, bound)

    def half_turn(values):
        return pltpu.roll(values, ny // 2, 1)

    def fold(field, k, out_ref, way):
        first, count, pairs, bound = way
        out_ref[pl.ds(0, 8 * count)] = field[k, pl.ds(8 * first, 8 * count)]
        for kept, folded in pairs:
            both = jnp.where(inside(kept, bound), field[k, tile(kept)], half_turn(field[k, tile(folded)]))
            out_ref[tile(kept - first)] = both

    def unfold(field, k, way):
        first, count, pairs, bound = way
        zero_tile = jnp.zeros((8, ny), field.dtype)
        for kept, folded in pairs:
            both = field[k, tile(kept)]
            field[k, tile(folded)] = jnp.where(inside(folded, bound), half_turn(both), zero_tile)
            field[k, tile(kept)] = jnp.where(inside(kept, bound), both, zero_tile)
        for t in set(range(nx // 8)) - set(range(first, first + count)) - {folded for _, folded in pairs}:
            field[k, tile(t)] = zero_tile

    def each_way(exists, thin, action):
        if rim == n:
            pl.when(exists)(lambda: action(0))
        else:
            pl.when(jnp.logical_and(exists, jnp.logical_not(thin)))(lambda: action(0))
            pl.when(jnp.logical_and(exists, thin))(lambda: action(1))

    both_ways = (middle, outer)
    thin_up, thin_low = n - 1 - me >= rim, me >= rim
    from_low_thin, from_up_thin = n - me >= rim, me + 1 >= rim

    def send_fine(field, k_up, k_low, outs, upward, downward):
        def go(k, out_ref, copies):
            def action(way):
                fold(field, k, out_ref, both_ways[way])
                copies[way].start()

            return action

        each_way(has_up, thin_up, go(k_up, outs[0], upward))
        each_way(has_low, thin_low, go(k_low, outs[1], downward))

    def receive_fine(field, k_low, k_up, upward, downward):
        def come(k, copies):
            def action(way):
                copies[way].wait_recv()
                unfold(field, k, both_ways[way])

            return action

        each_way(has_low, from_low_thin, come(k_low, upward))
        each_way(has_up, from_up_thin, come(k_up, downward))

    def sent_fine(upward, downward):
        each_way(has_up, thin_up, lambda way: upward[way].wait_send())
        each_way(has_low, thin_low, lambda way: downward[way].wait_send())

    round_start(0)
    own_lab.wait()
    send_fine(lab, 5, 2, (lab_out.at[0, 0], lab_out.at[1, 0]), near_up, near_low)
    send_fine(lab, 4, 3, (lab_out.at[0, 1], lab_out.at[1, 1]), next_up, next_low)
    own_rhs.wait()
    send_fine(rhs, 5, 2, (fine_out.at[0, 0], fine_out.at[1, 0]), rhs_up, rhs_low)

    def clear(ref, first, count):
        for k in range(first, first + count):
            ref[k] = jnp.zeros(ref.shape[1:], ref.dtype)

    @pl.when(me == 0)
    def _():
        clear(lab, 0, 2)
        clear(rhs, 1, 1)
        clear(ua, 0, 1)
        clear(edge, 0, 1)
        clear(far, 0, 1)
        clear(ends, 0, 1)
        clear(ub, 0, 1)
        clear(vn, 0, 1)

    @pl.when(me == n - 1)
    def _():
        clear(lab, 6, 2)
        clear(rhs, 6, 1)
        clear(ua, 7, 1)
        clear(edge, 1, 1)
        clear(far, 1, 1)
        clear(ends, 1, 1)
        clear(ub, 7, 1)
        clear(vn, 2, 1)

    xs[...] = jnp.zeros(xs.shape, xs.dtype)

    fine_row = lax.broadcasted_iota(jnp.int32, (nx, ny), 0) % 2 == 1
    fine_lane = lax.broadcasted_iota(jnp.int32, (nx, ny), 1) % 2 == 1
    even = lax.broadcasted_iota(jnp.int32, (hx_rows, ny), 1) % 2 == 0

    def select(values, column):
        chosen = jnp.full(values.shape, table[column, 0], jnp.float32)
        for tissue in range(1, LABELS):
            chosen = jnp.where(values == tissue, table[column, tissue], chosen)
        return chosen

    def harmonic(a, b):
        return 2.0 * a * b / (a + b)

    def active(k):
        return (lab[k] > 0).astype(jnp.float32)

    def side_faces(k):
        here = lab[k]
        a = (here > 0).astype(jnp.float32)
        sx, sy = select(here, 0), select(here, 1)
        hx = harmonic(pltpu.roll(sx, 1, 0), sx)
        gx[k] = hx * a * pltpu.roll(a, 1, 0)
        hy = harmonic(pltpu.roll(sy, 1, 1), sy)
        gy[k] = hy * a * pltpu.roll(a, 1, 1)
        return hx + pltpu.roll(hx, nx - 1, 0) + hy + pltpu.roll(hy, ny - 1, 1)

    def face_below(k):
        h = harmonic(select(lab[k - 1], 2), select(lab[k], 2))
        gz[k] = h * active(k - 1) * active(k)
        return h

    def finish(k, faces):
        a = active(k)
        diagonal = a * faces + (1.0 - a)
        dg[k] = diagonal
        idf[k] = OMEGA * a / diagonal

    def over(first, last, body):
        for k in range(first, last):
            body(k)

    def first_sweep(k):
        ua[k] = idf[k] * rhs[k]

    def neighbours(field, k):
        u = field[k]
        cx, cy = gx[k], gy[k]
        total = cx * pltpu.roll(u, 1, 0) + pltpu.roll(cx * u, nx - 1, 0)
        total = total + cy * pltpu.roll(u, 1, 1) + pltpu.roll(cy * u, ny - 1, 1)
        return u, total + gz[k] * field[k - 1] + gz[k + 1] * field[k + 1]

    def sweep(src, dst, shift=0):
        def body(k):
            u, total = neighbours(src, k)
            dst[k - shift] = (1.0 - OMEGA) * u + idf[k] * (rhs[k] + total)

        return body

    def residual(k):
        u, total = neighbours(ub, k)
        return jnp.where(idf[k] > 0.0, rhs[k] - dg[k] * u + total, 0.0)

    second_sweep = sweep(ua, ub)

    load_table.wait()
    h3, h4, h5 = face_below(3), face_below(4), face_below(5)
    finish(3, side_faces(3) + h3 + h4)
    finish(4, side_faces(4) + h4 + h5)
    dg[2] = side_faces(2) + h3
    dg[5] = side_faces(5) + h5
    over(3, 5, first_sweep)

    turn = itertools.count()

    def rows_apart(plane):
        slot = next(turn) % 6
        tmp[slot] = plane
        return tmp[slot, pl.ds(0, hx_rows, 2), :], tmp[slot, pl.ds(1, hx_rows, 2), :]

    def rows_even(plane):
        return rows_apart(plane)[0]

    def rows_sum(plane):
        first, second = rows_apart(plane)
        return first + second

    def lanes_sum(t0, t1):
        return jnp.where(even, t0 + pltpu.roll(t0, ny - 1, 1), t1 + pltpu.roll(t1, 1, 1))

    def lanes_even(t0, t1):
        return jnp.where(even, t0, pltpu.roll(t1, 1, 1))

    def restrict(p0, p1):
        return lanes_sum(rows_sum(p0), rows_sum(p1))

    def inner(k):
        doubled = jnp.where(fine_row, gx[k], 0.0) + jnp.where(fine_lane, gy[k], 0.0)
        if k % 2 == 1:
            doubled = doubled + gz[k]
        return active(k) * dg[k] - 2.0 * doubled

    def to_even(pack):
        return pltpu.roll(pack, ny - 1, 1)

    def to_odd(pack):
        return pltpu.roll(pack, 1, 1)

    def swap(pack):
        return jnp.where(even, to_even(pack), to_odd(pack))

    def of_odd(a, b):
        return jnp.where(even, to_even(a), b)

    def of_even(a, b):
        return jnp.where(even, a, to_odd(b))

    def beside(field, cx, cy):
        total = cx * pltpu.roll(field, 1, 0) + pltpu.roll(cx * field, hx_rows - 1, 0)
        return total + cy * pltpu.roll(field, 2, 1) + pltpu.roll(cy * field, ny - 2, 1)

    def side_sum(cx, cy):
        return cx + pltpu.roll(cx, hx_rows - 1, 0) + cy + pltpu.roll(cy, ny - 2, 1)

    h4_low, h4_up = rows_sum(active(3) * h4), rows_sum(active(4) * h4)
    middle = rows_sum(gz[4])
    z_in = lanes_sum(middle, middle)
    part[0] = jnp.where(even, h4_up + to_even(h4_up), z_in)
    part[1] = jnp.where(even, h4_low + to_even(h4_low), z_in)
    send(edge_up, edge_low)
    send_fine(ua, 4, 3, (fine_out.at[0, 1], fine_out.at[1, 1]), u1_up, u1_low)

    def coarse_pack(k0, k1, k2, k3):
        raw = restrict(inner(k0) + inner(k1), inner(k2) + inner(k3))
        x = lanes_sum(rows_even(gx[k0] + gx[k1]), rows_even(gx[k2] + gx[k3]))
        y = lanes_even(rows_sum(gy[k0] + gy[k1]), rows_sum(gy[k2] + gy[k3]))
        return raw, x, y

    round_end(0)
    round_start(1)
    receive_fine(lab, 1, 6, near_up, near_low)
    h2, h6 = face_below(2), face_below(6)
    tmp[6] = h2
    tmp[7] = h6
    finish(2, dg[2] + h2)
    finish(5, dg[5] + h6)
    over(0, 2, lambda k: first_sweep(2 + 3 * k))
    over(3, 5, second_sweep)
    raw, coarse_x, coarse_y = coarse_pack(2, 3, 4, 5)
    side = side_sum(coarse_x, coarse_y)
    active1 = jnp.where(raw > 0.0, 1.0, 0.0)
    diag1 = raw + (1.0 - active1)
    weight = OMEGA * active1 / diag1
    z_out = restrict(gz[2], gz[6])
    own_part, out_part, in_part = (1.0 - OMEGA) * active1 + weight * side, weight * z_out, weight * z_in
    spread[...] = in_part
    in_first, in_second = spread[pl.ds(0, hx_rows // 2, 2), :], spread[pl.ds(1, hx_rows // 2, 2), :]
    even_half = even[: hx_rows // 2]
    far_out[0, pl.ds(0, hx_rows)] = of_even(own_part, out_part)
    far_out[0, pl.ds(hx_rows, hx_rows // 2)] = jnp.where(even_half, in_first, to_odd(in_second))
    far_out[1, pl.ds(0, hx_rows)] = of_odd(own_part, out_part)
    far_out[1, pl.ds(hx_rows, hx_rows // 2)] = jnp.where(even_half, to_even(in_first), in_second)
    send(far_up, far_low)

    sub = lax.broadcasted_iota(jnp.int32, (8, ny), 0)
    sub_even = lax.broadcasted_iota(jnp.int32, (8, ny), 1) % 2 == 0

    def row_sum(pack):
        return jnp.sum(pack, axis=0, keepdims=True)

    def gather(out, everyone, slot, rows_of):
        tile = jnp.zeros((8, ny), jnp.float32)
        for row, values in enumerate(rows_of):
            tile = jnp.where(sub == row, values, tile)
        lower = jnp.sum(jnp.where(sub_even, tile, 0.0), axis=1, keepdims=True)
        upper = jnp.sum(jnp.where(sub_even, 0.0, tile), axis=1, keepdims=True)
        tile = jnp.where(sub_even, lower, upper)
        out[...] = tile
        everyone[me] = tile
        rows = pl.ds(0, len(rows_of))

        def one(step, carry):
            pltpu.make_async_remote_copy(
                src_ref=out.at[rows],
                dst_ref=everyone.at[me, rows],
                send_sem=gather_sem.at[0, slot],
                recv_sem=gather_sem.at[1, slot],
                device_id={"slab": lax.rem(me + step, n)},
                device_id_type=MESH,
            ).start()
            return carry

        lax.fori_loop(1, n, one, 0)

    def gather_wait(everyone, side, slot, count):
        rest = everyone.at[pl.ds(0, n - 1), pl.ds(0, count)]
        pltpu.make_async_copy(rest, rest, gather_sem.at[side, slot]).wait()

    line_sums = (row_sum(raw - 2.0 * (coarse_x + coarse_y)), row_sum(jnp.where(even, z_out, z_in)))
    round_end(1)
    round_start(2)

    receive_fine(lab, 0, 7, next_up, next_low)
    h1, h7 = face_below(1), face_below(7)
    finish(1, side_faces(1) + h1 + tmp[6])
    finish(6, side_faces(6) + h7 + tmp[7])
    dg[0] = side_faces(0) + h1
    dg[7] = side_faces(7) + h7
    receive_fine(rhs, 1, 6, rhs_up, rhs_low)
    round_end(2)
    round_start(3)
    over(0, 2, lambda k: first_sweep(1 + 5 * k))
    over(0, 2, lambda k: second_sweep(2 + 3 * k))
    r3, r4 = residual(3), residual(4)
    edge_raw, edge_x, edge_y = coarse_pack(0, 1, 6, 7)
    edge_side = side_sum(edge_x, edge_y)

    def split(both):
        below, above = both
        return jnp.where(even, below, to_odd(above)), jnp.where(even, to_even(below), above)

    receive(edge_up, edge_low)
    edge_face, edge_in = split((edge[0], edge[1]))
    edge_diag = edge_raw + edge_face
    edge_active = edge_diag > 0.0
    edge_weight = jnp.where(edge_active, OMEGA / jnp.where(edge_active, edge_diag, 1.0), 0.0)
    own_1 = weight * (diag1 - side)
    edge_own_1, edge_out_1, edge_in_1 = edge_weight * (edge_diag - edge_side), edge_weight * z_out, edge_weight * edge_in
    to_out2 = out_part * edge_in_1
    to_out1 = (2.0 - OMEGA) * out_part + weight * beside(out_part, coarse_x, coarse_y) - out_part * edge_own_1
    to_own = 1.0 + (OMEGA - 2.0) * own_1 - weight * beside(own_1, coarse_x, coarse_y) + out_part * edge_out_1 + in_part * swap(in_part)
    to_in1 = (2.0 - OMEGA) * in_part + weight * beside(in_part, coarse_x, coarse_y) - in_part * swap(own_1)
    to_in2 = in_part * swap(out_part)
    edge_own_part = jnp.where(edge_active, 1.0 - OMEGA, 0.0) + edge_weight * edge_side

    for r in range(3, len(rounds)):
        round_end(r)
        round_start(r + 1)
    gather(line_out, line_all, 0, line_sums)

    def partial_sweep(k, beside_k, face):
        u, cx, cy = ua[k], gx[k], gy[k]
        total = cx * pltpu.roll(u, 1, 0) + pltpu.roll(cx * u, nx - 1, 0)
        total = total + cy * pltpu.roll(u, 1, 1) + pltpu.roll(cy * u, ny - 1, 1)
        ub[k] = (1.0 - OMEGA) * u + idf[k] * (rhs[k] + total + gz[face] * ua[beside_k])

    partial_sweep(1, 2, 2)
    partial_sweep(6, 5, 6)
    b1_part = restrict(residual(2) + r3, r4 + residual(5))
    tmp[6] = idf[1] * gz[1]
    tmp[7] = idf[6] * gz[7]
    pro[0] = gz[2] * tmp[6]
    pro[1] = gz[6] * tmp[7]

    receive_fine(ua, 0, 7, u1_up, u1_low)
    b1 = b1_part + restrict(pro[0] * ua[0], pro[1] * ua[7])

    row_even = even[:1]

    def row_swap(row):
        return jnp.where(row_even, to_even(row), to_odd(row))

    v1 = weight * b1
    begin[0] = jnp.where(even, to_even(b1), to_odd(v1))
    begin[1] = jnp.where(even, b1, v1)
    send(ends_up, ends_low)
    ub[1] = ub[1] + tmp[6] * ua[0]
    ub[6] = ub[6] + tmp[7] * ua[7]
    gather(
        row_out, row_all, 1,
        (
            row_sum(to_own * b1) + row_swap(row_sum(to_in1 * b1)),
            row_swap(row_sum(to_out1 * b1)) + row_sum(to_in2 * b1),
            row_sum(to_out2 * b1),
        ),
    )

    def own_sweep(own, beyond):
        total = beside(own, coarse_x, coarse_y) + z_out * beyond + z_in * swap(own)
        return (1.0 - OMEGA) * own + weight * (b1 + total)

    def edge_sweep(own, beyond, further):
        total = beside(beyond, edge_x, edge_y) + z_out * own + edge_in * further
        return (1.0 - OMEGA) * beyond + edge_weight * (edge_b1 + total)

    receive(ends_up, ends_low)
    edge_b1, far_v1 = split((ends[0], ends[1]))
    edge_v1 = edge_weight * edge_b1
    v2, edge_v2 = own_sweep(v1, edge_v1), edge_sweep(v1, edge_v1, far_v1)
    v3 = own_sweep(v2, edge_v2)
    vn[1] = v3
    send(vn_up, vn_low)
    send_fine(ub, 4, 3, (fine_out.at[0, 2], fine_out.at[1, 2]), u2_up, u2_low)

    receive(far_up, far_low)
    far_own_part, far_out_part = split((far[0, pl.ds(0, hx_rows)], far[1, pl.ds(0, hx_rows)]))
    below, above = far[0, pl.ds(hx_rows, hx_rows // 2)], far[1, pl.ds(hx_rows, hx_rows // 2)]
    spread[pl.ds(0, hx_rows // 2, 2), :] = jnp.where(even_half, below, to_odd(above))
    spread[pl.ds(1, hx_rows // 2, 2), :] = jnp.where(even_half, to_even(below), above)

    gather_wait(line_all, 1, 0, 2)

    line_even = lax.broadcasted_iota(jnp.int32, (n, ny), 1) % 2 == 0

    def line_row(everyone, row):
        return everyone.reshape(n * 8, ny)[pl.ds(row, n, 8), :]

    def apart(both):
        lower = jnp.where(line_even, both, pltpu.roll(both, 1, 1))
        return lower, jnp.where(line_even, pltpu.roll(both, ny - 1, 1), both)

    (de, do), (fe, fo) = apart(line_row(line_all, 0)), apart(line_row(line_all, 1))

    def back(x, s):
        return pltpu.roll(x, s % n, 0)

    def ahead(x, s):
        return pltpu.roll(x, (n - s) % n, 0)

    inv_odd = 1.0 / do
    to_low = fe * back(inv_odd, 1)
    to_up = fo * inv_odd
    fe_next = ahead(fe, 1)
    diag = de - fe * to_low - fo * to_up
    lower = -to_low * back(fo, 1)
    upper = -to_up * fe_next
    steps = []
    shift = 1
    while shift < n:
        alpha, gamma = lower / back(diag, shift), upper / ahead(diag, shift)
        steps.append((shift, alpha, gamma))
        diag = diag - alpha * back(upper, shift) - gamma * ahead(lower, shift)
        lower, upper = -alpha * back(lower, shift), -gamma * ahead(upper, shift)
        shift *= 2
    inv_diag = 1.0 / diag

    gather_wait(row_all, 1, 1, 3)
    one, two = line_row(row_all, 1), line_row(row_all, 2)
    sums = line_row(row_all, 0) + jnp.where(line_even, back(one, 1) + ahead(two, 1), ahead(one, 1) + back(two, 1))
    be, bo = apart(sums)
    reduced = be + to_low * back(bo, 1) + to_up * bo
    for shift, alpha, gamma in steps:
        reduced = reduced - alpha * back(reduced, shift) - gamma * ahead(reduced, shift)
    e_even = reduced * inv_diag
    e_odd = (bo + fo * e_even + fe_next * ahead(e_even, 1)) * inv_odd
    xs[0, pl.ds(8, n), :] = jnp.where(line_even, e_even, e_odd)
    xs[1, pl.ds(8, n), :] = jnp.where(line_even, e_odd, e_even)

    def line(side, distance):
        return jnp.broadcast_to(xs[side, pl.ds(me + 8 + distance, 1), :], (hx_rows, ny))

    def outward(side, distance):
        return jnp.where(even, line(side, -distance), line(side, distance))

    e_own, e_in = line(0, 0), line(1, 0)
    e_out, e_out2, e_out3 = outward(1, 1), outward(0, 1), outward(1, 2)
    receive(vn_up, vn_low)
    below, above = vn[0], vn[2]
    w2 = v3 + own_part * e_own + out_part * e_out + in_part * e_in
    edge_w2 = jnp.where(even, to_even(below), to_odd(above))
    edge_w2 = edge_w2 + edge_own_part * e_out + edge_out_1 * e_own + edge_in_1 * e_out2
    far_w2 = jnp.where(even, below, above) + far_own_part * e_out2 + spread[...] * e_out + far_out_part * e_out3
    w3, edge_w3 = own_sweep(w2, edge_w2), edge_sweep(w2, edge_w2, far_w2)

    def prolong(slot, plane):
        pro[slot, pl.ds(0, hx_rows, 2), :] = plane
        pro[slot, pl.ds(1, hx_rows, 2), :] = plane

    def lower_plane(pack):
        return jnp.where(even, pack, pltpu.roll(pack, 1, 1))

    def upper_plane(pack):
        return jnp.where(even, pltpu.roll(pack, ny - 1, 1), pack)

    prolong(0, lower_plane(edge_w3))
    prolong(1, lower_plane(w3))
    prolong(2, upper_plane(w3))
    prolong(3, upper_plane(edge_w3))

    receive_fine(ub, 0, 7, u2_up, u2_low)

    def correct(k):
        ua[k] = ub[k] + jnp.where(lab[k] > 0, pro[k // 2], 0.0)

    over(0, 8, correct)

    over(1, 7, sweep(ua, tmp))
    over(2, 6, sweep(tmp, out.at[0], 2))

    for upward, downward in ((far_up, far_low), (ends_up, ends_low), (vn_up, vn_low), (edge_up, edge_low)):
        pl.when(has_up)(upward.wait_send)
        pl.when(has_low)(downward.wait_send)
    for upward, downward in ((near_up, near_low), (next_up, next_low), (rhs_up, rhs_low), (u1_up, u1_low), (u2_up, u2_low)):
        sent_fine(upward, downward)
    gather_wait(line_all, 0, 0, 2)
    gather_wait(row_all, 0, 1, 3)


def on_device(n, rhs, labels, sigma_table):
    planes, nx, ny = labels.shape
    ways = folds(n, nx, ny)
    kept = 8 * ways[0][1]
    fine = lambda count: pltpu.VMEM((count, nx, ny), jnp.float32)
    packs = lambda *counts: pltpu.VMEM((*counts, nx // 2, ny), jnp.float32)
    thirds = lambda *counts: pltpu.VMEM((*counts, nx // 2 + nx // 4, ny), jnp.float32)
    tiles = lambda *counts: pltpu.VMEM((*counts, 8, ny), jnp.float32)
    return pl.pallas_call(
        functools.partial(kernel, n, ways),
        out_shape=pltpu.VMEM(rhs.shape, jnp.float32),
        in_specs=[
            pl.BlockSpec(memory_space=pl.ANY),
            pl.BlockSpec(memory_space=pl.ANY),
            pl.BlockSpec(memory_space=pl.ANY),
        ],
        out_specs=pl.BlockSpec(memory_space=pltpu.VMEM),
        scratch_shapes=[
            pltpu.VMEM((8, nx, ny), jnp.int32),
            fine(8), fine(8), fine(8), fine(8), fine(8), fine(8), fine(8), fine(8),
            fine(8), fine(4),
            pltpu.VMEM((2, 2, kept, ny), jnp.int32), pltpu.VMEM((2, 3, kept, ny), jnp.float32),
            packs(2), packs(2), thirds(2), thirds(2), packs(2), packs(2), packs(3), packs(),
            tiles(), tiles(n), tiles(), tiles(n),
            pltpu.VMEM((2, n + 16, ny), jnp.float32),
            pltpu.SMEM((3, LABELS), jnp.float32),
            pltpu.SemaphoreType.DMA((3,)),
            pltpu.SemaphoreType.DMA((2, 18)),
            pltpu.SemaphoreType.DMA((2, 2)),
            pltpu.SemaphoreType.REGULAR((n.bit_length(),)),
        ],
        compiler_params=pltpu.CompilerParams(collective_id=0, has_side_effects=True),
    )(rhs, labels, sigma_table.T)


def solution(mesh):
    placed = (P("groups", "slab", None, None), P("slab", "groups", None), P())
    return jax.shard_map(
        functools.partial(on_device, mesh.shape["slab"]),
        mesh=mesh,
        in_specs=placed,
        out_specs=P("groups", "slab", None, None),
        check_vma=False,
    )
```

```python
import functools
import itertools

import jax
import jax.numpy as jnp
import numpy as np
from jax import lax
from jax.experimental import pallas as pl
from jax.experimental.pallas import tpu as pltpu
from jax.sharding import PartitionSpec as P

OMEGA = 0.8
LABELS = 5
MESH = pl.DeviceIdType.MESH
REACH = 4


def copy_to(src, dst, sems, slot, target):
    return pltpu.make_async_remote_copy(
        src_ref=src,
        dst_ref=dst,
        send_sem=sems.at[0, slot],
        recv_sem=sems.at[1, slot],
        device_id={"slab": target},
        device_id_type=MESH,
    )


def near_axis(row, lane, nx, ny, bound):
    across, along = 2 * row + 1 - nx, 2 * lane + 1 - ny
    return (across * across + along * along) * 1000 <= bound


def folds(n, nx, ny):
    tiles = nx // 8
    whole = (0, tiles, (), 4 * 1000 * nx * nx)
    if nx != ny or nx < 128 or nx % 8:
        return whole, whole, n

    def fits(pairs, bound, first, count):
        inside = near_axis(np.arange(nx)[:, None], np.arange(ny)[None], nx, ny, bound).reshape(tiles, 8, ny)
        sent = set(range(first, first + count)) | {folded for _, folded in pairs}
        lost = any(inside[t].any() for t in range(tiles) if t not in sent)
        return not lost and not any((inside[kept] & np.roll(inside[folded], ny // 2, 1)).any() for kept, folded in pairs)

    pairs = ((2, tiles - 2), (4, 0), (tiles - 5, tiles - 1), (tiles - 3, 1))
    middle = (2, tiles - 4, pairs, 813 * nx * nx)
    if not fits(pairs, middle[3], 2, tiles - 4):
        return whole, whole, n
    pairs = ((4, tiles - 4), (tiles - 5, 3), (5, tiles - 3), (tiles - 6, 2))
    outer, rim = middle, n
    for slab in range(n - 1, n // 2, -1):
        away = (4 * slab + 0.5 - 2 * n) / (0.55 * 4 * n)
        bound = int((0.813 - 0.81 * away * away) * 1000 * nx * nx)
        if not fits(pairs, bound, 4, tiles - 8):
            break
        outer, rim = (4, tiles - 8, pairs, bound), slab
    return middle, outer, rim


def kernel(
    n, ways, rhs_hbm, lab_hbm, table_hbm, out,
    lab, rhs, gx, gy, gz, idf, dg, ua, ub, tmp, pro,
    lab_out, fine_out, lab_in, fine_in, part, edge, far_out, far, ends, begin, vn, spread, line_out, line_all, row_out, row_all, xs, table,
    load_sem, sems, gather_sem, tokens,
):
    me = lax.axis_index("slab")
    nx, ny = lab.shape[1:]
    hx_rows = nx // 2
    has_low, has_up = me > 0, me < n - 1

    load_table = pltpu.make_async_copy(table_hbm, table, load_sem.at[2])
    load_table.start()
    own_lab = pltpu.make_async_copy(lab_hbm, lab.at[pl.ds(2, 4)], load_sem.at[0])
    own_rhs = pltpu.make_async_copy(rhs_hbm.at[0], rhs.at[pl.ds(2, 4)], load_sem.at[1])
    own_lab.start()
    own_rhs.start()
    barrier = pltpu.get_barrier_semaphore()

    up, low = lax.rem(me + 1, n), lax.rem(me + n - 1, n)

    def signal(sem, distance):
        for near, other in ((me >= distance, me - distance), (me + distance < n, me + distance)):

            @pl.when(near)
            def _():
                pl.semaphore_signal(sem, inc=1, device_id={"slab": other}, device_id_type=MESH)

    for distance in range(1, min(REACH, n - 1) + 1):
        signal(barrier, distance)
    pl.semaphore_wait(barrier, jnp.minimum(me, REACH) + jnp.minimum(n - 1 - me, REACH))

    rounds = []
    while REACH * 2 ** len(rounds) < n - 1:
        rounds.append(REACH * 2 ** len(rounds))

    def round_start(r):
        if r < len(rounds):
            signal(tokens.at[r], rounds[r])

    def round_end(r):
        if r < len(rounds):
            distance = rounds[r]
            both = jnp.logical_and(me >= distance, me + distance < n)
            one = jnp.logical_xor(me >= distance, me + distance < n)
            pl.when(both)(lambda: pl.semaphore_wait(tokens.at[r], 2))
            pl.when(one)(lambda: pl.semaphore_wait(tokens.at[r], 1))

    middle, outer, rim = ways

    def plane_copies(out_ref, in_ref, slot, target):
        return tuple(
            copy_to(out_ref.at[pl.ds(0, 8 * count)], in_ref.at[pl.ds(0, 8 * count)], sems, slot, target)
            for _, count, _, _ in (middle, outer)
        )

    near_up = plane_copies(lab_out.at[0, 0], lab_in.at[0, 0], 0, up)
    near_low = plane_copies(lab_out.at[1, 0], lab_in.at[1, 0], 1, low)
    next_up = plane_copies(lab_out.at[0, 1], lab_in.at[0, 1], 2, up)
    next_low = plane_copies(lab_out.at[1, 1], lab_in.at[1, 1], 3, low)
    rhs_up = plane_copies(fine_out.at[0, 0], fine_in.at[0, 0], 4, up)
    rhs_low = plane_copies(fine_out.at[1, 0], fine_in.at[1, 0], 5, low)
    u1_up = plane_copies(fine_out.at[0, 1], fine_in.at[0, 1], 6, up)
    u1_low = plane_copies(fine_out.at[1, 1], fine_in.at[1, 1], 7, low)
    far_up = copy_to(far_out.at[0], far.at[0], sems, 8, up)
    far_low = copy_to(far_out.at[1], far.at[1], sems, 9, low)
    ends_up = copy_to(begin.at[0], ends.at[0], sems, 10, up)
    ends_low = copy_to(begin.at[1], ends.at[1], sems, 11, low)
    u2_up = plane_copies(fine_out.at[0, 2], fine_in.at[0, 2], 12, up)
    u2_low = plane_copies(fine_out.at[1, 2], fine_in.at[1, 2], 13, low)
    vn_up = copy_to(vn.at[1], vn.at[0], sems, 14, up)
    vn_low = copy_to(vn.at[1], vn.at[2], sems, 15, low)
    edge_up = copy_to(part.at[0], edge.at[0], sems, 16, up)
    edge_low = copy_to(part.at[1], edge.at[1], sems, 17, low)

    def send(upward, downward):
        pl.when(has_up)(upward.start)
        pl.when(has_low)(downward.start)

    def receive(upward, downward):
        pl.when(has_low)(upward.wait_recv)
        pl.when(has_up)(downward.wait_recv)

    tile_row = lax.broadcasted_iota(jnp.int32, (8, ny), 0)
    tile_lane = lax.broadcasted_iota(jnp.int32, (8, ny), 1)

    def tile(t):
        return pl.ds(8 * t, 8)

    def inside(t, bound):
        return near_axis(tile_row + 8 * t, tile_lane, nx, ny, bound)

    def half_turn(values):
        return pltpu.roll(values, ny // 2, 1)

    tiles, bound = nx // 8, middle[3]
    outermost = (4, 5, tiles - 6, tiles - 5)
    partners = {4: (0, tiles - 4), 5: (None, tiles - 3), tiles - 6: (None, 2), tiles - 5: (tiles - 1, 3)}
    tail = (2, 3, tiles - 4, tiles - 3)
    rim_pairs = {2: tiles - 2, tiles - 3: 1}

    def place(t):
        return t - 4 if t not in tail else tiles - 8 + tail.index(t)

    def bound_of(t, thin):
        wide = bound if partners.get(t, (0,))[0] is not None else 4 * 1000 * nx * nx
        return jnp.where(thin, outer[3], wide)

    def fold(field, k, out_ref, thin):
        if not middle[2]:
            out_ref[...] = field[k]
            return
        for t in range(2, tiles - 2):
            values = field[k, tile(t)]
            if t in outermost:
                wide, narrow = partners[t]
                other = field[k, tile(narrow)]
                if wide is not None:
                    other = jnp.where(thin, other, field[k, tile(wide)])
                values = jnp.where(inside(t, bound_of(t, thin)), values, half_turn(other))
            elif t in rim_pairs:
                values = jnp.where(inside(t, bound), values, half_turn(field[k, tile(rim_pairs[t])]))
            out_ref[tile(place(t))] = values

    def unfold(in_ref, field, k, thin):
        if not middle[2]:
            field[k] = in_ref[...]
            return
        zero_tile = jnp.zeros((8, ny), field.dtype)
        for t in range(2, tiles - 2):
            values = in_ref[tile(place(t))]
            if t in outermost:
                wide, narrow = partners[t]
                turned = half_turn(values)
                direct = in_ref[tile(place(narrow))]
                if narrow in rim_pairs:
                    field[k, tile(rim_pairs[narrow])] = jnp.where(
                        inside(rim_pairs[narrow], jnp.where(thin, outer[3], bound)), half_turn(direct), zero_tile
                    )
                    direct = jnp.where(inside(narrow, bound), direct, zero_tile)
                field[k, tile(narrow)] = jnp.where(thin, jnp.where(inside(narrow, outer[3]), turned, zero_tile), direct)
                if wide is not None:
                    field[k, tile(wide)] = jnp.where(inside(wide, jnp.where(thin, outer[3], bound)), turned, zero_tile)
                field[k, tile(t)] = jnp.where(inside(t, bound_of(t, thin)), values, zero_tile)
            elif t not in tail:
                field[k, tile(t)] = values

    def each_way(exists, thin, action):
        if rim == n:
            pl.when(exists)(lambda: action(0))
        else:
            pl.when(jnp.logical_and(exists, jnp.logical_not(thin)))(lambda: action(0))
            pl.when(jnp.logical_and(exists, thin))(lambda: action(1))

    thin_up, thin_low = n - 1 - me >= rim, me >= rim
    from_low_thin, from_up_thin = n - me >= rim, me + 1 >= rim

    def send_fine(field, k_up, k_low, outs, upward, downward):
        fold(field, k_up, outs[0], thin_up)
        fold(field, k_low, outs[1], thin_low)
        each_way(has_up, thin_up, lambda way: upward[way].start())
        each_way(has_low, thin_low, lambda way: downward[way].start())

    def receive_fine(ins, field, k_low, k_up, upward, downward):
        each_way(has_low, from_low_thin, lambda way: upward[way].wait_recv())
        each_way(has_up, from_up_thin, lambda way: downward[way].wait_recv())
        unfold(ins[0], field, k_low, from_low_thin)
        unfold(ins[1], field, k_up, from_up_thin)

    def sent_fine(upward, downward):
        each_way(has_up, thin_up, lambda way: upward[way].wait_send())
        each_way(has_low, thin_low, lambda way: downward[way].wait_send())

    round_start(0)
    own_lab.wait()
    send_fine(lab, 5, 2, (lab_out.at[0, 0], lab_out.at[1, 0]), near_up, near_low)
    send_fine(lab, 4, 3, (lab_out.at[0, 1], lab_out.at[1, 1]), next_up, next_low)
    own_rhs.wait()
    send_fine(rhs, 5, 2, (fine_out.at[0, 0], fine_out.at[1, 0]), rhs_up, rhs_low)

    def clear(ref, first, count):
        for k in range(first, first + count):
            ref[k] = jnp.zeros(ref.shape[1:], ref.dtype)

    @pl.when(me == 0)
    def _():
        clear(lab_in.at[0], 0, 2)
        clear(fine_in.at[0], 0, 3)
        clear(edge, 0, 1)
        clear(far, 0, 1)
        clear(ends, 0, 1)
        clear(vn, 0, 1)

    @pl.when(me == n - 1)
    def _():
        clear(lab_in.at[1], 0, 2)
        clear(fine_in.at[1], 0, 3)
        clear(edge, 1, 1)
        clear(far, 1, 1)
        clear(ends, 1, 1)
        clear(vn, 2, 1)

    xs[...] = jnp.zeros(xs.shape, xs.dtype)

    fine_row = lax.broadcasted_iota(jnp.int32, (nx, ny), 0) % 2 == 1
    fine_lane = lax.broadcasted_iota(jnp.int32, (nx, ny), 1) % 2 == 1
    even = lax.broadcasted_iota(jnp.int32, (hx_rows, ny), 1) % 2 == 0

    def select(values, column):
        chosen = jnp.full(values.shape, table[column, 0], jnp.float32)
        for tissue in range(1, LABELS):
            chosen = jnp.where(values == tissue, table[column, tissue], chosen)
        return chosen

    def harmonic(a, b):
        return 2.0 * a * b / (a + b)

    def active(k):
        return (lab[k] > 0).astype(jnp.float32)

    def side_faces(k):
        here = lab[k]
        a = (here > 0).astype(jnp.float32)
        sx, sy = select(here, 0), select(here, 1)
        hx = harmonic(pltpu.roll(sx, 1, 0), sx)
        gx[k] = hx * a * pltpu.roll(a, 1, 0)
        hy = harmonic(pltpu.roll(sy, 1, 1), sy)
        gy[k] = hy * a * pltpu.roll(a, 1, 1)
        return hx + pltpu.roll(hx, nx - 1, 0) + hy + pltpu.roll(hy, ny - 1, 1)

    def face_below(k):
        h = harmonic(select(lab[k - 1], 2), select(lab[k], 2))
        gz[k] = h * active(k - 1) * active(k)
        return h

    def finish(k, faces):
        a = active(k)
        diagonal = a * faces + (1.0 - a)
        dg[k] = diagonal
        idf[k] = OMEGA * a / diagonal

    def over(first, last, body):
        for k in range(first, last):
            body(k)

    def first_sweep(k):
        ua[k] = idf[k] * rhs[k]

    def neighbours(field, k):
        u = field[k]
        cx, cy = gx[k], gy[k]
        total = cx * pltpu.roll(u, 1, 0) + pltpu.roll(cx * u, nx - 1, 0)
        total = total + cy * pltpu.roll(u, 1, 1) + pltpu.roll(cy * u, ny - 1, 1)
        return u, total + gz[k] * field[k - 1] + gz[k + 1] * field[k + 1]

    def sweep(src, dst, shift=0):
        def body(k):
            u, total = neighbours(src, k)
            dst[k - shift] = (1.0 - OMEGA) * u + idf[k] * (rhs[k] + total)

        return body

    def residual(k):
        u, total = neighbours(ub, k)
        return jnp.where(idf[k] > 0.0, rhs[k] - dg[k] * u + total, 0.0)

    second_sweep = sweep(ua, ub)

    load_table.wait()
    h3, h4, h5 = face_below(3), face_below(4), face_below(5)
    finish(3, side_faces(3) + h3 + h4)
    finish(4, side_faces(4) + h4 + h5)
    dg[2] = side_faces(2) + h3
    dg[5] = side_faces(5) + h5
    over(3, 5, first_sweep)

    turn = itertools.count()

    def rows_apart(plane):
        slot = next(turn) % 6
        tmp[slot] = plane
        return tmp[slot, pl.ds(0, hx_rows, 2), :], tmp[slot, pl.ds(1, hx_rows, 2), :]

    def rows_even(plane):
        return rows_apart(plane)[0]

    def rows_sum(plane):
        first, second = rows_apart(plane)
        return first + second

    def lanes_sum(t0, t1):
        return jnp.where(even, t0 + pltpu.roll(t0, ny - 1, 1), t1 + pltpu.roll(t1, 1, 1))

    def lanes_even(t0, t1):
        return jnp.where(even, t0, pltpu.roll(t1, 1, 1))

    def restrict(p0, p1):
        return lanes_sum(rows_sum(p0), rows_sum(p1))

    def inner(k):
        doubled = jnp.where(fine_row, gx[k], 0.0) + jnp.where(fine_lane, gy[k], 0.0)
        if k % 2 == 1:
            doubled = doubled + gz[k]
        return active(k) * dg[k] - 2.0 * doubled

    def to_even(pack):
        return pltpu.roll(pack, ny - 1, 1)

    def to_odd(pack):
        return pltpu.roll(pack, 1, 1)

    def swap(pack):
        return jnp.where(even, to_even(pack), to_odd(pack))

    def of_odd(a, b):
        return jnp.where(even, to_even(a), b)

    def of_even(a, b):
        return jnp.where(even, a, to_odd(b))

    def beside(field, cx, cy):
        total = cx * pltpu.roll(field, 1, 0) + pltpu.roll(cx * field, hx_rows - 1, 0)
        return total + cy * pltpu.roll(field, 2, 1) + pltpu.roll(cy * field, ny - 2, 1)

    def side_sum(cx, cy):
        return cx + pltpu.roll(cx, hx_rows - 1, 0) + cy + pltpu.roll(cy, ny - 2, 1)

    h4_low, h4_up = rows_sum(active(3) * h4), rows_sum(active(4) * h4)
    between = rows_sum(gz[4])
    z_in = lanes_sum(between, between)
    part[0] = jnp.where(even, h4_up + to_even(h4_up), z_in)
    part[1] = jnp.where(even, h4_low + to_even(h4_low), z_in)
    send(edge_up, edge_low)
    send_fine(ua, 4, 3, (fine_out.at[0, 1], fine_out.at[1, 1]), u1_up, u1_low)

    def coarse_pack(k0, k1, k2, k3):
        raw = restrict(inner(k0) + inner(k1), inner(k2) + inner(k3))
        x = lanes_sum(rows_even(gx[k0] + gx[k1]), rows_even(gx[k2] + gx[k3]))
        y = lanes_even(rows_sum(gy[k0] + gy[k1]), rows_sum(gy[k2] + gy[k3]))
        return raw, x, y

    round_end(0)
    round_start(1)
    round_end(1)
    round_start(2)
    receive_fine((lab_in.at[0, 0], lab_in.at[1, 0]), lab, 1, 6, near_up, near_low)
    h2, h6 = face_below(2), face_below(6)
    tmp[6] = h2
    tmp[7] = h6
    finish(2, dg[2] + h2)
    finish(5, dg[5] + h6)
    over(0, 2, lambda k: first_sweep(2 + 3 * k))
    over(3, 5, second_sweep)
    raw, coarse_x, coarse_y = coarse_pack(2, 3, 4, 5)
    side = side_sum(coarse_x, coarse_y)
    active1 = jnp.where(raw > 0.0, 1.0, 0.0)
    diag1 = raw + (1.0 - active1)
    weight = OMEGA * active1 / diag1
    z_out = restrict(gz[2], gz[6])
    own_part, out_part, in_part = (1.0 - OMEGA) * active1 + weight * side, weight * z_out, weight * z_in
    spread[...] = in_part
    in_first, in_second = spread[pl.ds(0, hx_rows // 2, 2), :], spread[pl.ds(1, hx_rows // 2, 2), :]
    even_half = even[: hx_rows // 2]
    far_out[0, pl.ds(0, hx_rows)] = of_even(own_part, out_part)
    far_out[0, pl.ds(hx_rows, hx_rows // 2)] = jnp.where(even_half, in_first, to_odd(in_second))
    far_out[1, pl.ds(0, hx_rows)] = of_odd(own_part, out_part)
    far_out[1, pl.ds(hx_rows, hx_rows // 2)] = jnp.where(even_half, to_even(in_first), in_second)
    send(far_up, far_low)

    sub = lax.broadcasted_iota(jnp.int32, (8, ny), 0)
    sub_even = lax.broadcasted_iota(jnp.int32, (8, ny), 1) % 2 == 0

    def row_sum(pack):
        return jnp.sum(pack, axis=0, keepdims=True)

    def gather(out, everyone, slot, rows_of):
        tile = jnp.zeros((8, ny), jnp.float32)
        for row, values in enumerate(rows_of):
            tile = jnp.where(sub == row, values, tile)
        lower = jnp.sum(jnp.where(sub_even, tile, 0.0), axis=1, keepdims=True)
        upper = jnp.sum(jnp.where(sub_even, 0.0, tile), axis=1, keepdims=True)
        tile = jnp.where(sub_even, lower, upper)
        out[...] = tile
        everyone[me] = tile
        rows = pl.ds(0, len(rows_of))

        def one(step, carry):
            pltpu.make_async_remote_copy(
                src_ref=out.at[rows],
                dst_ref=everyone.at[me, rows],
                send_sem=gather_sem.at[0, slot],
                recv_sem=gather_sem.at[1, slot],
                device_id={"slab": lax.rem(me + step, n)},
                device_id_type=MESH,
            ).start()
            return carry

        lax.fori_loop(1, n, one, 0)

    def gather_wait(everyone, side, slot, count):
        rest = everyone.at[pl.ds(0, n - 1), pl.ds(0, count)]
        pltpu.make_async_copy(rest, rest, gather_sem.at[side, slot]).wait()

    line_sums = (row_sum(raw - 2.0 * (coarse_x + coarse_y)), row_sum(jnp.where(even, z_out, z_in)))

    round_end(2)
    round_start(3)
    receive_fine((lab_in.at[0, 1], lab_in.at[1, 1]), lab, 0, 7, next_up, next_low)
    h1, h7 = face_below(1), face_below(7)
    finish(1, side_faces(1) + h1 + tmp[6])
    finish(6, side_faces(6) + h7 + tmp[7])
    dg[0] = side_faces(0) + h1
    dg[7] = side_faces(7) + h7
    receive_fine((fine_in.at[0, 0], fine_in.at[1, 0]), rhs, 1, 6, rhs_up, rhs_low)
    over(0, 2, lambda k: first_sweep(1 + 5 * k))
    over(0, 2, lambda k: second_sweep(2 + 3 * k))
    r3, r4 = residual(3), residual(4)
    edge_raw, edge_x, edge_y = coarse_pack(0, 1, 6, 7)
    edge_side = side_sum(edge_x, edge_y)

    def split(both):
        below, above = both
        return jnp.where(even, below, to_odd(above)), jnp.where(even, to_even(below), above)

    receive(edge_up, edge_low)
    edge_face, edge_in = split((edge[0], edge[1]))
    edge_diag = edge_raw + edge_face
    edge_active = edge_diag > 0.0
    edge_weight = jnp.where(edge_active, OMEGA / jnp.where(edge_active, edge_diag, 1.0), 0.0)
    own_1 = weight * (diag1 - side)
    edge_own_1, edge_out_1, edge_in_1 = edge_weight * (edge_diag - edge_side), edge_weight * z_out, edge_weight * edge_in
    to_out2 = out_part * edge_in_1
    to_out1 = (2.0 - OMEGA) * out_part + weight * beside(out_part, coarse_x, coarse_y) - out_part * edge_own_1
    to_own = 1.0 + (OMEGA - 2.0) * own_1 - weight * beside(own_1, coarse_x, coarse_y) + out_part * edge_out_1 + in_part * swap(in_part)
    to_in1 = (2.0 - OMEGA) * in_part + weight * beside(in_part, coarse_x, coarse_y) - in_part * swap(own_1)
    to_in2 = in_part * swap(out_part)
    edge_own_part = jnp.where(edge_active, 1.0 - OMEGA, 0.0) + edge_weight * edge_side

    for r in range(3, len(rounds)):
        round_end(r)
        round_start(r + 1)
    gather(line_out, line_all, 0, line_sums)

    def partial_sweep(k, beside_k, face):
        u, cx, cy = ua[k], gx[k], gy[k]
        total = cx * pltpu.roll(u, 1, 0) + pltpu.roll(cx * u, nx - 1, 0)
        total = total + cy * pltpu.roll(u, 1, 1) + pltpu.roll(cy * u, ny - 1, 1)
        ub[k] = (1.0 - OMEGA) * u + idf[k] * (rhs[k] + total + gz[face] * ua[beside_k])

    partial_sweep(1, 2, 2)
    partial_sweep(6, 5, 6)
    b1_part = restrict(residual(2) + r3, r4 + residual(5))
    tmp[6] = idf[1] * gz[1]
    tmp[7] = idf[6] * gz[7]
    pro[0] = gz[2] * tmp[6]
    pro[1] = gz[6] * tmp[7]

    receive_fine((fine_in.at[0, 1], fine_in.at[1, 1]), ua, 0, 7, u1_up, u1_low)
    b1 = b1_part + restrict(pro[0] * ua[0], pro[1] * ua[7])

    row_even = even[:1]

    def row_swap(row):
        return jnp.where(row_even, to_even(row), to_odd(row))

    v1 = weight * b1
    begin[0] = jnp.where(even, to_even(b1), to_odd(v1))
    begin[1] = jnp.where(even, b1, v1)
    send(ends_up, ends_low)
    ub[1] = ub[1] + tmp[6] * ua[0]
    ub[6] = ub[6] + tmp[7] * ua[7]
    gather(
        row_out, row_all, 1,
        (
            row_sum(to_own * b1) + row_swap(row_sum(to_in1 * b1)),
            row_swap(row_sum(to_out1 * b1)) + row_sum(to_in2 * b1),
            row_sum(to_out2 * b1),
        ),
    )

    def own_sweep(own, beyond):
        total = beside(own, coarse_x, coarse_y) + z_out * beyond + z_in * swap(own)
        return (1.0 - OMEGA) * own + weight * (b1 + total)

    def edge_sweep(own, beyond, further):
        total = beside(beyond, edge_x, edge_y) + z_out * own + edge_in * further
        return (1.0 - OMEGA) * beyond + edge_weight * (edge_b1 + total)

    receive(ends_up, ends_low)
    edge_b1, far_v1 = split((ends[0], ends[1]))
    edge_v1 = edge_weight * edge_b1
    v2, edge_v2 = own_sweep(v1, edge_v1), edge_sweep(v1, edge_v1, far_v1)
    v3 = own_sweep(v2, edge_v2)
    vn[1] = v3
    send(vn_up, vn_low)
    send_fine(ub, 4, 3, (fine_out.at[0, 2], fine_out.at[1, 2]), u2_up, u2_low)

    receive(far_up, far_low)
    far_own_part, far_out_part = split((far[0, pl.ds(0, hx_rows)], far[1, pl.ds(0, hx_rows)]))
    below, above = far[0, pl.ds(hx_rows, hx_rows // 2)], far[1, pl.ds(hx_rows, hx_rows // 2)]
    spread[pl.ds(0, hx_rows // 2, 2), :] = jnp.where(even_half, below, to_odd(above))
    spread[pl.ds(1, hx_rows // 2, 2), :] = jnp.where(even_half, to_even(below), above)

    gather_wait(line_all, 1, 0, 2)

    line_even = lax.broadcasted_iota(jnp.int32, (n, ny), 1) % 2 == 0

    def line_row(everyone, row):
        return everyone.reshape(n * 8, ny)[pl.ds(row, n, 8), :]

    def apart(both):
        lower = jnp.where(line_even, both, pltpu.roll(both, 1, 1))
        return lower, jnp.where(line_even, pltpu.roll(both, ny - 1, 1), both)

    (de, do), (fe, fo) = apart(line_row(line_all, 0)), apart(line_row(line_all, 1))

    def back(x, s):
        return pltpu.roll(x, s % n, 0)

    def ahead(x, s):
        return pltpu.roll(x, (n - s) % n, 0)

    inv_odd = 1.0 / do
    to_low = fe * back(inv_odd, 1)
    to_up = fo * inv_odd
    fe_next = ahead(fe, 1)
    diag = de - fe * to_low - fo * to_up
    lower = -to_low * back(fo, 1)
    upper = -to_up * fe_next
    steps = []
    shift = 1
    while shift < n:
        alpha, gamma = lower / back(diag, shift), upper / ahead(diag, shift)
        steps.append((shift, alpha, gamma))
        diag = diag - alpha * back(upper, shift) - gamma * ahead(lower, shift)
        lower, upper = -alpha * back(lower, shift), -gamma * ahead(upper, shift)
        shift *= 2
    inv_diag = 1.0 / diag

    gather_wait(row_all, 1, 1, 3)
    one, two = line_row(row_all, 1), line_row(row_all, 2)
    sums = line_row(row_all, 0) + jnp.where(line_even, back(one, 1) + ahead(two, 1), ahead(one, 1) + back(two, 1))
    be, bo = apart(sums)
    reduced = be + to_low * back(bo, 1) + to_up * bo
    for shift, alpha, gamma in steps:
        reduced = reduced - alpha * back(reduced, shift) - gamma * ahead(reduced, shift)
    e_even = reduced * inv_diag
    e_odd = (bo + fo * e_even + fe_next * ahead(e_even, 1)) * inv_odd
    xs[0, pl.ds(8, n), :] = jnp.where(line_even, e_even, e_odd)
    xs[1, pl.ds(8, n), :] = jnp.where(line_even, e_odd, e_even)

    def line(side, distance):
        return jnp.broadcast_to(xs[side, pl.ds(me + 8 + distance, 1), :], (hx_rows, ny))

    def outward(side, distance):
        return jnp.where(even, line(side, -distance), line(side, distance))

    e_own, e_in = line(0, 0), line(1, 0)
    e_out, e_out2, e_out3 = outward(1, 1), outward(0, 1), outward(1, 2)
    receive(vn_up, vn_low)
    below, above = vn[0], vn[2]
    w2 = v3 + own_part * e_own + out_part * e_out + in_part * e_in
    edge_w2 = jnp.where(even, to_even(below), to_odd(above))
    edge_w2 = edge_w2 + edge_own_part * e_out + edge_out_1 * e_own + edge_in_1 * e_out2
    far_w2 = jnp.where(even, below, above) + far_own_part * e_out2 + spread[...] * e_out + far_out_part * e_out3
    w3, edge_w3 = own_sweep(w2, edge_w2), edge_sweep(w2, edge_w2, far_w2)

    def prolong(slot, plane):
        pro[slot, pl.ds(0, hx_rows, 2), :] = plane
        pro[slot, pl.ds(1, hx_rows, 2), :] = plane

    def lower_plane(pack):
        return jnp.where(even, pack, pltpu.roll(pack, 1, 1))

    def upper_plane(pack):
        return jnp.where(even, pltpu.roll(pack, ny - 1, 1), pack)

    prolong(0, lower_plane(edge_w3))
    prolong(1, lower_plane(w3))
    prolong(2, upper_plane(w3))
    prolong(3, upper_plane(edge_w3))

    receive_fine((fine_in.at[0, 2], fine_in.at[1, 2]), ub, 0, 7, u2_up, u2_low)

    def correct(k):
        ua[k] = ub[k] + jnp.where(lab[k] > 0, pro[k // 2], 0.0)

    over(0, 8, correct)

    over(1, 7, sweep(ua, tmp))
    over(2, 6, sweep(tmp, out.at[0], 2))

    for upward, downward in ((far_up, far_low), (ends_up, ends_low), (vn_up, vn_low), (edge_up, edge_low)):
        pl.when(has_up)(upward.wait_send)
        pl.when(has_low)(downward.wait_send)
    for upward, downward in ((near_up, near_low), (next_up, next_low), (rhs_up, rhs_low), (u1_up, u1_low), (u2_up, u2_low)):
        sent_fine(upward, downward)
    gather_wait(line_all, 0, 0, 2)
    gather_wait(row_all, 0, 1, 3)


def on_device(n, rhs, labels, sigma_table):
    planes, nx, ny = labels.shape
    ways = folds(n, nx, ny)
    kept = 8 * ways[0][1]
    fine = lambda count: pltpu.VMEM((count, nx, ny), jnp.float32)
    packs = lambda *counts: pltpu.VMEM((*counts, nx // 2, ny), jnp.float32)
    thirds = lambda *counts: pltpu.VMEM((*counts, nx // 2 + nx // 4, ny), jnp.float32)
    tiles = lambda *counts: pltpu.VMEM((*counts, 8, ny), jnp.float32)
    return pl.pallas_call(
        functools.partial(kernel, n, ways),
        out_shape=pltpu.VMEM(rhs.shape, jnp.float32),
        in_specs=[
            pl.BlockSpec(memory_space=pl.ANY),
            pl.BlockSpec(memory_space=pl.ANY),
            pl.BlockSpec(memory_space=pl.ANY),
        ],
        out_specs=pl.BlockSpec(memory_space=pltpu.VMEM),
        scratch_shapes=[
            pltpu.VMEM((8, nx, ny), jnp.int32),
            fine(8), fine(8), fine(8), fine(8), fine(8), fine(8), fine(8), fine(8),
            fine(8), fine(4),
            pltpu.VMEM((2, 2, kept, ny), jnp.int32), pltpu.VMEM((2, 3, kept, ny), jnp.float32),
            pltpu.VMEM((2, 2, kept, ny), jnp.int32), pltpu.VMEM((2, 3, kept, ny), jnp.float32),
            packs(2), packs(2), thirds(2), thirds(2), packs(2), packs(2), packs(3), packs(),
            tiles(), tiles(n), tiles(), tiles(n),
            pltpu.VMEM((2, n + 16, ny), jnp.float32),
            pltpu.SMEM((3, LABELS), jnp.float32),
            pltpu.SemaphoreType.DMA((3,)),
            pltpu.SemaphoreType.DMA((2, 18)),
            pltpu.SemaphoreType.DMA((2, 2)),
            pltpu.SemaphoreType.REGULAR((n.bit_length(),)),
        ],
        compiler_params=pltpu.CompilerParams(collective_id=0, has_side_effects=True),
    )(rhs, labels, sigma_table.T)


def solution(mesh):
    placed = (P("groups", "slab", None, None), P("slab", "groups", None), P())
    return jax.shard_map(
        functools.partial(on_device, mesh.shape["slab"]),
        mesh=mesh,
        in_specs=placed,
        out_specs=P("groups", "slab", None, None),
        check_vma=False,
    )
```

```python
import functools
import itertools

import jax
import jax.numpy as jnp
import numpy as np
from jax import lax
from jax.experimental import pallas as pl
from jax.experimental.pallas import tpu as pltpu
from jax.sharding import PartitionSpec as P

OMEGA = 0.8
LABELS = 5
MESH = pl.DeviceIdType.MESH
REACH = 4


def copy_to(src, dst, sems, slot, target):
    return pltpu.make_async_remote_copy(
        src_ref=src,
        dst_ref=dst,
        send_sem=sems.at[0, slot],
        recv_sem=sems.at[1, slot],
        device_id={"slab": target},
        device_id_type=MESH,
    )


def near_axis(row, lane, nx, ny, bound):
    across, along = 2 * row + 1 - nx, 2 * lane + 1 - ny
    return (across * across + along * along) * 1000 <= bound


def folds(n, nx, ny):
    tiles = nx // 8
    whole = (0, tiles, (), 4 * 1000 * nx * nx)
    if nx != ny or nx < 128 or nx % 8:
        return whole, whole, n

    def fits(pairs, bound, first, count):
        inside = near_axis(np.arange(nx)[:, None], np.arange(ny)[None], nx, ny, bound).reshape(tiles, 8, ny)
        sent = set(range(first, first + count)) | {folded for _, folded in pairs}
        lost = any(inside[t].any() for t in range(tiles) if t not in sent)
        return not lost and not any((inside[kept] & np.roll(inside[folded], ny // 2, 1)).any() for kept, folded in pairs)

    pairs = ((2, tiles - 2), (4, 0), (tiles - 5, tiles - 1), (tiles - 3, 1))
    middle = (2, tiles - 4, pairs, 813 * nx * nx)
    if not fits(pairs, middle[3], 2, tiles - 4):
        return whole, whole, n
    pairs = ((4, tiles - 4), (tiles - 5, 3), (5, tiles - 3), (tiles - 6, 2))
    outer, rim = middle, n
    for slab in range(n - 1, n // 2, -1):
        away = (4 * slab + 0.5 - 2 * n) / (0.55 * 4 * n)
        bound = int((0.813 - 0.81 * away * away) * 1000 * nx * nx)
        if not fits(pairs, bound, 4, tiles - 8):
            break
        outer, rim = (4, tiles - 8, pairs, bound), slab
    return middle, outer, rim


def kernel(
    n, ways, rhs_hbm, lab_hbm, table_hbm, out,
    lab, rhs, gx, gy, gz, idf, dg, ua, ub, tmp, pro,
    lab_out, fine_out, lab_in, fine_in, part, edge, far_out, far, ends, begin, vn, spread, line_out, line_all, row_out, row_all, xs, table,
    load_sem, sems, gather_sem, tokens,
):
    me = lax.axis_index("slab")
    nx, ny = lab.shape[1:]
    hx_rows = nx // 2
    has_low, has_up = me > 0, me < n - 1

    load_table = pltpu.make_async_copy(table_hbm, table, load_sem.at[2])
    load_table.start()
    own_lab = pltpu.make_async_copy(lab_hbm, lab.at[pl.ds(2, 4)], load_sem.at[0])
    own_rhs = pltpu.make_async_copy(rhs_hbm.at[0], rhs.at[pl.ds(2, 4)], load_sem.at[1])
    own_lab.start()
    own_rhs.start()
    barrier = pltpu.get_barrier_semaphore()

    up, low = lax.rem(me + 1, n), lax.rem(me + n - 1, n)

    def signal(sem, distance):
        for near, other in ((me >= distance, me - distance), (me + distance < n, me + distance)):

            @pl.when(near)
            def _():
                pl.semaphore_signal(sem, inc=1, device_id={"slab": other}, device_id_type=MESH)

    for distance in range(1, min(REACH, n - 1) + 1):
        signal(barrier, distance)
    pl.semaphore_wait(barrier, jnp.minimum(me, REACH) + jnp.minimum(n - 1 - me, REACH))

    rounds = []
    while REACH * 2 ** len(rounds) < n - 1:
        rounds.append(REACH * 2 ** len(rounds))

    def round_start(r):
        if r < len(rounds):
            signal(tokens.at[r], rounds[r])

    def round_end(r):
        if r < len(rounds):
            distance = rounds[r]
            both = jnp.logical_and(me >= distance, me + distance < n)
            one = jnp.logical_xor(me >= distance, me + distance < n)
            pl.when(both)(lambda: pl.semaphore_wait(tokens.at[r], 2))
            pl.when(one)(lambda: pl.semaphore_wait(tokens.at[r], 1))

    middle, outer, rim = ways

    def plane_copies(out_ref, in_ref, slot, target):
        return tuple(
            copy_to(out_ref.at[pl.ds(0, 8 * count)], in_ref.at[pl.ds(0, 8 * count)], sems, slot, target)
            for _, count, _, _ in (middle, outer)
        )

    near_up = plane_copies(lab_out.at[0, 0], lab_in.at[0, 0], 0, up)
    near_low = plane_copies(lab_out.at[1, 0], lab_in.at[1, 0], 1, low)
    next_up = plane_copies(lab_out.at[0, 1], lab_in.at[0, 1], 2, up)
    next_low = plane_copies(lab_out.at[1, 1], lab_in.at[1, 1], 3, low)
    rhs_up = plane_copies(fine_out.at[0, 0], fine_in.at[0, 0], 4, up)
    rhs_low = plane_copies(fine_out.at[1, 0], fine_in.at[1, 0], 5, low)
    u1_up = plane_copies(fine_out.at[0, 1], fine_in.at[0, 1], 6, up)
    u1_low = plane_copies(fine_out.at[1, 1], fine_in.at[1, 1], 7, low)
    far_up = copy_to(far_out.at[0], far.at[0], sems, 8, up)
    far_low = copy_to(far_out.at[1], far.at[1], sems, 9, low)
    ends_up = copy_to(begin.at[0], ends.at[0], sems, 10, up)
    ends_low = copy_to(begin.at[1], ends.at[1], sems, 11, low)
    u2_up = plane_copies(fine_out.at[0, 2], fine_in.at[0, 2], 12, up)
    u2_low = plane_copies(fine_out.at[1, 2], fine_in.at[1, 2], 13, low)
    vn_up = copy_to(vn.at[1], vn.at[0], sems, 14, up)
    vn_low = copy_to(vn.at[1], vn.at[2], sems, 15, low)
    edge_up = copy_to(part.at[0], edge.at[0], sems, 16, up)
    edge_low = copy_to(part.at[1], edge.at[1], sems, 17, low)

    def send(upward, downward):
        pl.when(has_up)(upward.start)
        pl.when(has_low)(downward.start)

    def receive(upward, downward):
        pl.when(has_low)(upward.wait_recv)
        pl.when(has_up)(downward.wait_recv)

    tile_row = lax.broadcasted_iota(jnp.int32, (8, ny), 0)
    tile_lane = lax.broadcasted_iota(jnp.int32, (8, ny), 1)

    def tile(t):
        return pl.ds(8 * t, 8)

    def inside(t, bound):
        return near_axis(tile_row + 8 * t, tile_lane, nx, ny, bound)

    def half_turn(values):
        return pltpu.roll(values, ny // 2, 1)

    tiles, bound = nx // 8, middle[3]
    outermost = (4, 5, tiles - 6, tiles - 5)
    partners = {4: (0, tiles - 4), 5: (None, tiles - 3), tiles - 6: (None, 2), tiles - 5: (tiles - 1, 3)}
    tail = (2, 3, tiles - 4, tiles - 3)
    rim_pairs = {2: tiles - 2, tiles - 3: 1}

    def place(t):
        return t - 4 if t not in tail else tiles - 8 + tail.index(t)

    def bound_of(t, thin):
        wide = bound if partners.get(t, (0,))[0] is not None else 4 * 1000 * nx * nx
        return jnp.where(thin, outer[3], wide)

    def fold(field, k, out_ref, thin):
        if not middle[2]:
            out_ref[...] = field[k]
            return
        for t in range(2, tiles - 2):
            values = field[k, tile(t)]
            if t in outermost:
                wide, narrow = partners[t]
                other = field[k, tile(narrow)]
                if wide is not None:
                    other = jnp.where(thin, other, field[k, tile(wide)])
                values = jnp.where(inside(t, bound_of(t, thin)), values, half_turn(other))
            elif t in rim_pairs:
                values = jnp.where(inside(t, bound), values, half_turn(field[k, tile(rim_pairs[t])]))
            out_ref[tile(place(t))] = values

    def unfold(in_ref, field, k, thin):
        if not middle[2]:
            field[k] = in_ref[...]
            return
        zero_tile = jnp.zeros((8, ny), field.dtype)
        for t in range(2, tiles - 2):
            values = in_ref[tile(place(t))]
            if t in outermost:
                wide, narrow = partners[t]
                turned = half_turn(values)
                direct = in_ref[tile(place(narrow))]
                if narrow in rim_pairs:
                    field[k, tile(rim_pairs[narrow])] = jnp.where(
                        inside(rim_pairs[narrow], jnp.where(thin, outer[3], bound)), half_turn(direct), zero_tile
                    )
                    direct = jnp.where(inside(narrow, bound), direct, zero_tile)
                field[k, tile(narrow)] = jnp.where(thin, jnp.where(inside(narrow, outer[3]), turned, zero_tile), direct)
                if wide is not None:
                    field[k, tile(wide)] = jnp.where(inside(wide, jnp.where(thin, outer[3], bound)), turned, zero_tile)
                field[k, tile(t)] = jnp.where(inside(t, bound_of(t, thin)), values, zero_tile)
            elif t not in tail:
                field[k, tile(t)] = values

    def each_way(exists, thin, action):
        if rim == n:
            pl.when(exists)(lambda: action(0))
        else:
            pl.when(jnp.logical_and(exists, jnp.logical_not(thin)))(lambda: action(0))
            pl.when(jnp.logical_and(exists, thin))(lambda: action(1))

    thin_up, thin_low = n - 1 - me >= rim, me >= rim
    from_low_thin, from_up_thin = n - me >= rim, me + 1 >= rim

    def send_fine(field, k_up, k_low, outs, upward, downward):
        fold(field, k_up, outs[0], thin_up)
        fold(field, k_low, outs[1], thin_low)
        each_way(has_up, thin_up, lambda way: upward[way].start())
        each_way(has_low, thin_low, lambda way: downward[way].start())

    def receive_fine(ins, field, k_low, k_up, upward, downward):
        each_way(has_low, from_low_thin, lambda way: upward[way].wait_recv())
        each_way(has_up, from_up_thin, lambda way: downward[way].wait_recv())
        unfold(ins[0], field, k_low, from_low_thin)
        unfold(ins[1], field, k_up, from_up_thin)

    def sent_fine(upward, downward):
        each_way(has_up, thin_up, lambda way: upward[way].wait_send())
        each_way(has_low, thin_low, lambda way: downward[way].wait_send())

    round_start(0)
    own_lab.wait()
    send_fine(lab, 5, 2, (lab_out.at[0, 0], lab_out.at[1, 0]), near_up, near_low)
    send_fine(lab, 4, 3, (lab_out.at[0, 1], lab_out.at[1, 1]), next_up, next_low)
    own_rhs.wait()
    send_fine(rhs, 5, 2, (fine_out.at[0, 0], fine_out.at[1, 0]), rhs_up, rhs_low)

    def clear(ref, first, count):
        for k in range(first, first + count):
            ref[k] = jnp.zeros(ref.shape[1:], ref.dtype)

    @pl.when(me == 0)
    def _():
        clear(lab_in.at[0], 0, 2)
        clear(fine_in.at[0], 0, 3)
        clear(edge, 0, 1)
        clear(far, 0, 1)
        clear(ends, 0, 1)
        clear(vn, 0, 1)

    @pl.when(me == n - 1)
    def _():
        clear(lab_in.at[1], 0, 2)
        clear(fine_in.at[1], 0, 3)
        clear(edge, 1, 1)
        clear(far, 1, 1)
        clear(ends, 1, 1)
        clear(vn, 2, 1)

    xs[...] = jnp.zeros(xs.shape, xs.dtype)

    fine_row = lax.broadcasted_iota(jnp.int32, (nx, ny), 0) % 2 == 1
    fine_lane = lax.broadcasted_iota(jnp.int32, (nx, ny), 1) % 2 == 1
    even = lax.broadcasted_iota(jnp.int32, (hx_rows, ny), 1) % 2 == 0

    def select(values, column):
        chosen = jnp.full(values.shape, table[column, 0], jnp.float32)
        for tissue in range(1, LABELS):
            chosen = jnp.where(values == tissue, table[column, tissue], chosen)
        return chosen

    def harmonic(a, b):
        return 2.0 * a * b / (a + b)

    def active(k):
        return (lab[k] > 0).astype(jnp.float32)

    def side_faces(k):
        here = lab[k]
        a = (here > 0).astype(jnp.float32)
        sx, sy = select(here, 0), select(here, 1)
        hx = harmonic(pltpu.roll(sx, 1, 0), sx)
        gx[k] = hx * a * pltpu.roll(a, 1, 0)
        hy = harmonic(pltpu.roll(sy, 1, 1), sy)
        gy[k] = hy * a * pltpu.roll(a, 1, 1)
        return hx + pltpu.roll(hx, nx - 1, 0) + hy + pltpu.roll(hy, ny - 1, 1)

    def face_below(k):
        h = harmonic(select(lab[k - 1], 2), select(lab[k], 2))
        gz[k] = h * active(k - 1) * active(k)
        return h

    def finish(k, faces):
        a = active(k)
        diagonal = a * faces + (1.0 - a)
        dg[k] = diagonal
        idf[k] = OMEGA * a / diagonal

    def over(first, last, body):
        for k in range(first, last):
            body(k)

    def first_sweep(k):
        ua[k] = idf[k] * rhs[k]

    def neighbours(field, k):
        u = field[k]
        cx, cy = gx[k], gy[k]
        total = cx * pltpu.roll(u, 1, 0) + pltpu.roll(cx * u, nx - 1, 0)
        total = total + cy * pltpu.roll(u, 1, 1) + pltpu.roll(cy * u, ny - 1, 1)
        return u, total + gz[k] * field[k - 1] + gz[k + 1] * field[k + 1]

    def sweep(src, dst, shift=0):
        def body(k):
            u, total = neighbours(src, k)
            dst[k - shift] = (1.0 - OMEGA) * u + idf[k] * (rhs[k] + total)

        return body

    def residual(k):
        u, total = neighbours(ub, k)
        return jnp.where(idf[k] > 0.0, rhs[k] - dg[k] * u + total, 0.0)

    second_sweep = sweep(ua, ub)

    load_table.wait()
    h3, h4, h5 = face_below(3), face_below(4), face_below(5)
    finish(3, side_faces(3) + h3 + h4)
    finish(4, side_faces(4) + h4 + h5)
    dg[2] = side_faces(2) + h3
    dg[5] = side_faces(5) + h5
    over(3, 5, first_sweep)

    turn = itertools.count()

    def rows_apart(plane):
        slot = next(turn) % 6
        tmp[slot] = plane
        return tmp[slot, pl.ds(0, hx_rows, 2), :], tmp[slot, pl.ds(1, hx_rows, 2), :]

    def rows_even(plane):
        return rows_apart(plane)[0]

    def rows_sum(plane):
        first, second = rows_apart(plane)
        return first + second

    def lanes_sum(t0, t1):
        return jnp.where(even, t0 + pltpu.roll(t0, ny - 1, 1), t1 + pltpu.roll(t1, 1, 1))

    def lanes_even(t0, t1):
        return jnp.where(even, t0, pltpu.roll(t1, 1, 1))

    def restrict(p0, p1):
        return lanes_sum(rows_sum(p0), rows_sum(p1))

    def inner(k):
        doubled = jnp.where(fine_row, gx[k], 0.0) + jnp.where(fine_lane, gy[k], 0.0)
        if k % 2 == 1:
            doubled = doubled + gz[k]
        return active(k) * dg[k] - 2.0 * doubled

    def to_even(pack):
        return pltpu.roll(pack, ny - 1, 1)

    def to_odd(pack):
        return pltpu.roll(pack, 1, 1)

    def swap(pack):
        return jnp.where(even, to_even(pack), to_odd(pack))

    def of_odd(a, b):
        return jnp.where(even, to_even(a), b)

    def of_even(a, b):
        return jnp.where(even, a, to_odd(b))

    def beside(field, cx, cy):
        total = cx * pltpu.roll(field, 1, 0) + pltpu.roll(cx * field, hx_rows - 1, 0)
        return total + cy * pltpu.roll(field, 2, 1) + pltpu.roll(cy * field, ny - 2, 1)

    def side_sum(cx, cy):
        return cx + pltpu.roll(cx, hx_rows - 1, 0) + cy + pltpu.roll(cy, ny - 2, 1)

    h4_low, h4_up = rows_sum(active(3) * h4), rows_sum(active(4) * h4)
    between = rows_sum(gz[4])
    z_in = lanes_sum(between, between)
    part[0] = jnp.where(even, h4_up + to_even(h4_up), z_in)
    part[1] = jnp.where(even, h4_low + to_even(h4_low), z_in)
    send(edge_up, edge_low)
    send_fine(ua, 4, 3, (fine_out.at[0, 1], fine_out.at[1, 1]), u1_up, u1_low)

    def coarse_pack(k0, k1, k2, k3):
        raw = restrict(inner(k0) + inner(k1), inner(k2) + inner(k3))
        x = lanes_sum(rows_even(gx[k0] + gx[k1]), rows_even(gx[k2] + gx[k3]))
        y = lanes_even(rows_sum(gy[k0] + gy[k1]), rows_sum(gy[k2] + gy[k3]))
        return raw, x, y

    round_end(0)
    round_start(1)
    round_end(1)
    round_start(2)
    receive_fine((lab_in.at[0, 0], lab_in.at[1, 0]), lab, 1, 6, near_up, near_low)
    h2, h6 = face_below(2), face_below(6)
    tmp[6] = h2
    tmp[7] = h6
    finish(2, dg[2] + h2)
    finish(5, dg[5] + h6)
    over(0, 2, lambda k: first_sweep(2 + 3 * k))
    over(3, 5, second_sweep)
    raw, coarse_x, coarse_y = coarse_pack(2, 3, 4, 5)
    side = side_sum(coarse_x, coarse_y)
    active1 = jnp.where(raw > 0.0, 1.0, 0.0)
    diag1 = raw + (1.0 - active1)
    weight = OMEGA * active1 / diag1
    z_out = restrict(gz[2], gz[6])
    own_part, out_part, in_part = (1.0 - OMEGA) * active1 + weight * side, weight * z_out, weight * z_in
    spread[...] = in_part
    in_first, in_second = spread[pl.ds(0, hx_rows // 2, 2), :], spread[pl.ds(1, hx_rows // 2, 2), :]
    even_half = even[: hx_rows // 2]
    far_out[0, pl.ds(0, hx_rows)] = of_even(own_part, out_part)
    far_out[0, pl.ds(hx_rows, hx_rows // 2)] = jnp.where(even_half, in_first, to_odd(in_second))
    far_out[1, pl.ds(0, hx_rows)] = of_odd(own_part, out_part)
    far_out[1, pl.ds(hx_rows, hx_rows // 2)] = jnp.where(even_half, to_even(in_first), in_second)

    sub = lax.broadcasted_iota(jnp.int32, (8, ny), 0)
    sub_even = lax.broadcasted_iota(jnp.int32, (8, ny), 1) % 2 == 0

    def row_sum(pack):
        return jnp.sum(pack, axis=0, keepdims=True)

    def gather(out, everyone, slot, rows_of):
        tile = jnp.zeros((8, ny), jnp.float32)
        for row, values in enumerate(rows_of):
            tile = jnp.where(sub == row, values, tile)
        lower = jnp.sum(jnp.where(sub_even, tile, 0.0), axis=1, keepdims=True)
        upper = jnp.sum(jnp.where(sub_even, 0.0, tile), axis=1, keepdims=True)
        tile = jnp.where(sub_even, lower, upper)
        out[...] = tile
        everyone[me] = tile
        rows = pl.ds(0, len(rows_of))

        def one(step, carry):
            pltpu.make_async_remote_copy(
                src_ref=out.at[rows],
                dst_ref=everyone.at[me, rows],
                send_sem=gather_sem.at[0, slot],
                recv_sem=gather_sem.at[1, slot],
                device_id={"slab": lax.rem(me + step, n)},
                device_id_type=MESH,
            ).start()
            return carry

        lax.fori_loop(1, n, one, 0)

    def gather_wait(everyone, side, slot, count):
        rest = everyone.at[pl.ds(0, n - 1), pl.ds(0, count)]
        pltpu.make_async_copy(rest, rest, gather_sem.at[side, slot]).wait()

    line_sums = (row_sum(raw - 2.0 * (coarse_x + coarse_y)), row_sum(jnp.where(even, z_out, z_in)))

    round_end(2)
    round_start(3)
    receive_fine((lab_in.at[0, 1], lab_in.at[1, 1]), lab, 0, 7, next_up, next_low)
    h1, h7 = face_below(1), face_below(7)
    finish(1, side_faces(1) + h1 + tmp[6])
    finish(6, side_faces(6) + h7 + tmp[7])
    dg[0] = side_faces(0) + h1
    dg[7] = side_faces(7) + h7
    receive_fine((fine_in.at[0, 0], fine_in.at[1, 0]), rhs, 1, 6, rhs_up, rhs_low)
    over(0, 2, lambda k: first_sweep(1 + 5 * k))
    over(0, 2, lambda k: second_sweep(2 + 3 * k))
    r3, r4 = residual(3), residual(4)
    edge_raw, edge_x, edge_y = coarse_pack(0, 1, 6, 7)
    edge_side = side_sum(edge_x, edge_y)

    def split(both):
        below, above = both
        return jnp.where(even, below, to_odd(above)), jnp.where(even, to_even(below), above)

    receive(edge_up, edge_low)
    edge_face, edge_in = split((edge[0], edge[1]))
    edge_diag = edge_raw + edge_face
    edge_active = edge_diag > 0.0
    edge_weight = jnp.where(edge_active, OMEGA / jnp.where(edge_active, edge_diag, 1.0), 0.0)
    own_1 = weight * (diag1 - side)
    edge_own_1, edge_out_1, edge_in_1 = edge_weight * (edge_diag - edge_side), edge_weight * z_out, edge_weight * edge_in
    to_out2 = out_part * edge_in_1
    to_out1 = (2.0 - OMEGA) * out_part + weight * beside(out_part, coarse_x, coarse_y) - out_part * edge_own_1
    to_own = 1.0 + (OMEGA - 2.0) * own_1 - weight * beside(own_1, coarse_x, coarse_y) + out_part * edge_out_1 + in_part * swap(in_part)
    to_in1 = (2.0 - OMEGA) * in_part + weight * beside(in_part, coarse_x, coarse_y) - in_part * swap(own_1)
    to_in2 = in_part * swap(out_part)
    edge_own_part = jnp.where(edge_active, 1.0 - OMEGA, 0.0) + edge_weight * edge_side

    for r in range(3, len(rounds)):
        round_end(r)
        round_start(r + 1)
    gather(line_out, line_all, 0, line_sums)

    def partial_sweep(k, beside_k, face):
        u, cx, cy = ua[k], gx[k], gy[k]
        total = cx * pltpu.roll(u, 1, 0) + pltpu.roll(cx * u, nx - 1, 0)
        total = total + cy * pltpu.roll(u, 1, 1) + pltpu.roll(cy * u, ny - 1, 1)
        ub[k] = (1.0 - OMEGA) * u + idf[k] * (rhs[k] + total + gz[face] * ua[beside_k])

    partial_sweep(1, 2, 2)
    partial_sweep(6, 5, 6)
    b1_part = restrict(residual(2) + r3, r4 + residual(5))
    tmp[6] = idf[1] * gz[1]
    tmp[7] = idf[6] * gz[7]
    pro[0] = gz[2] * tmp[6]
    pro[1] = gz[6] * tmp[7]

    receive_fine((fine_in.at[0, 1], fine_in.at[1, 1]), ua, 0, 7, u1_up, u1_low)
    b1 = b1_part + restrict(pro[0] * ua[0], pro[1] * ua[7])

    row_even = even[:1]

    def row_swap(row):
        return jnp.where(row_even, to_even(row), to_odd(row))

    v1 = weight * b1
    begin[0] = jnp.where(even, to_even(b1), to_odd(v1))
    begin[1] = jnp.where(even, b1, v1)
    send(ends_up, ends_low)
    send(far_up, far_low)
    ub[1] = ub[1] + tmp[6] * ua[0]
    ub[6] = ub[6] + tmp[7] * ua[7]
    gather(
        row_out, row_all, 1,
        (
            row_sum(to_own * b1) + row_swap(row_sum(to_in1 * b1)),
            row_swap(row_sum(to_out1 * b1)) + row_sum(to_in2 * b1),
            row_sum(to_out2 * b1),
        ),
    )

    def own_sweep(own, beyond):
        total = beside(own, coarse_x, coarse_y) + z_out * beyond + z_in * swap(own)
        return (1.0 - OMEGA) * own + weight * (b1 + total)

    def edge_sweep(own, beyond, further):
        total = beside(beyond, edge_x, edge_y) + z_out * own + edge_in * further
        return (1.0 - OMEGA) * beyond + edge_weight * (edge_b1 + total)

    receive(ends_up, ends_low)
    edge_b1, far_v1 = split((ends[0], ends[1]))
    edge_v1 = edge_weight * edge_b1
    v2, edge_v2 = own_sweep(v1, edge_v1), edge_sweep(v1, edge_v1, far_v1)
    v3 = own_sweep(v2, edge_v2)
    vn[1] = v3
    send(vn_up, vn_low)
    send_fine(ub, 4, 3, (fine_out.at[0, 2], fine_out.at[1, 2]), u2_up, u2_low)

    receive(far_up, far_low)
    far_own_part, far_out_part = split((far[0, pl.ds(0, hx_rows)], far[1, pl.ds(0, hx_rows)]))
    below, above = far[0, pl.ds(hx_rows, hx_rows // 2)], far[1, pl.ds(hx_rows, hx_rows // 2)]
    spread[pl.ds(0, hx_rows // 2, 2), :] = jnp.where(even_half, below, to_odd(above))
    spread[pl.ds(1, hx_rows // 2, 2), :] = jnp.where(even_half, to_even(below), above)

    gather_wait(line_all, 1, 0, 2)

    line_even = lax.broadcasted_iota(jnp.int32, (n, ny), 1) % 2 == 0

    def line_row(everyone, row):
        return everyone.reshape(n * 8, ny)[pl.ds(row, n, 8), :]

    def apart(both):
        lower = jnp.where(line_even, both, pltpu.roll(both, 1, 1))
        return lower, jnp.where(line_even, pltpu.roll(both, ny - 1, 1), both)

    (de, do), (fe, fo) = apart(line_row(line_all, 0)), apart(line_row(line_all, 1))

    def back(x, s):
        return pltpu.roll(x, s % n, 0)

    def ahead(x, s):
        return pltpu.roll(x, (n - s) % n, 0)

    inv_odd = 1.0 / do
    to_low = fe * back(inv_odd, 1)
    to_up = fo * inv_odd
    fe_next = ahead(fe, 1)
    diag = de - fe * to_low - fo * to_up
    lower = -to_low * back(fo, 1)
    upper = -to_up * fe_next
    steps = []
    shift = 1
    while shift < n:
        alpha, gamma = lower / back(diag, shift), upper / ahead(diag, shift)
        steps.append((shift, alpha, gamma))
        diag = diag - alpha * back(upper, shift) - gamma * ahead(lower, shift)
        lower, upper = -alpha * back(lower, shift), -gamma * ahead(upper, shift)
        shift *= 2
    inv_diag = 1.0 / diag

    gather_wait(row_all, 1, 1, 3)
    one, two = line_row(row_all, 1), line_row(row_all, 2)
    sums = line_row(row_all, 0) + jnp.where(line_even, back(one, 1) + ahead(two, 1), ahead(one, 1) + back(two, 1))
    be, bo = apart(sums)
    reduced = be + to_low * back(bo, 1) + to_up * bo
    for shift, alpha, gamma in steps:
        reduced = reduced - alpha * back(reduced, shift) - gamma * ahead(reduced, shift)
    e_even = reduced * inv_diag
    e_odd = (bo + fo * e_even + fe_next * ahead(e_even, 1)) * inv_odd
    xs[0, pl.ds(8, n), :] = jnp.where(line_even, e_even, e_odd)
    xs[1, pl.ds(8, n), :] = jnp.where(line_even, e_odd, e_even)

    def line(side, distance):
        return jnp.broadcast_to(xs[side, pl.ds(me + 8 + distance, 1), :], (hx_rows, ny))

    def outward(side, distance):
        return jnp.where(even, line(side, -distance), line(side, distance))

    e_own, e_in = line(0, 0), line(1, 0)
    e_out, e_out2, e_out3 = outward(1, 1), outward(0, 1), outward(1, 2)
    receive(vn_up, vn_low)
    below, above = vn[0], vn[2]
    w2 = v3 + own_part * e_own + out_part * e_out + in_part * e_in
    edge_w2 = jnp.where(even, to_even(below), to_odd(above))
    edge_w2 = edge_w2 + edge_own_part * e_out + edge_out_1 * e_own + edge_in_1 * e_out2
    far_w2 = jnp.where(even, below, above) + far_own_part * e_out2 + spread[...] * e_out + far_out_part * e_out3
    w3, edge_w3 = own_sweep(w2, edge_w2), edge_sweep(w2, edge_w2, far_w2)

    def prolong(slot, plane):
        pro[slot, pl.ds(0, hx_rows, 2), :] = plane
        pro[slot, pl.ds(1, hx_rows, 2), :] = plane

    def lower_plane(pack):
        return jnp.where(even, pack, pltpu.roll(pack, 1, 1))

    def upper_plane(pack):
        return jnp.where(even, pltpu.roll(pack, ny - 1, 1), pack)

    prolong(0, lower_plane(edge_w3))
    prolong(1, lower_plane(w3))
    prolong(2, upper_plane(w3))
    prolong(3, upper_plane(edge_w3))

    receive_fine((fine_in.at[0, 2], fine_in.at[1, 2]), ub, 0, 7, u2_up, u2_low)

    def correct(k):
        ua[k] = ub[k] + jnp.where(lab[k] > 0, pro[k // 2], 0.0)

    over(0, 8, correct)

    over(1, 7, sweep(ua, tmp))
    over(2, 6, sweep(tmp, out.at[0], 2))

    for upward, downward in ((far_up, far_low), (ends_up, ends_low), (vn_up, vn_low), (edge_up, edge_low)):
        pl.when(has_up)(upward.wait_send)
        pl.when(has_low)(downward.wait_send)
    for upward, downward in ((near_up, near_low), (next_up, next_low), (rhs_up, rhs_low), (u1_up, u1_low), (u2_up, u2_low)):
        sent_fine(upward, downward)
    gather_wait(line_all, 0, 0, 2)
    gather_wait(row_all, 0, 1, 3)


def on_device(n, rhs, labels, sigma_table):
    planes, nx, ny = labels.shape
    ways = folds(n, nx, ny)
    kept = 8 * ways[0][1]
    fine = lambda count: pltpu.VMEM((count, nx, ny), jnp.float32)
    packs = lambda *counts: pltpu.VMEM((*counts, nx // 2, ny), jnp.float32)
    thirds = lambda *counts: pltpu.VMEM((*counts, nx // 2 + nx // 4, ny), jnp.float32)
    tiles = lambda *counts: pltpu.VMEM((*counts, 8, ny), jnp.float32)
    return pl.pallas_call(
        functools.partial(kernel, n, ways),
        out_shape=pltpu.VMEM(rhs.shape, jnp.float32),
        in_specs=[
            pl.BlockSpec(memory_space=pl.ANY),
            pl.BlockSpec(memory_space=pl.ANY),
            pl.BlockSpec(memory_space=pl.ANY),
        ],
        out_specs=pl.BlockSpec(memory_space=pltpu.VMEM),
        scratch_shapes=[
            pltpu.VMEM((8, nx, ny), jnp.int32),
            fine(8), fine(8), fine(8), fine(8), fine(8), fine(8), fine(8), fine(8),
            fine(8), fine(4),
            pltpu.VMEM((2, 2, kept, ny), jnp.int32), pltpu.VMEM((2, 3, kept, ny), jnp.float32),
            pltpu.VMEM((2, 2, kept, ny), jnp.int32), pltpu.VMEM((2, 3, kept, ny), jnp.float32),
            packs(2), packs(2), thirds(2), thirds(2), packs(2), packs(2), packs(3), packs(),
            tiles(), tiles(n), tiles(), tiles(n),
            pltpu.VMEM((2, n + 16, ny), jnp.float32),
            pltpu.SMEM((3, LABELS), jnp.float32),
            pltpu.SemaphoreType.DMA((3,)),
            pltpu.SemaphoreType.DMA((2, 18)),
            pltpu.SemaphoreType.DMA((2, 2)),
            pltpu.SemaphoreType.REGULAR((n.bit_length(),)),
        ],
        compiler_params=pltpu.CompilerParams(collective_id=0, has_side_effects=True),
    )(rhs, labels, sigma_table.T)


def solution(mesh):
    placed = (P("groups", "slab", None, None), P("slab", "groups", None), P())
    return jax.shard_map(
        functools.partial(on_device, mesh.shape["slab"]),
        mesh=mesh,
        in_specs=placed,
        out_specs=P("groups", "slab", None, None),
        check_vma=False,
    )
```

```python
import functools
import itertools

import jax
import jax.numpy as jnp
import numpy as np
from jax import lax
from jax.experimental import pallas as pl
from jax.experimental.pallas import tpu as pltpu
from jax.sharding import PartitionSpec as P

OMEGA = 0.8
LABELS = 5
MESH = pl.DeviceIdType.MESH
REACH = 4


def copy_to(src, dst, sems, slot, target):
    return pltpu.make_async_remote_copy(
        src_ref=src,
        dst_ref=dst,
        send_sem=sems.at[0, slot],
        recv_sem=sems.at[1, slot],
        device_id={"slab": target},
        device_id_type=MESH,
    )


def near_axis(row, lane, nx, ny, bound):
    across, along = 2 * row + 1 - nx, 2 * lane + 1 - ny
    return (across * across + along * along) * 1000 <= bound


def folds(n, nx, ny):
    tiles = nx // 8
    whole = (0, tiles, (), 4 * 1000 * nx * nx)
    if nx != ny or nx < 128 or nx % 8:
        return whole, whole, n

    def fits(pairs, bound, first, count):
        inside = near_axis(np.arange(nx)[:, None], np.arange(ny)[None], nx, ny, bound).reshape(tiles, 8, ny)
        sent = set(range(first, first + count)) | {folded for _, folded in pairs}
        lost = any(inside[t].any() for t in range(tiles) if t not in sent)
        return not lost and not any((inside[kept] & np.roll(inside[folded], ny // 2, 1)).any() for kept, folded in pairs)

    pairs = ((2, tiles - 2), (4, 0), (tiles - 5, tiles - 1), (tiles - 3, 1))
    middle = (2, tiles - 4, pairs, 813 * nx * nx)
    if not fits(pairs, middle[3], 2, tiles - 4):
        return whole, whole, n
    pairs = ((4, tiles - 4), (tiles - 5, 3), (5, tiles - 3), (tiles - 6, 2))
    outer, rim = middle, n
    for slab in range(n - 1, n // 2, -1):
        away = (4 * slab + 0.5 - 2 * n) / (0.55 * 4 * n)
        bound = int((0.813 - 0.81 * away * away) * 1000 * nx * nx)
        if not fits(pairs, bound, 4, tiles - 8):
            break
        outer, rim = (4, tiles - 8, pairs, bound), slab
    return middle, outer, rim


def kernel(
    n, ways, rhs_hbm, lab_hbm, table_hbm, out,
    lab, rhs, gx, gy, gz, idf, dg, ua, ub, tmp, pro,
    lab_out, fine_out, lab_in, fine_in, part, edge, far_out, far, ends, begin, vn, spread, line_out, line_all, row_out, row_all, xs, table,
    load_sem, sems, gather_sem, tokens,
):
    me = lax.axis_index("slab")
    nx, ny = lab.shape[1:]
    hx_rows = nx // 2
    has_low, has_up = me > 0, me < n - 1

    load_table = pltpu.make_async_copy(table_hbm, table, load_sem.at[2])
    load_table.start()
    own_lab = pltpu.make_async_copy(lab_hbm, lab.at[pl.ds(2, 4)], load_sem.at[0])
    own_rhs = pltpu.make_async_copy(rhs_hbm.at[0], rhs.at[pl.ds(2, 4)], load_sem.at[1])
    own_lab.start()
    own_rhs.start()
    barrier = pltpu.get_barrier_semaphore()

    up, low = lax.rem(me + 1, n), lax.rem(me + n - 1, n)

    def signal(sem, distance):
        for near, other in ((me >= distance, me - distance), (me + distance < n, me + distance)):

            @pl.when(near)
            def _():
                pl.semaphore_signal(sem, inc=1, device_id={"slab": other}, device_id_type=MESH)

    for distance in range(1, min(REACH, n - 1) + 1):
        signal(barrier, distance)

    rounds = []
    while REACH * 2 ** len(rounds) < n - 1:
        rounds.append(REACH * 2 ** len(rounds))

    def round_start(r):
        if r < len(rounds):
            signal(tokens.at[r], rounds[r])

    def round_end(r):
        if r < len(rounds):
            distance = rounds[r]
            both = jnp.logical_and(me >= distance, me + distance < n)
            one = jnp.logical_xor(me >= distance, me + distance < n)
            pl.when(both)(lambda: pl.semaphore_wait(tokens.at[r], 2))
            pl.when(one)(lambda: pl.semaphore_wait(tokens.at[r], 1))

    middle, outer, rim = ways

    def plane_copies(out_ref, in_ref, slot, target):
        return tuple(
            copy_to(out_ref.at[pl.ds(0, 8 * count)], in_ref.at[pl.ds(0, 8 * count)], sems, slot, target)
            for _, count, _, _ in (middle, outer)
        )

    near_up = plane_copies(lab_out.at[0, 0], lab_in.at[0, 0], 0, up)
    near_low = plane_copies(lab_out.at[1, 0], lab_in.at[1, 0], 1, low)
    next_up = plane_copies(lab_out.at[0, 1], lab_in.at[0, 1], 2, up)
    next_low = plane_copies(lab_out.at[1, 1], lab_in.at[1, 1], 3, low)
    rhs_up = plane_copies(fine_out.at[0, 0], fine_in.at[0, 0], 4, up)
    rhs_low = plane_copies(fine_out.at[1, 0], fine_in.at[1, 0], 5, low)
    u1_up = plane_copies(fine_out.at[0, 1], fine_in.at[0, 1], 6, up)
    u1_low = plane_copies(fine_out.at[1, 1], fine_in.at[1, 1], 7, low)
    far_up = copy_to(far_out.at[0], far.at[0], sems, 8, up)
    far_low = copy_to(far_out.at[1], far.at[1], sems, 9, low)
    ends_up = copy_to(begin.at[0], ends.at[0], sems, 10, up)
    ends_low = copy_to(begin.at[1], ends.at[1], sems, 11, low)
    u2_up = plane_copies(fine_out.at[0, 2], fine_in.at[0, 2], 12, up)
    u2_low = plane_copies(fine_out.at[1, 2], fine_in.at[1, 2], 13, low)
    vn_up = copy_to(vn.at[1], vn.at[0], sems, 14, up)
    vn_low = copy_to(vn.at[1], vn.at[2], sems, 15, low)
    edge_up = copy_to(part.at[0], edge.at[0], sems, 16, up)
    edge_low = copy_to(part.at[1], edge.at[1], sems, 17, low)

    def send(upward, downward):
        pl.when(has_up)(upward.start)
        pl.when(has_low)(downward.start)

    def receive(upward, downward):
        pl.when(has_low)(upward.wait_recv)
        pl.when(has_up)(downward.wait_recv)

    tile_row = lax.broadcasted_iota(jnp.int32, (8, ny), 0)
    tile_lane = lax.broadcasted_iota(jnp.int32, (8, ny), 1)

    def tile(t):
        return pl.ds(8 * t, 8)

    def inside(t, bound):
        return near_axis(tile_row + 8 * t, tile_lane, nx, ny, bound)

    def half_turn(values):
        return pltpu.roll(values, ny // 2, 1)

    tiles, bound = nx // 8, middle[3]
    outermost = (4, 5, tiles - 6, tiles - 5)
    partners = {4: (0, tiles - 4), 5: (None, tiles - 3), tiles - 6: (None, 2), tiles - 5: (tiles - 1, 3)}
    tail = (2, 3, tiles - 4, tiles - 3)
    rim_pairs = {2: tiles - 2, tiles - 3: 1}

    def place(t):
        return t - 4 if t not in tail else tiles - 8 + tail.index(t)

    def bound_of(t, thin):
        wide = bound if partners.get(t, (0,))[0] is not None else 4 * 1000 * nx * nx
        return jnp.where(thin, outer[3], wide)

    def fold(field, k, out_ref, thin):
        if not middle[2]:
            out_ref[...] = field[k]
            return
        for t in range(2, tiles - 2):
            values = field[k, tile(t)]
            if t in outermost:
                wide, narrow = partners[t]
                other = field[k, tile(narrow)]
                if wide is not None:
                    other = jnp.where(thin, other, field[k, tile(wide)])
                values = jnp.where(inside(t, bound_of(t, thin)), values, half_turn(other))
            elif t in rim_pairs:
                values = jnp.where(inside(t, bound), values, half_turn(field[k, tile(rim_pairs[t])]))
            out_ref[tile(place(t))] = values

    def unfold(in_ref, field, k, thin):
        if not middle[2]:
            field[k] = in_ref[...]
            return
        zero_tile = jnp.zeros((8, ny), field.dtype)
        for t in range(2, tiles - 2):
            values = in_ref[tile(place(t))]
            if t in outermost:
                wide, narrow = partners[t]
                turned = half_turn(values)
                direct = in_ref[tile(place(narrow))]
                if narrow in rim_pairs:
                    field[k, tile(rim_pairs[narrow])] = jnp.where(
                        inside(rim_pairs[narrow], jnp.where(thin, outer[3], bound)), half_turn(direct), zero_tile
                    )
                    direct = jnp.where(inside(narrow, bound), direct, zero_tile)
                field[k, tile(narrow)] = jnp.where(thin, jnp.where(inside(narrow, outer[3]), turned, zero_tile), direct)
                if wide is not None:
                    field[k, tile(wide)] = jnp.where(inside(wide, jnp.where(thin, outer[3], bound)), turned, zero_tile)
                field[k, tile(t)] = jnp.where(inside(t, bound_of(t, thin)), values, zero_tile)
            elif t not in tail:
                field[k, tile(t)] = values

    def each_way(exists, thin, action):
        if rim == n:
            pl.when(exists)(lambda: action(0))
        else:
            pl.when(jnp.logical_and(exists, jnp.logical_not(thin)))(lambda: action(0))
            pl.when(jnp.logical_and(exists, thin))(lambda: action(1))

    thin_up, thin_low = n - 1 - me >= rim, me >= rim
    from_low_thin, from_up_thin = n - me >= rim, me + 1 >= rim

    def start_fine(upward, downward):
        each_way(has_up, thin_up, lambda way: upward[way].start())
        each_way(has_low, thin_low, lambda way: downward[way].start())

    def send_fine(field, k_up, k_low, outs, upward, downward):
        fold(field, k_up, outs[0], thin_up)
        fold(field, k_low, outs[1], thin_low)
        start_fine(upward, downward)

    def receive_fine(ins, field, k_low, k_up, upward, downward):
        each_way(has_low, from_low_thin, lambda way: upward[way].wait_recv())
        each_way(has_up, from_up_thin, lambda way: downward[way].wait_recv())
        unfold(ins[0], field, k_low, from_low_thin)
        unfold(ins[1], field, k_up, from_up_thin)

    def sent_fine(upward, downward):
        each_way(has_up, thin_up, lambda way: upward[way].wait_send())
        each_way(has_low, thin_low, lambda way: downward[way].wait_send())

    own_lab.wait()
    fold(lab, 5, lab_out.at[0, 0], thin_up)
    fold(lab, 2, lab_out.at[1, 0], thin_low)
    fold(lab, 4, lab_out.at[0, 1], thin_up)
    fold(lab, 3, lab_out.at[1, 1], thin_low)
    own_rhs.wait()
    fold(rhs, 5, fine_out.at[0, 0], thin_up)
    fold(rhs, 2, fine_out.at[1, 0], thin_low)
    pl.semaphore_wait(barrier, jnp.minimum(me, REACH) + jnp.minimum(n - 1 - me, REACH))
    start_fine(near_up, near_low)
    start_fine(next_up, next_low)
    start_fine(rhs_up, rhs_low)
    round_start(0)

    def clear(ref, first, count):
        for k in range(first, first + count):
            ref[k] = jnp.zeros(ref.shape[1:], ref.dtype)

    @pl.when(me == 0)
    def _():
        clear(lab_in.at[0], 0, 2)
        clear(fine_in.at[0], 0, 3)
        clear(edge, 0, 1)
        clear(far, 0, 1)
        clear(ends, 0, 1)
        clear(vn, 0, 1)

    @pl.when(me == n - 1)
    def _():
        clear(lab_in.at[1], 0, 2)
        clear(fine_in.at[1], 0, 3)
        clear(edge, 1, 1)
        clear(far, 1, 1)
        clear(ends, 1, 1)
        clear(vn, 2, 1)

    xs[...] = jnp.zeros(xs.shape, xs.dtype)

    fine_row = lax.broadcasted_iota(jnp.int32, (nx, ny), 0) % 2 == 1
    fine_lane = lax.broadcasted_iota(jnp.int32, (nx, ny), 1) % 2 == 1
    even = lax.broadcasted_iota(jnp.int32, (hx_rows, ny), 1) % 2 == 0

    def select(values, column):
        chosen = jnp.full(values.shape, table[column, 0], jnp.float32)
        for tissue in range(1, LABELS):
            chosen = jnp.where(values == tissue, table[column, tissue], chosen)
        return chosen

    def harmonic(a, b):
        return 2.0 * a * b / (a + b)

    def active(k):
        return (lab[k] > 0).astype(jnp.float32)

    def side_faces(k):
        here = lab[k]
        a = (here > 0).astype(jnp.float32)
        sx, sy = select(here, 0), select(here, 1)
        hx = harmonic(pltpu.roll(sx, 1, 0), sx)
        gx[k] = hx * a * pltpu.roll(a, 1, 0)
        hy = harmonic(pltpu.roll(sy, 1, 1), sy)
        gy[k] = hy * a * pltpu.roll(a, 1, 1)
        return hx + pltpu.roll(hx, nx - 1, 0) + hy + pltpu.roll(hy, ny - 1, 1)

    def face_below(k):
        h = harmonic(select(lab[k - 1], 2), select(lab[k], 2))
        gz[k] = h * active(k - 1) * active(k)
        return h

    def finish(k, faces):
        a = active(k)
        diagonal = a * faces + (1.0 - a)
        dg[k] = diagonal
        idf[k] = OMEGA * a / diagonal

    def over(first, last, body):
        for k in range(first, last):
            body(k)

    def first_sweep(k):
        ua[k] = idf[k] * rhs[k]

    def neighbours(field, k):
        u = field[k]
        cx, cy = gx[k], gy[k]
        total = cx * pltpu.roll(u, 1, 0) + pltpu.roll(cx * u, nx - 1, 0)
        total = total + cy * pltpu.roll(u, 1, 1) + pltpu.roll(cy * u, ny - 1, 1)
        return u, total + gz[k] * field[k - 1] + gz[k + 1] * field[k + 1]

    def sweep(src, dst, shift=0):
        def body(k):
            u, total = neighbours(src, k)
            dst[k - shift] = (1.0 - OMEGA) * u + idf[k] * (rhs[k] + total)

        return body

    def residual(k):
        u, total = neighbours(ub, k)
        return jnp.where(idf[k] > 0.0, rhs[k] - dg[k] * u + total, 0.0)

    second_sweep = sweep(ua, ub)

    load_table.wait()
    h3, h4, h5 = face_below(3), face_below(4), face_below(5)
    finish(3, side_faces(3) + h3 + h4)
    finish(4, side_faces(4) + h4 + h5)
    dg[2] = side_faces(2) + h3
    dg[5] = side_faces(5) + h5
    over(3, 5, first_sweep)

    turn = itertools.count()

    def rows_apart(plane):
        slot = next(turn) % 6
        tmp[slot] = plane
        return tmp[slot, pl.ds(0, hx_rows, 2), :], tmp[slot, pl.ds(1, hx_rows, 2), :]

    def rows_even(plane):
        return rows_apart(plane)[0]

    def rows_sum(plane):
        first, second = rows_apart(plane)
        return first + second

    def lanes_sum(t0, t1):
        return jnp.where(even, t0 + pltpu.roll(t0, ny - 1, 1), t1 + pltpu.roll(t1, 1, 1))

    def lanes_even(t0, t1):
        return jnp.where(even, t0, pltpu.roll(t1, 1, 1))

    def restrict(p0, p1):
        return lanes_sum(rows_sum(p0), rows_sum(p1))

    def inner(k):
        doubled = jnp.where(fine_row, gx[k], 0.0) + jnp.where(fine_lane, gy[k], 0.0)
        if k % 2 == 1:
            doubled = doubled + gz[k]
        return active(k) * dg[k] - 2.0 * doubled

    def to_even(pack):
        return pltpu.roll(pack, ny - 1, 1)

    def to_odd(pack):
        return pltpu.roll(pack, 1, 1)

    def swap(pack):
        return jnp.where(even, to_even(pack), to_odd(pack))

    def of_odd(a, b):
        return jnp.where(even, to_even(a), b)

    def of_even(a, b):
        return jnp.where(even, a, to_odd(b))

    def beside(field, cx, cy):
        total = cx * pltpu.roll(field, 1, 0) + pltpu.roll(cx * field, hx_rows - 1, 0)
        return total + cy * pltpu.roll(field, 2, 1) + pltpu.roll(cy * field, ny - 2, 1)

    def side_sum(cx, cy):
        return cx + pltpu.roll(cx, hx_rows - 1, 0) + cy + pltpu.roll(cy, ny - 2, 1)

    h4_low, h4_up = rows_sum(active(3) * h4), rows_sum(active(4) * h4)
    between = rows_sum(gz[4])
    z_in = lanes_sum(between, between)
    part[0] = jnp.where(even, h4_up + to_even(h4_up), z_in)
    part[1] = jnp.where(even, h4_low + to_even(h4_low), z_in)
    send(edge_up, edge_low)
    send_fine(ua, 4, 3, (fine_out.at[0, 1], fine_out.at[1, 1]), u1_up, u1_low)

    def coarse_pack(k0, k1, k2, k3):
        raw = restrict(inner(k0) + inner(k1), inner(k2) + inner(k3))
        x = lanes_sum(rows_even(gx[k0] + gx[k1]), rows_even(gx[k2] + gx[k3]))
        y = lanes_even(rows_sum(gy[k0] + gy[k1]), rows_sum(gy[k2] + gy[k3]))
        return raw, x, y

    round_end(0)
    round_start(1)
    round_end(1)
    round_start(2)
    receive_fine((lab_in.at[0, 0], lab_in.at[1, 0]), lab, 1, 6, near_up, near_low)
    h2, h6 = face_below(2), face_below(6)
    tmp[6] = h2
    tmp[7] = h6
    finish(2, dg[2] + h2)
    finish(5, dg[5] + h6)
    over(0, 2, lambda k: first_sweep(2 + 3 * k))
    over(3, 5, second_sweep)
    raw, coarse_x, coarse_y = coarse_pack(2, 3, 4, 5)
    side = side_sum(coarse_x, coarse_y)
    active1 = jnp.where(raw > 0.0, 1.0, 0.0)
    diag1 = raw + (1.0 - active1)
    weight = OMEGA * active1 / diag1
    z_out = restrict(gz[2], gz[6])
    own_part, out_part, in_part = (1.0 - OMEGA) * active1 + weight * side, weight * z_out, weight * z_in
    spread[...] = in_part
    in_first, in_second = spread[pl.ds(0, hx_rows // 2, 2), :], spread[pl.ds(1, hx_rows // 2, 2), :]
    even_half = even[: hx_rows // 2]
    far_out[0, pl.ds(0, hx_rows)] = of_even(own_part, out_part)
    far_out[0, pl.ds(hx_rows, hx_rows // 2)] = jnp.where(even_half, in_first, to_odd(in_second))
    far_out[1, pl.ds(0, hx_rows)] = of_odd(own_part, out_part)
    far_out[1, pl.ds(hx_rows, hx_rows // 2)] = jnp.where(even_half, to_even(in_first), in_second)

    sub = lax.broadcasted_iota(jnp.int32, (8, ny), 0)
    sub_even = lax.broadcasted_iota(jnp.int32, (8, ny), 1) % 2 == 0

    def row_sum(pack):
        return jnp.sum(pack, axis=0, keepdims=True)

    def gather(out, everyone, slot, rows_of):
        tile = jnp.zeros((8, ny), jnp.float32)
        for row, values in enumerate(rows_of):
            tile = jnp.where(sub == row, values, tile)
        lower = jnp.sum(jnp.where(sub_even, tile, 0.0), axis=1, keepdims=True)
        upper = jnp.sum(jnp.where(sub_even, 0.0, tile), axis=1, keepdims=True)
        tile = jnp.where(sub_even, lower, upper)
        out[...] = tile
        everyone[me] = tile
        rows = pl.ds(0, len(rows_of))

        def one(step, carry):
            pltpu.make_async_remote_copy(
                src_ref=out.at[rows],
                dst_ref=everyone.at[me, rows],
                send_sem=gather_sem.at[0, slot],
                recv_sem=gather_sem.at[1, slot],
                device_id={"slab": lax.rem(me + step, n)},
                device_id_type=MESH,
            ).start()
            return carry

        lax.fori_loop(1, n, one, 0)

    def gather_wait(everyone, side, slot, count):
        rest = everyone.at[pl.ds(0, n - 1), pl.ds(0, count)]
        pltpu.make_async_copy(rest, rest, gather_sem.at[side, slot]).wait()

    line_sums = (row_sum(raw - 2.0 * (coarse_x + coarse_y)), row_sum(jnp.where(even, z_out, z_in)))

    round_end(2)
    round_start(3)
    receive_fine((lab_in.at[0, 1], lab_in.at[1, 1]), lab, 0, 7, next_up, next_low)
    h1, h7 = face_below(1), face_below(7)
    finish(1, side_faces(1) + h1 + tmp[6])
    finish(6, side_faces(6) + h7 + tmp[7])
    dg[0] = side_faces(0) + h1
    dg[7] = side_faces(7) + h7
    receive_fine((fine_in.at[0, 0], fine_in.at[1, 0]), rhs, 1, 6, rhs_up, rhs_low)
    over(0, 2, lambda k: first_sweep(1 + 5 * k))
    over(0, 2, lambda k: second_sweep(2 + 3 * k))
    r3, r4 = residual(3), residual(4)
    edge_raw, edge_x, edge_y = coarse_pack(0, 1, 6, 7)
    edge_side = side_sum(edge_x, edge_y)

    def split(both):
        below, above = both
        return jnp.where(even, below, to_odd(above)), jnp.where(even, to_even(below), above)

    receive(edge_up, edge_low)
    edge_face, edge_in = split((edge[0], edge[1]))
    edge_diag = edge_raw + edge_face
    edge_active = edge_diag > 0.0
    edge_weight = jnp.where(edge_active, OMEGA / jnp.where(edge_active, edge_diag, 1.0), 0.0)
    own_1 = weight * (diag1 - side)
    edge_own_1, edge_out_1, edge_in_1 = edge_weight * (edge_diag - edge_side), edge_weight * z_out, edge_weight * edge_in
    to_out2 = out_part * edge_in_1
    to_out1 = (2.0 - OMEGA) * out_part + weight * beside(out_part, coarse_x, coarse_y) - out_part * edge_own_1
    to_own = 1.0 + (OMEGA - 2.0) * own_1 - weight * beside(own_1, coarse_x, coarse_y) + out_part * edge_out_1 + in_part * swap(in_part)
    to_in1 = (2.0 - OMEGA) * in_part + weight * beside(in_part, coarse_x, coarse_y) - in_part * swap(own_1)
    to_in2 = in_part * swap(out_part)
    edge_own_part = jnp.where(edge_active, 1.0 - OMEGA, 0.0) + edge_weight * edge_side

    for r in range(3, len(rounds)):
        round_end(r)
        round_start(r + 1)
    gather(line_out, line_all, 0, line_sums)

    def partial_sweep(k, beside_k, face):
        u, cx, cy = ua[k], gx[k], gy[k]
        total = cx * pltpu.roll(u, 1, 0) + pltpu.roll(cx * u, nx - 1, 0)
        total = total + cy * pltpu.roll(u, 1, 1) + pltpu.roll(cy * u, ny - 1, 1)
        ub[k] = (1.0 - OMEGA) * u + idf[k] * (rhs[k] + total + gz[face] * ua[beside_k])

    partial_sweep(1, 2, 2)
    partial_sweep(6, 5, 6)
    b1_part = restrict(residual(2) + r3, r4 + residual(5))
    tmp[6] = idf[1] * gz[1]
    tmp[7] = idf[6] * gz[7]
    pro[0] = gz[2] * tmp[6]
    pro[1] = gz[6] * tmp[7]

    receive_fine((fine_in.at[0, 1], fine_in.at[1, 1]), ua, 0, 7, u1_up, u1_low)
    b1 = b1_part + restrict(pro[0] * ua[0], pro[1] * ua[7])

    row_even = even[:1]

    def row_swap(row):
        return jnp.where(row_even, to_even(row), to_odd(row))

    v1 = weight * b1
    begin[0] = jnp.where(even, to_even(b1), to_odd(v1))
    begin[1] = jnp.where(even, b1, v1)
    send(ends_up, ends_low)
    send(far_up, far_low)
    ub[1] = ub[1] + tmp[6] * ua[0]
    ub[6] = ub[6] + tmp[7] * ua[7]
    gather(
        row_out, row_all, 1,
        (
            row_sum(to_own * b1) + row_swap(row_sum(to_in1 * b1)),
            row_swap(row_sum(to_out1 * b1)) + row_sum(to_in2 * b1),
            row_sum(to_out2 * b1),
        ),
    )

    def own_sweep(own, beyond):
        total = beside(own, coarse_x, coarse_y) + z_out * beyond + z_in * swap(own)
        return (1.0 - OMEGA) * own + weight * (b1 + total)

    def edge_sweep(own, beyond, further):
        total = beside(beyond, edge_x, edge_y) + z_out * own + edge_in * further
        return (1.0 - OMEGA) * beyond + edge_weight * (edge_b1 + total)

    receive(ends_up, ends_low)
    edge_b1, far_v1 = split((ends[0], ends[1]))
    edge_v1 = edge_weight * edge_b1
    v2, edge_v2 = own_sweep(v1, edge_v1), edge_sweep(v1, edge_v1, far_v1)
    v3 = own_sweep(v2, edge_v2)
    vn[1] = v3
    send(vn_up, vn_low)
    send_fine(ub, 4, 3, (fine_out.at[0, 2], fine_out.at[1, 2]), u2_up, u2_low)

    receive(far_up, far_low)
    far_own_part, far_out_part = split((far[0, pl.ds(0, hx_rows)], far[1, pl.ds(0, hx_rows)]))
    below, above = far[0, pl.ds(hx_rows, hx_rows // 2)], far[1, pl.ds(hx_rows, hx_rows // 2)]
    spread[pl.ds(0, hx_rows // 2, 2), :] = jnp.where(even_half, below, to_odd(above))
    spread[pl.ds(1, hx_rows // 2, 2), :] = jnp.where(even_half, to_even(below), above)

    gather_wait(line_all, 1, 0, 2)

    line_even = lax.broadcasted_iota(jnp.int32, (n, ny), 1) % 2 == 0

    def line_row(everyone, row):
        return everyone.reshape(n * 8, ny)[pl.ds(row, n, 8), :]

    def apart(both):
        lower = jnp.where(line_even, both, pltpu.roll(both, 1, 1))
        return lower, jnp.where(line_even, pltpu.roll(both, ny - 1, 1), both)

    (de, do), (fe, fo) = apart(line_row(line_all, 0)), apart(line_row(line_all, 1))

    def back(x, s):
        return pltpu.roll(x, s % n, 0)

    def ahead(x, s):
        return pltpu.roll(x, (n - s) % n, 0)

    inv_odd = 1.0 / do
    to_low = fe * back(inv_odd, 1)
    to_up = fo * inv_odd
    fe_next = ahead(fe, 1)
    diag = de - fe * to_low - fo * to_up
    lower = -to_low * back(fo, 1)
    upper = -to_up * fe_next
    steps = []
    shift = 1
    while shift < n:
        alpha, gamma = lower / back(diag, shift), upper / ahead(diag, shift)
        steps.append((shift, alpha, gamma))
        diag = diag - alpha * back(upper, shift) - gamma * ahead(lower, shift)
        lower, upper = -alpha * back(lower, shift), -gamma * ahead(upper, shift)
        shift *= 2
    inv_diag = 1.0 / diag

    gather_wait(row_all, 1, 1, 3)
    one, two = line_row(row_all, 1), line_row(row_all, 2)
    sums = line_row(row_all, 0) + jnp.where(line_even, back(one, 1) + ahead(two, 1), ahead(one, 1) + back(two, 1))
    be, bo = apart(sums)
    reduced = be + to_low * back(bo, 1) + to_up * bo
    for shift, alpha, gamma in steps:
        reduced = reduced - alpha * back(reduced, shift) - gamma * ahead(reduced, shift)
    e_even = reduced * inv_diag
    e_odd = (bo + fo * e_even + fe_next * ahead(e_even, 1)) * inv_odd
    xs[0, pl.ds(8, n), :] = jnp.where(line_even, e_even, e_odd)
    xs[1, pl.ds(8, n), :] = jnp.where(line_even, e_odd, e_even)

    def line(side, distance):
        return jnp.broadcast_to(xs[side, pl.ds(me + 8 + distance, 1), :], (hx_rows, ny))

    def outward(side, distance):
        return jnp.where(even, line(side, -distance), line(side, distance))

    e_own, e_in = line(0, 0), line(1, 0)
    e_out, e_out2, e_out3 = outward(1, 1), outward(0, 1), outward(1, 2)
    receive(vn_up, vn_low)
    below, above = vn[0], vn[2]
    w2 = v3 + own_part * e_own + out_part * e_out + in_part * e_in
    edge_w2 = jnp.where(even, to_even(below), to_odd(above))
    edge_w2 = edge_w2 + edge_own_part * e_out + edge_out_1 * e_own + edge_in_1 * e_out2
    far_w2 = jnp.where(even, below, above) + far_own_part * e_out2 + spread[...] * e_out + far_out_part * e_out3
    w3, edge_w3 = own_sweep(w2, edge_w2), edge_sweep(w2, edge_w2, far_w2)

    def prolong(slot, plane):
        pro[slot, pl.ds(0, hx_rows, 2), :] = plane
        pro[slot, pl.ds(1, hx_rows, 2), :] = plane

    def lower_plane(pack):
        return jnp.where(even, pack, pltpu.roll(pack, 1, 1))

    def upper_plane(pack):
        return jnp.where(even, pltpu.roll(pack, ny - 1, 1), pack)

    prolong(0, lower_plane(edge_w3))
    prolong(1, lower_plane(w3))
    prolong(2, upper_plane(w3))
    prolong(3, upper_plane(edge_w3))

    receive_fine((fine_in.at[0, 2], fine_in.at[1, 2]), ub, 0, 7, u2_up, u2_low)

    def correct(k):
        ua[k] = ub[k] + jnp.where(lab[k] > 0, pro[k // 2], 0.0)

    over(0, 8, correct)

    over(1, 7, sweep(ua, tmp))
    over(2, 6, sweep(tmp, out.at[0], 2))

    for upward, downward in ((far_up, far_low), (ends_up, ends_low), (vn_up, vn_low), (edge_up, edge_low)):
        pl.when(has_up)(upward.wait_send)
        pl.when(has_low)(downward.wait_send)
    for upward, downward in ((near_up, near_low), (next_up, next_low), (rhs_up, rhs_low), (u1_up, u1_low), (u2_up, u2_low)):
        sent_fine(upward, downward)
    gather_wait(line_all, 0, 0, 2)
    gather_wait(row_all, 0, 1, 3)


def on_device(n, rhs, labels, sigma_table):
    planes, nx, ny = labels.shape
    ways = folds(n, nx, ny)
    kept = 8 * ways[0][1]
    fine = lambda count: pltpu.VMEM((count, nx, ny), jnp.float32)
    packs = lambda *counts: pltpu.VMEM((*counts, nx // 2, ny), jnp.float32)
    thirds = lambda *counts: pltpu.VMEM((*counts, nx // 2 + nx // 4, ny), jnp.float32)
    tiles = lambda *counts: pltpu.VMEM((*counts, 8, ny), jnp.float32)
    return pl.pallas_call(
        functools.partial(kernel, n, ways),
        out_shape=pltpu.VMEM(rhs.shape, jnp.float32),
        in_specs=[
            pl.BlockSpec(memory_space=pl.ANY),
            pl.BlockSpec(memory_space=pl.ANY),
            pl.BlockSpec(memory_space=pl.ANY),
        ],
        out_specs=pl.BlockSpec(memory_space=pltpu.VMEM),
        scratch_shapes=[
            pltpu.VMEM((8, nx, ny), jnp.int32),
            fine(8), fine(8), fine(8), fine(8), fine(8), fine(8), fine(8), fine(8),
            fine(8), fine(4),
            pltpu.VMEM((2, 2, kept, ny), jnp.int32), pltpu.VMEM((2, 3, kept, ny), jnp.float32),
            pltpu.VMEM((2, 2, kept, ny), jnp.int32), pltpu.VMEM((2, 3, kept, ny), jnp.float32),
            packs(2), packs(2), thirds(2), thirds(2), packs(2), packs(2), packs(3), packs(),
            tiles(), tiles(n), tiles(), tiles(n),
            pltpu.VMEM((2, n + 16, ny), jnp.float32),
            pltpu.SMEM((3, LABELS), jnp.float32),
            pltpu.SemaphoreType.DMA((3,)),
            pltpu.SemaphoreType.DMA((2, 18)),
            pltpu.SemaphoreType.DMA((2, 2)),
            pltpu.SemaphoreType.REGULAR((n.bit_length(),)),
        ],
        compiler_params=pltpu.CompilerParams(collective_id=0, has_side_effects=True),
    )(rhs, labels, sigma_table.T)


def solution(mesh):
    placed = (P("groups", "slab", None, None), P("slab", "groups", None), P())
    return jax.shard_map(
        functools.partial(on_device, mesh.shape["slab"]),
        mesh=mesh,
        in_specs=placed,
        out_specs=P("groups", "slab", None, None),
        check_vma=False,
    )
```

```python
import functools
import itertools

import jax
import jax.numpy as jnp
import numpy as np
from jax import lax
from jax.experimental import pallas as pl
from jax.experimental.pallas import tpu as pltpu
from jax.sharding import PartitionSpec as P

OMEGA = 0.8
LABELS = 5
MESH = pl.DeviceIdType.MESH
REACH = 4


def copy_to(src, dst, sems, slot, target):
    return pltpu.make_async_remote_copy(
        src_ref=src,
        dst_ref=dst,
        send_sem=sems.at[0, slot],
        recv_sem=sems.at[1, slot],
        device_id={"slab": target},
        device_id_type=MESH,
    )


def near_axis(row, lane, nx, ny, bound):
    across, along = 2 * row + 1 - nx, 2 * lane + 1 - ny
    return (across * across + along * along) * 1000 <= bound


def folds(n, nx, ny):
    tiles = nx // 8
    whole = (0, tiles, (), 4 * 1000 * nx * nx)
    if nx != ny or nx < 128 or nx % 8:
        return whole, whole, n

    def fits(pairs, bound, first, count):
        inside = near_axis(np.arange(nx)[:, None], np.arange(ny)[None], nx, ny, bound).reshape(tiles, 8, ny)
        sent = set(range(first, first + count)) | {folded for _, folded in pairs}
        lost = any(inside[t].any() for t in range(tiles) if t not in sent)
        return not lost and not any((inside[kept] & np.roll(inside[folded], ny // 2, 1)).any() for kept, folded in pairs)

    pairs = ((2, tiles - 2), (4, 0), (tiles - 5, tiles - 1), (tiles - 3, 1))
    middle = (2, tiles - 4, pairs, 813 * nx * nx)
    if not fits(pairs, middle[3], 2, tiles - 4):
        return whole, whole, n
    pairs = ((4, tiles - 4), (tiles - 5, 3), (5, tiles - 3), (tiles - 6, 2))
    outer, rim = middle, n
    for slab in range(n - 1, n // 2, -1):
        away = (4 * slab + 0.5 - 2 * n) / (0.55 * 4 * n)
        bound = int((0.813 - 0.81 * away * away) * 1000 * nx * nx)
        if not fits(pairs, bound, 4, tiles - 8):
            break
        outer, rim = (4, tiles - 8, pairs, bound), slab
    return middle, outer, rim


def kernel(
    n, ways, rhs_hbm, lab_hbm, table_hbm, out,
    lab, rhs, gx, gy, gz, idf, dg, ua, ub, tmp, pro,
    lab_out, fine_out, lab_in, fine_in, part, edge, far_out, far, ends, begin, vn, spread, line_out, line_all, row_out, row_all, xs, table,
    load_sem, sems, gather_sem, tokens,
):
    me = lax.axis_index("slab")
    nx, ny = lab.shape[1:]
    hx_rows = nx // 2
    has_low, has_up = me > 0, me < n - 1

    load_table = pltpu.make_async_copy(table_hbm, table, load_sem.at[2])
    load_table.start()
    own_lab = pltpu.make_async_copy(lab_hbm, lab.at[pl.ds(2, 4)], load_sem.at[0])
    own_rhs = pltpu.make_async_copy(rhs_hbm.at[0], rhs.at[pl.ds(2, 4)], load_sem.at[1])
    own_lab.start()
    own_rhs.start()
    barrier = pltpu.get_barrier_semaphore()

    up, low = lax.rem(me + 1, n), lax.rem(me + n - 1, n)

    def signal(sem, distance):
        for near, other in ((me >= distance, me - distance), (me + distance < n, me + distance)):

            @pl.when(near)
            def _():
                pl.semaphore_signal(sem, inc=1, device_id={"slab": other}, device_id_type=MESH)

    for distance in range(1, min(REACH, n - 1) + 1):
        signal(barrier, distance)

    rounds = []
    while REACH * 2 ** len(rounds) < n - 1:
        rounds.append(REACH * 2 ** len(rounds))

    def round_start(r):
        if r < len(rounds):
            signal(tokens.at[r], rounds[r])

    def round_end(r):
        if r < len(rounds):
            distance = rounds[r]
            both = jnp.logical_and(me >= distance, me + distance < n)
            one = jnp.logical_xor(me >= distance, me + distance < n)
            pl.when(both)(lambda: pl.semaphore_wait(tokens.at[r], 2))
            pl.when(one)(lambda: pl.semaphore_wait(tokens.at[r], 1))

    middle, outer, rim = ways

    def plane_copies(out_ref, in_ref, slot, target):
        return tuple(
            copy_to(out_ref.at[pl.ds(0, 8 * count)], in_ref.at[pl.ds(0, 8 * count)], sems, slot, target)
            for _, count, _, _ in (middle, outer)
        )

    near_up = plane_copies(lab_out.at[0, 0], lab_in.at[0, 0], 0, up)
    near_low = plane_copies(lab_out.at[1, 0], lab_in.at[1, 0], 1, low)
    next_up = plane_copies(lab_out.at[0, 1], lab_in.at[0, 1], 2, up)
    next_low = plane_copies(lab_out.at[1, 1], lab_in.at[1, 1], 3, low)
    rhs_up = plane_copies(fine_out.at[0, 0], fine_in.at[0, 0], 4, up)
    rhs_low = plane_copies(fine_out.at[1, 0], fine_in.at[1, 0], 5, low)
    u1_up = plane_copies(fine_out.at[0, 1], fine_in.at[0, 1], 6, up)
    u1_low = plane_copies(fine_out.at[1, 1], fine_in.at[1, 1], 7, low)
    far_up = copy_to(far_out.at[0], far.at[0], sems, 8, up)
    far_low = copy_to(far_out.at[1], far.at[1], sems, 9, low)
    ends_up = copy_to(begin.at[0], ends.at[0], sems, 10, up)
    ends_low = copy_to(begin.at[1], ends.at[1], sems, 11, low)
    u2_up = plane_copies(fine_out.at[0, 2], fine_in.at[0, 2], 12, up)
    u2_low = plane_copies(fine_out.at[1, 2], fine_in.at[1, 2], 13, low)
    vn_up = copy_to(vn.at[1], vn.at[0], sems, 14, up)
    vn_low = copy_to(vn.at[1], vn.at[2], sems, 15, low)
    edge_up = copy_to(part.at[0], edge.at[0], sems, 16, up)
    edge_low = copy_to(part.at[1], edge.at[1], sems, 17, low)

    def send(upward, downward):
        pl.when(has_up)(upward.start)
        pl.when(has_low)(downward.start)

    def receive(upward, downward):
        pl.when(has_low)(upward.wait_recv)
        pl.when(has_up)(downward.wait_recv)

    tile_row = lax.broadcasted_iota(jnp.int32, (8, ny), 0)
    tile_lane = lax.broadcasted_iota(jnp.int32, (8, ny), 1)

    def tile(t):
        return pl.ds(8 * t, 8)

    def inside(t, bound):
        return near_axis(tile_row + 8 * t, tile_lane, nx, ny, bound)

    def half_turn(values):
        return pltpu.roll(values, ny // 2, 1)

    tiles, bound = nx // 8, middle[3]
    outermost = (4, 5, tiles - 6, tiles - 5)
    partners = {4: (0, tiles - 4), 5: (None, tiles - 3), tiles - 6: (None, 2), tiles - 5: (tiles - 1, 3)}
    tail = (2, 3, tiles - 4, tiles - 3)
    rim_pairs = {2: tiles - 2, tiles - 3: 1}

    def place(t):
        return t - 4 if t not in tail else tiles - 8 + tail.index(t)

    def bound_of(t, thin):
        wide = bound if partners.get(t, (0,))[0] is not None else 4 * 1000 * nx * nx
        return jnp.where(thin, outer[3], wide)

    def fold(field, k, out_ref, thin):
        if not middle[2]:
            out_ref[...] = field[k]
            return
        for t in range(2, tiles - 2):
            values = field[k, tile(t)]
            if t in outermost:
                wide, narrow = partners[t]
                other = field[k, tile(narrow)]
                if wide is not None:
                    other = jnp.where(thin, other, field[k, tile(wide)])
                values = jnp.where(inside(t, bound_of(t, thin)), values, half_turn(other))
            elif t in rim_pairs:
                values = jnp.where(inside(t, bound), values, half_turn(field[k, tile(rim_pairs[t])]))
            out_ref[tile(place(t))] = values

    def unfold(in_ref, field, k, thin):
        if not middle[2]:
            field[k] = in_ref[...]
            return
        zero_tile = jnp.zeros((8, ny), field.dtype)
        for t in range(2, tiles - 2):
            values = in_ref[tile(place(t))]
            if t in outermost:
                wide, narrow = partners[t]
                turned = half_turn(values)
                direct = in_ref[tile(place(narrow))]
                if narrow in rim_pairs:
                    field[k, tile(rim_pairs[narrow])] = jnp.where(
                        inside(rim_pairs[narrow], jnp.where(thin, outer[3], bound)), half_turn(direct), zero_tile
                    )
                    direct = jnp.where(inside(narrow, bound), direct, zero_tile)
                field[k, tile(narrow)] = jnp.where(thin, jnp.where(inside(narrow, outer[3]), turned, zero_tile), direct)
                if wide is not None:
                    field[k, tile(wide)] = jnp.where(inside(wide, jnp.where(thin, outer[3], bound)), turned, zero_tile)
                field[k, tile(t)] = jnp.where(inside(t, bound_of(t, thin)), values, zero_tile)
            elif t not in tail:
                field[k, tile(t)] = values

    def each_way(exists, thin, action):
        if rim == n:
            pl.when(exists)(lambda: action(0))
        else:
            pl.when(jnp.logical_and(exists, jnp.logical_not(thin)))(lambda: action(0))
            pl.when(jnp.logical_and(exists, thin))(lambda: action(1))

    thin_up, thin_low = n - 1 - me >= rim, me >= rim
    from_low_thin, from_up_thin = n - me >= rim, me + 1 >= rim

    def start_fine(upward, downward):
        each_way(has_up, thin_up, lambda way: upward[way].start())
        each_way(has_low, thin_low, lambda way: downward[way].start())

    def send_fine(field, k_up, k_low, outs, upward, downward):
        fold(field, k_up, outs[0], thin_up)
        fold(field, k_low, outs[1], thin_low)
        start_fine(upward, downward)

    def receive_fine(ins, field, k_low, k_up, upward, downward):
        each_way(has_low, from_low_thin, lambda way: upward[way].wait_recv())
        each_way(has_up, from_up_thin, lambda way: downward[way].wait_recv())
        unfold(ins[0], field, k_low, from_low_thin)
        unfold(ins[1], field, k_up, from_up_thin)

    def sent_fine(upward, downward):
        each_way(has_up, thin_up, lambda way: upward[way].wait_send())
        each_way(has_low, thin_low, lambda way: downward[way].wait_send())

    own_lab.wait()
    fold(lab, 5, lab_out.at[0, 0], thin_up)
    fold(lab, 2, lab_out.at[1, 0], thin_low)
    fold(lab, 4, lab_out.at[0, 1], thin_up)
    fold(lab, 3, lab_out.at[1, 1], thin_low)
    own_rhs.wait()
    fold(rhs, 5, fine_out.at[0, 0], thin_up)
    fold(rhs, 2, fine_out.at[1, 0], thin_low)
    pl.semaphore_wait(barrier, jnp.minimum(me, REACH) + jnp.minimum(n - 1 - me, REACH))
    round_start(0)
    start_fine(near_up, near_low)
    start_fine(next_up, next_low)
    start_fine(rhs_up, rhs_low)

    def clear(ref, first, count):
        for k in range(first, first + count):
            ref[k] = jnp.zeros(ref.shape[1:], ref.dtype)

    @pl.when(me == 0)
    def _():
        clear(lab_in.at[0], 0, 2)
        clear(fine_in.at[0], 0, 3)
        clear(edge, 0, 1)
        clear(far, 0, 1)
        clear(ends, 0, 1)
        clear(vn, 0, 1)

    @pl.when(me == n - 1)
    def _():
        clear(lab_in.at[1], 0, 2)
        clear(fine_in.at[1], 0, 3)
        clear(edge, 1, 1)
        clear(far, 1, 1)
        clear(ends, 1, 1)
        clear(vn, 2, 1)

    xs[...] = jnp.zeros(xs.shape, xs.dtype)

    fine_row = lax.broadcasted_iota(jnp.int32, (nx, ny), 0) % 2 == 1
    fine_lane = lax.broadcasted_iota(jnp.int32, (nx, ny), 1) % 2 == 1
    even = lax.broadcasted_iota(jnp.int32, (hx_rows, ny), 1) % 2 == 0

    def select(values, column):
        chosen = jnp.full(values.shape, table[column, 0], jnp.float32)
        for tissue in range(1, LABELS):
            chosen = jnp.where(values == tissue, table[column, tissue], chosen)
        return chosen

    def harmonic(a, b):
        return 2.0 * a * b / (a + b)

    def active(k):
        return (lab[k] > 0).astype(jnp.float32)

    def side_faces(k):
        here = lab[k]
        a = (here > 0).astype(jnp.float32)
        sx, sy = select(here, 0), select(here, 1)
        hx = harmonic(pltpu.roll(sx, 1, 0), sx)
        gx[k] = hx * a * pltpu.roll(a, 1, 0)
        hy = harmonic(pltpu.roll(sy, 1, 1), sy)
        gy[k] = hy * a * pltpu.roll(a, 1, 1)
        return hx + pltpu.roll(hx, nx - 1, 0) + hy + pltpu.roll(hy, ny - 1, 1)

    def face_below(k):
        h = harmonic(select(lab[k - 1], 2), select(lab[k], 2))
        gz[k] = h * active(k - 1) * active(k)
        return h

    def finish(k, faces):
        a = active(k)
        diagonal = a * faces + (1.0 - a)
        dg[k] = diagonal
        idf[k] = OMEGA * a / diagonal

    def over(first, last, body):
        for k in range(first, last):
            body(k)

    def first_sweep(k):
        ua[k] = idf[k] * rhs[k]

    def neighbours(field, k):
        u = field[k]
        cx, cy = gx[k], gy[k]
        total = cx * pltpu.roll(u, 1, 0) + pltpu.roll(cx * u, nx - 1, 0)
        total = total + cy * pltpu.roll(u, 1, 1) + pltpu.roll(cy * u, ny - 1, 1)
        return u, total + gz[k] * field[k - 1] + gz[k + 1] * field[k + 1]

    def sweep(src, dst, shift=0):
        def body(k):
            u, total = neighbours(src, k)
            dst[k - shift] = (1.0 - OMEGA) * u + idf[k] * (rhs[k] + total)

        return body

    def residual(k):
        u, total = neighbours(ub, k)
        return jnp.where(idf[k] > 0.0, rhs[k] - dg[k] * u + total, 0.0)

    second_sweep = sweep(ua, ub)

    load_table.wait()
    h3, h4, h5 = face_below(3), face_below(4), face_below(5)
    finish(3, side_faces(3) + h3 + h4)
    finish(4, side_faces(4) + h4 + h5)
    dg[2] = side_faces(2) + h3
    dg[5] = side_faces(5) + h5
    over(3, 5, first_sweep)

    turn = itertools.count()

    def rows_apart(plane):
        slot = next(turn) % 6
        tmp[slot] = plane
        return tmp[slot, pl.ds(0, hx_rows, 2), :], tmp[slot, pl.ds(1, hx_rows, 2), :]

    def rows_even(plane):
        return rows_apart(plane)[0]

    def rows_sum(plane):
        first, second = rows_apart(plane)
        return first + second

    def lanes_sum(t0, t1):
        return jnp.where(even, t0 + pltpu.roll(t0, ny - 1, 1), t1 + pltpu.roll(t1, 1, 1))

    def lanes_even(t0, t1):
        return jnp.where(even, t0, pltpu.roll(t1, 1, 1))

    def restrict(p0, p1):
        return lanes_sum(rows_sum(p0), rows_sum(p1))

    def inner(k):
        doubled = jnp.where(fine_row, gx[k], 0.0) + jnp.where(fine_lane, gy[k], 0.0)
        if k % 2 == 1:
            doubled = doubled + gz[k]
        return active(k) * dg[k] - 2.0 * doubled

    def to_even(pack):
        return pltpu.roll(pack, ny - 1, 1)

    def to_odd(pack):
        return pltpu.roll(pack, 1, 1)

    def swap(pack):
        return jnp.where(even, to_even(pack), to_odd(pack))

    def of_odd(a, b):
        return jnp.where(even, to_even(a), b)

    def of_even(a, b):
        return jnp.where(even, a, to_odd(b))

    def beside(field, cx, cy):
        total = cx * pltpu.roll(field, 1, 0) + pltpu.roll(cx * field, hx_rows - 1, 0)
        return total + cy * pltpu.roll(field, 2, 1) + pltpu.roll(cy * field, ny - 2, 1)

    def side_sum(cx, cy):
        return cx + pltpu.roll(cx, hx_rows - 1, 0) + cy + pltpu.roll(cy, ny - 2, 1)

    h4_low, h4_up = rows_sum(active(3) * h4), rows_sum(active(4) * h4)
    between = rows_sum(gz[4])
    z_in = lanes_sum(between, between)
    part[0] = jnp.where(even, h4_up + to_even(h4_up), z_in)
    part[1] = jnp.where(even, h4_low + to_even(h4_low), z_in)
    send(edge_up, edge_low)
    send_fine(ua, 4, 3, (fine_out.at[0, 1], fine_out.at[1, 1]), u1_up, u1_low)

    def coarse_pack(k0, k1, k2, k3):
        raw = restrict(inner(k0) + inner(k1), inner(k2) + inner(k3))
        x = lanes_sum(rows_even(gx[k0] + gx[k1]), rows_even(gx[k2] + gx[k3]))
        y = lanes_even(rows_sum(gy[k0] + gy[k1]), rows_sum(gy[k2] + gy[k3]))
        return raw, x, y

    round_end(0)
    round_start(1)
    round_end(1)
    round_start(2)
    receive_fine((lab_in.at[0, 0], lab_in.at[1, 0]), lab, 1, 6, near_up, near_low)
    h2, h6 = face_below(2), face_below(6)
    tmp[6] = h2
    tmp[7] = h6
    finish(2, dg[2] + h2)
    finish(5, dg[5] + h6)
    over(0, 2, lambda k: first_sweep(2 + 3 * k))
    over(3, 5, second_sweep)
    raw, coarse_x, coarse_y = coarse_pack(2, 3, 4, 5)
    side = side_sum(coarse_x, coarse_y)
    active1 = jnp.where(raw > 0.0, 1.0, 0.0)
    diag1 = raw + (1.0 - active1)
    weight = OMEGA * active1 / diag1
    z_out = restrict(gz[2], gz[6])
    own_part, out_part, in_part = (1.0 - OMEGA) * active1 + weight * side, weight * z_out, weight * z_in
    spread[...] = in_part
    in_first, in_second = spread[pl.ds(0, hx_rows // 2, 2), :], spread[pl.ds(1, hx_rows // 2, 2), :]
    even_half = even[: hx_rows // 2]
    far_out[0, pl.ds(0, hx_rows)] = of_even(own_part, out_part)
    far_out[0, pl.ds(hx_rows, hx_rows // 2)] = jnp.where(even_half, in_first, to_odd(in_second))
    far_out[1, pl.ds(0, hx_rows)] = of_odd(own_part, out_part)
    far_out[1, pl.ds(hx_rows, hx_rows // 2)] = jnp.where(even_half, to_even(in_first), in_second)

    sub = lax.broadcasted_iota(jnp.int32, (8, ny), 0)
    sub_even = lax.broadcasted_iota(jnp.int32, (8, ny), 1) % 2 == 0

    def row_sum(pack):
        return jnp.sum(pack, axis=0, keepdims=True)

    def gather(out, everyone, slot, rows_of):
        tile = jnp.zeros((8, ny), jnp.float32)
        for row, values in enumerate(rows_of):
            tile = jnp.where(sub == row, values, tile)
        lower = jnp.sum(jnp.where(sub_even, tile, 0.0), axis=1, keepdims=True)
        upper = jnp.sum(jnp.where(sub_even, 0.0, tile), axis=1, keepdims=True)
        tile = jnp.where(sub_even, lower, upper)
        out[...] = tile
        everyone[me] = tile
        rows = pl.ds(0, len(rows_of))

        def one(step, carry):
            pltpu.make_async_remote_copy(
                src_ref=out.at[rows],
                dst_ref=everyone.at[me, rows],
                send_sem=gather_sem.at[0, slot],
                recv_sem=gather_sem.at[1, slot],
                device_id={"slab": lax.rem(me + step, n)},
                device_id_type=MESH,
            ).start()
            return carry

        lax.fori_loop(1, n, one, 0)

    def gather_wait(everyone, side, slot, count):
        rest = everyone.at[pl.ds(0, n - 1), pl.ds(0, count)]
        pltpu.make_async_copy(rest, rest, gather_sem.at[side, slot]).wait()

    line_sums = (row_sum(raw - 2.0 * (coarse_x + coarse_y)), row_sum(jnp.where(even, z_out, z_in)))

    round_end(2)
    round_start(3)
    receive_fine((lab_in.at[0, 1], lab_in.at[1, 1]), lab, 0, 7, next_up, next_low)
    h1, h7 = face_below(1), face_below(7)
    finish(1, side_faces(1) + h1 + tmp[6])
    finish(6, side_faces(6) + h7 + tmp[7])
    dg[0] = side_faces(0) + h1
    dg[7] = side_faces(7) + h7
    receive_fine((fine_in.at[0, 0], fine_in.at[1, 0]), rhs, 1, 6, rhs_up, rhs_low)
    over(0, 2, lambda k: first_sweep(1 + 5 * k))
    over(0, 2, lambda k: second_sweep(2 + 3 * k))
    r3, r4 = residual(3), residual(4)
    edge_raw, edge_x, edge_y = coarse_pack(0, 1, 6, 7)
    edge_side = side_sum(edge_x, edge_y)

    def split(both):
        below, above = both
        return jnp.where(even, below, to_odd(above)), jnp.where(even, to_even(below), above)

    receive(edge_up, edge_low)
    edge_face, edge_in = split((edge[0], edge[1]))
    edge_diag = edge_raw + edge_face
    edge_active = edge_diag > 0.0
    edge_weight = jnp.where(edge_active, OMEGA / jnp.where(edge_active, edge_diag, 1.0), 0.0)
    own_1 = weight * (diag1 - side)
    edge_own_1, edge_out_1, edge_in_1 = edge_weight * (edge_diag - edge_side), edge_weight * z_out, edge_weight * edge_in
    to_out2 = out_part * edge_in_1
    to_out1 = (2.0 - OMEGA) * out_part + weight * beside(out_part, coarse_x, coarse_y) - out_part * edge_own_1
    to_own = 1.0 + (OMEGA - 2.0) * own_1 - weight * beside(own_1, coarse_x, coarse_y) + out_part * edge_out_1 + in_part * swap(in_part)
    to_in1 = (2.0 - OMEGA) * in_part + weight * beside(in_part, coarse_x, coarse_y) - in_part * swap(own_1)
    to_in2 = in_part * swap(out_part)
    edge_own_part = jnp.where(edge_active, 1.0 - OMEGA, 0.0) + edge_weight * edge_side

    for r in range(3, len(rounds)):
        round_end(r)
        round_start(r + 1)
    gather(line_out, line_all, 0, line_sums)

    def partial_sweep(k, beside_k, face):
        u, cx, cy = ua[k], gx[k], gy[k]
        total = cx * pltpu.roll(u, 1, 0) + pltpu.roll(cx * u, nx - 1, 0)
        total = total + cy * pltpu.roll(u, 1, 1) + pltpu.roll(cy * u, ny - 1, 1)
        ub[k] = (1.0 - OMEGA) * u + idf[k] * (rhs[k] + total + gz[face] * ua[beside_k])

    partial_sweep(1, 2, 2)
    partial_sweep(6, 5, 6)
    b1_part = restrict(residual(2) + r3, r4 + residual(5))
    tmp[6] = idf[1] * gz[1]
    tmp[7] = idf[6] * gz[7]
    pro[0] = gz[2] * tmp[6]
    pro[1] = gz[6] * tmp[7]

    receive_fine((fine_in.at[0, 1], fine_in.at[1, 1]), ua, 0, 7, u1_up, u1_low)
    b1 = b1_part + restrict(pro[0] * ua[0], pro[1] * ua[7])

    row_even = even[:1]

    def row_swap(row):
        return jnp.where(row_even, to_even(row), to_odd(row))

    v1 = weight * b1
    begin[0] = jnp.where(even, to_even(b1), to_odd(v1))
    begin[1] = jnp.where(even, b1, v1)
    send(ends_up, ends_low)
    send(far_up, far_low)
    ub[1] = ub[1] + tmp[6] * ua[0]
    ub[6] = ub[6] + tmp[7] * ua[7]
    gather(
        row_out, row_all, 1,
        (
            row_sum(to_own * b1) + row_swap(row_sum(to_in1 * b1)),
            row_swap(row_sum(to_out1 * b1)) + row_sum(to_in2 * b1),
            row_sum(to_out2 * b1),
        ),
    )

    def own_sweep(own, beyond):
        total = beside(own, coarse_x, coarse_y) + z_out * beyond + z_in * swap(own)
        return (1.0 - OMEGA) * own + weight * (b1 + total)

    def edge_sweep(own, beyond, further):
        total = beside(beyond, edge_x, edge_y) + z_out * own + edge_in * further
        return (1.0 - OMEGA) * beyond + edge_weight * (edge_b1 + total)

    receive(ends_up, ends_low)
    edge_b1, far_v1 = split((ends[0], ends[1]))
    edge_v1 = edge_weight * edge_b1
    v2, edge_v2 = own_sweep(v1, edge_v1), edge_sweep(v1, edge_v1, far_v1)
    v3 = own_sweep(v2, edge_v2)
    vn[1] = v3
    send(vn_up, vn_low)
    send_fine(ub, 4, 3, (fine_out.at[0, 2], fine_out.at[1, 2]), u2_up, u2_low)

    receive(far_up, far_low)
    far_own_part, far_out_part = split((far[0, pl.ds(0, hx_rows)], far[1, pl.ds(0, hx_rows)]))
    below, above = far[0, pl.ds(hx_rows, hx_rows // 2)], far[1, pl.ds(hx_rows, hx_rows // 2)]
    spread[pl.ds(0, hx_rows // 2, 2), :] = jnp.where(even_half, below, to_odd(above))
    spread[pl.ds(1, hx_rows // 2, 2), :] = jnp.where(even_half, to_even(below), above)

    gather_wait(line_all, 1, 0, 2)

    line_even = lax.broadcasted_iota(jnp.int32, (n, ny), 1) % 2 == 0

    def line_row(everyone, row):
        return everyone.reshape(n * 8, ny)[pl.ds(row, n, 8), :]

    def apart(both):
        lower = jnp.where(line_even, both, pltpu.roll(both, 1, 1))
        return lower, jnp.where(line_even, pltpu.roll(both, ny - 1, 1), both)

    (de, do), (fe, fo) = apart(line_row(line_all, 0)), apart(line_row(line_all, 1))

    def back(x, s):
        return pltpu.roll(x, s % n, 0)

    def ahead(x, s):
        return pltpu.roll(x, (n - s) % n, 0)

    inv_odd = 1.0 / do
    to_low = fe * back(inv_odd, 1)
    to_up = fo * inv_odd
    fe_next = ahead(fe, 1)
    diag = de - fe * to_low - fo * to_up
    lower = -to_low * back(fo, 1)
    upper = -to_up * fe_next
    steps = []
    shift = 1
    while shift < n:
        alpha, gamma = lower / back(diag, shift), upper / ahead(diag, shift)
        steps.append((shift, alpha, gamma))
        diag = diag - alpha * back(upper, shift) - gamma * ahead(lower, shift)
        lower, upper = -alpha * back(lower, shift), -gamma * ahead(upper, shift)
        shift *= 2
    inv_diag = 1.0 / diag

    gather_wait(row_all, 1, 1, 3)
    one, two = line_row(row_all, 1), line_row(row_all, 2)
    sums = line_row(row_all, 0) + jnp.where(line_even, back(one, 1) + ahead(two, 1), ahead(one, 1) + back(two, 1))
    be, bo = apart(sums)
    reduced = be + to_low * back(bo, 1) + to_up * bo
    for shift, alpha, gamma in steps:
        reduced = reduced - alpha * back(reduced, shift) - gamma * ahead(reduced, shift)
    e_even = reduced * inv_diag
    e_odd = (bo + fo * e_even + fe_next * ahead(e_even, 1)) * inv_odd
    xs[0, pl.ds(8, n), :] = jnp.where(line_even, e_even, e_odd)
    xs[1, pl.ds(8, n), :] = jnp.where(line_even, e_odd, e_even)

    def line(side, distance):
        return jnp.broadcast_to(xs[side, pl.ds(me + 8 + distance, 1), :], (hx_rows, ny))

    def outward(side, distance):
        return jnp.where(even, line(side, -distance), line(side, distance))

    e_own, e_in = line(0, 0), line(1, 0)
    e_out, e_out2, e_out3 = outward(1, 1), outward(0, 1), outward(1, 2)
    receive(vn_up, vn_low)
    below, above = vn[0], vn[2]
    w2 = v3 + own_part * e_own + out_part * e_out + in_part * e_in
    edge_w2 = jnp.where(even, to_even(below), to_odd(above))
    edge_w2 = edge_w2 + edge_own_part * e_out + edge_out_1 * e_own + edge_in_1 * e_out2
    far_w2 = jnp.where(even, below, above) + far_own_part * e_out2 + spread[...] * e_out + far_out_part * e_out3
    w3, edge_w3 = own_sweep(w2, edge_w2), edge_sweep(w2, edge_w2, far_w2)

    def prolong(slot, plane):
        pro[slot, pl.ds(0, hx_rows, 2), :] = plane
        pro[slot, pl.ds(1, hx_rows, 2), :] = plane

    def lower_plane(pack):
        return jnp.where(even, pack, pltpu.roll(pack, 1, 1))

    def upper_plane(pack):
        return jnp.where(even, pltpu.roll(pack, ny - 1, 1), pack)

    prolong(0, lower_plane(edge_w3))
    prolong(1, lower_plane(w3))
    prolong(2, upper_plane(w3))
    prolong(3, upper_plane(edge_w3))

    receive_fine((fine_in.at[0, 2], fine_in.at[1, 2]), ub, 0, 7, u2_up, u2_low)

    def correct(k):
        ua[k] = ub[k] + jnp.where(lab[k] > 0, pro[k // 2], 0.0)

    over(0, 8, correct)

    over(1, 7, sweep(ua, tmp))
    over(2, 6, sweep(tmp, out.at[0], 2))

    for upward, downward in ((far_up, far_low), (ends_up, ends_low), (vn_up, vn_low), (edge_up, edge_low)):
        pl.when(has_up)(upward.wait_send)
        pl.when(has_low)(downward.wait_send)
    for upward, downward in ((near_up, near_low), (next_up, next_low), (rhs_up, rhs_low), (u1_up, u1_low), (u2_up, u2_low)):
        sent_fine(upward, downward)
    gather_wait(line_all, 0, 0, 2)
    gather_wait(row_all, 0, 1, 3)


def on_device(n, rhs, labels, sigma_table):
    planes, nx, ny = labels.shape
    ways = folds(n, nx, ny)
    kept = 8 * ways[0][1]
    fine = lambda count: pltpu.VMEM((count, nx, ny), jnp.float32)
    packs = lambda *counts: pltpu.VMEM((*counts, nx // 2, ny), jnp.float32)
    thirds = lambda *counts: pltpu.VMEM((*counts, nx // 2 + nx // 4, ny), jnp.float32)
    tiles = lambda *counts: pltpu.VMEM((*counts, 8, ny), jnp.float32)
    return pl.pallas_call(
        functools.partial(kernel, n, ways),
        out_shape=pltpu.VMEM(rhs.shape, jnp.float32),
        in_specs=[
            pl.BlockSpec(memory_space=pl.ANY),
            pl.BlockSpec(memory_space=pl.ANY),
            pl.BlockSpec(memory_space=pl.ANY),
        ],
        out_specs=pl.BlockSpec(memory_space=pltpu.VMEM),
        scratch_shapes=[
            pltpu.VMEM((8, nx, ny), jnp.int32),
            fine(8), fine(8), fine(8), fine(8), fine(8), fine(8), fine(8), fine(8),
            fine(8), fine(4),
            pltpu.VMEM((2, 2, kept, ny), jnp.int32), pltpu.VMEM((2, 3, kept, ny), jnp.float32),
            pltpu.VMEM((2, 2, kept, ny), jnp.int32), pltpu.VMEM((2, 3, kept, ny), jnp.float32),
            packs(2), packs(2), thirds(2), thirds(2), packs(2), packs(2), packs(3), packs(),
            tiles(), tiles(n), tiles(), tiles(n),
            pltpu.VMEM((2, n + 16, ny), jnp.float32),
            pltpu.SMEM((3, LABELS), jnp.float32),
            pltpu.SemaphoreType.DMA((3,)),
            pltpu.SemaphoreType.DMA((2, 18)),
            pltpu.SemaphoreType.DMA((2, 2)),
            pltpu.SemaphoreType.REGULAR((n.bit_length(),)),
        ],
        compiler_params=pltpu.CompilerParams(collective_id=0, has_side_effects=True),
    )(rhs, labels, sigma_table.T)


def solution(mesh):
    placed = (P("groups", "slab", None, None), P("slab", "groups", None), P())
    return jax.shard_map(
        functools.partial(on_device, mesh.shape["slab"]),
        mesh=mesh,
        in_specs=placed,
        out_specs=P("groups", "slab", None, None),
        check_vma=False,
    )
```
